256 devices in a mesh: gx: 8 (over y, core), gy: 32 (over x, z).
Axes of the slice: x: 4, y: 4, z: 8, core: 2. Of those that a mesh axis runs over, the one named last changes fastest.
Arguments:
- right_side: float32 [64, 512, 256], P('gx', 'gy'), may hold values from -8 to 8
- velocity: float32 [3, 64, 512, 256], P(None, 'gx', 'gy'), may hold values from 0.1 to 3
- deflation: bfloat16 [32, 64, 512, 256], P(None, 'gx', 'gy'), may hold values from -0.1875 to 0.1875
- inverse_rows: float32 [8192, 8192], P(('gx', 'gy')), may hold values from -0.0625 to 0.0625
Outputs:
- solution_field: float32 [64, 512, 256], P('gx', 'gy')
- residual: float32 [64, 512, 256], P('gx', 'gy')
The draws below stay inside these ranges and needn't reach their ends.
All inputs are finite; a program needn't handle non-finite values.
Results may differ from the reference program's by a relative error of at most 0.005.
Values sent between devices are 32-bit elements; how exact they have to be, the bound alone decides.
A program may use at most 64 MiB of HBM per device.

```python
import math
import jax
import jax.numpy as jnp
from jax import lax

CX = 8
CY = 16
NZ = 256
KD = 32
DEPTH = 2
CHEB = 4
NX = 64
NY = 512
KC = 8192
N_GX = 8
N_GY = 32


def level_of(key, extent, split, low, top_value):
    def one(position, parts):
        steps = jax.random.uniform(jax.random.fold_in(jax.random.fold_in(key, 6), position), (parts,), jnp.float32, low / len(split), top_value / len(split))
        return jnp.repeat(jnp.exp(steps), extent[position] // parts).reshape((-1,) + (1,) * (len(extent) - position - 1))

    level = one(*split[0])
    for cut in split[1:]:
        level = level * one(*cut)
    return level


def gaussian(key, extent, width, most, split=(), kind=jnp.bfloat16):
    array = width * jax.random.normal(key, extent, jnp.float32)
    if split:
        array = array * level_of(key, extent, split, -0.22, 0.18)
    return jnp.clip(array, -most, most).astype(kind)


def setup_inputs(seed: int = 0) -> dict:
    arg_keys = jax.random.split(jax.random.key(seed), 5)
    right_side = gaussian(arg_keys[0], (NX, NY, NZ), 1.0, 8.0, ((0, 8), (1, 32)), jnp.float32)
    velocity = jnp.clip(jnp.exp(math.log(3.0) - 3.4011974 * jax.random.uniform(arg_keys[1], (3, NX, NY, NZ), jnp.float32) ** level_of(arg_keys[1], (3, NX, NY, NZ), ((1, 8), (2, 32)), -0.2, 0.2)), 0.1, 3.0)
    deflation = gaussian(arg_keys[2], (KD, NX, NY, NZ), ((KD * CX * CY * NZ) ** -0.25), 0.1875, ((1, 8), (2, 32)))
    inverse_rows = gaussian(arg_keys[3], (KC, KC), KC ** -0.5, 0.0625, ((0, 256),), jnp.float32)
    return dict(right_side=right_side, velocity=velocity, deflation=deflation, inverse_rows=inverse_rows)


cheb_center = 1.0
cheb_radius = 0.9


def upwind(padded, velocity):
    centre = padded[1:-1, 1:-1, 1:-1]
    diagonal = 6.0 + velocity[0] + velocity[1] + velocity[2]
    beside = padded[2:, 1:-1, 1:-1] + (1.0 + velocity[0]) * padded[:-2, 1:-1, 1:-1]
    beside = beside + padded[1:-1, 2:, 1:-1] + (1.0 + velocity[1]) * padded[1:-1, :-2, 1:-1]
    beside = beside + padded[1:-1, 1:-1, 2:] + (1.0 + velocity[2]) * padded[1:-1, 1:-1, :-2]
    return diagonal * centre - beside


def box_apply(field, velocity):
    return upwind(jnp.pad(field, 1), velocity)


def chebyshev(source, velocity, inside):
    inverse_diag = 1.0 / (6.0 + velocity[0] + velocity[1] + velocity[2])
    sigma_ratio = cheb_center / cheb_radius
    rho_now = 1.0 / sigma_ratio
    update = inverse_diag * source / cheb_center * inside
    estimate = update
    remainder = source
    for sweep_index in range(CHEB - 1):
        remainder = remainder - box_apply(update, velocity)
        rho_next = 1.0 / (2.0 * sigma_ratio - rho_now)
        update = (rho_next * rho_now * update + (2.0 * rho_next / cheb_radius) * inverse_diag * remainder) * inside
        estimate = estimate + update
        rho_now = rho_next
    return estimate


def assemble(blocks):
    return blocks.reshape(N_GX, N_GY, CX, CY, NZ).transpose(0, 2, 1, 3, 4).reshape(CX * N_GX, CY * N_GY, NZ)


def precondition(residual, velocity, deflation, inverse_rows):
    count = N_GX * N_GY
    numbers = jnp.arange(count, dtype=jnp.int32)
    rounded = residual.astype(jnp.bfloat16)
    zero = jnp.zeros((), jnp.int32)

    def local_vectors(number):
        start_x = (number // N_GY * CX).astype(jnp.int32)
        start_y = (number % N_GY * CY).astype(jnp.int32)
        local = lax.dynamic_slice(deflation, (zero, start_x, start_y, zero), (KD, CX, CY, NZ))
        return local.reshape(KD, CX * CY * NZ), start_x, start_y

    def restrict_one(number):
        local, start_x, start_y = local_vectors(number)
        piece = lax.dynamic_slice(rounded, (start_x, start_y, zero), (CX, CY, NZ)).reshape(CX * CY * NZ)
        return jnp.dot(local, piece, preferred_element_type=jnp.float32)

    coarse = lax.map(restrict_one, numbers).reshape(count * KD)
    solved = jnp.dot(inverse_rows, coarse, precision=lax.Precision.HIGHEST).astype(jnp.bfloat16)
    solved = solved.reshape(count, KD)

    def prolong_one(item):
        number, weights = item
        local, start_x, start_y = local_vectors(number)
        return jnp.dot(weights, local, preferred_element_type=jnp.float32).reshape(CX, CY, NZ)

    correction = assemble(lax.map(prolong_one, (numbers, solved)))
    remaining = residual - box_apply(correction, velocity)
    padded_rest = jnp.pad(remaining, ((DEPTH, DEPTH), (DEPTH, DEPTH), (0, 0)))
    padded_vel = jnp.pad(velocity, ((0, 0), (DEPTH, DEPTH), (DEPTH, DEPTH), (0, 0)))
    padded_in = jnp.pad(jnp.ones((CX * N_GX, CY * N_GY, 1), residual.dtype), ((DEPTH, DEPTH), (DEPTH, DEPTH), (0, 0)))
    wide_x = CX + 2 * DEPTH
    wide_y = CY + 2 * DEPTH

    def smooth_one(number):
        start_x = (number // N_GY * CX).astype(jnp.int32)
        start_y = (number % N_GY * CY).astype(jnp.int32)
        source = lax.dynamic_slice(padded_rest, (start_x, start_y, zero), (wide_x, wide_y, NZ))
        vel_box = lax.dynamic_slice(padded_vel, (zero, start_x, start_y, zero), (3, wide_x, wide_y, NZ))
        inside = lax.dynamic_slice(padded_in, (start_x, start_y, zero), (wide_x, wide_y, 1))
        estimate = chebyshev(source, vel_box, inside)
        return estimate[DEPTH:DEPTH + CX, DEPTH:DEPTH + CY]

    return correction + assemble(lax.map(smooth_one, numbers))


def reference(right_side, velocity, deflation, inverse_rows):
    residual = right_side
    rho_now = jnp.sum(residual * residual)
    search = precondition(residual, velocity, deflation, inverse_rows)
    image = box_apply(search, velocity)
    alpha_step = rho_now / jnp.sum(residual * image)
    middle = residual - alpha_step * image
    smoothed = precondition(middle, velocity, deflation, inverse_rows)
    turned = box_apply(smoothed, velocity)
    omega_step = jnp.sum(turned * middle) / jnp.sum(turned * turned)
    solution_field = alpha_step * search + omega_step * smoothed
    return solution_field, middle - omega_step * turned
```

```python
import jax
import jax.numpy as jnp
from jax import lax
from jax.experimental import pallas as pl
from jax.experimental.pallas import tpu as pltpu
from jax.sharding import PartitionSpec as P

F32 = jnp.float32
BF16 = jnp.bfloat16
MESH = pl.DeviceIdType.MESH
SX, SY, NZ = 8, 16, 256
KD = 32
DEPTH = 2
CHEB = 4
ZG = 8
QUAD = 128 // KD
ROWS = 24
SIGMA = 1.0 / 0.9


def iota(shape, dim):
    return lax.broadcasted_iota(jnp.int32, shape, dim)


def padded(low, middle, high):
    gap = 4 - low.shape[0]
    parts = [low, middle, high]
    if gap:
        fill = jnp.zeros((gap, NZ), F32)
        parts = [fill] + parts + [fill]
    return jnp.concatenate(parts, axis=0)


def kernel(
    ngx, ngy,
    r_hbm, vel_hbm, defl_hbm, inv_hbm, sol_ref, res_ref,
    defl, inv, base, base_lo, base_hi, base_plo, base_phi,
    coef, q24, corr, corr_lo, corr_hi, corr_plo, corr_phi, ext, left, upd_a, upd_b, est,
    face, face_lo, face_hi, face_own, face_plo, face_phi,
    img, img_lo, img_hi, img_plo, img_phi, search, image, wfield, row_a, row_b,
    local_sem, ag_send, ag_recv, halo_send, halo_recv,
):
    gx = lax.axis_index("gx")
    gy = lax.axis_index("gy")
    xg = ngy // ZG
    zpos = lax.rem(gy, ZG)
    xpos = lax.div(gy, ZG)
    line = xpos * ZG
    group = ngx * xg
    seat = gx * xg + xpos
    east, west = lax.rem(gx + 1, ngx), lax.rem(gx + ngx - 1, ngx)
    north, south = lax.rem(gy + 1, ngy), lax.rem(gy + ngy - 1, ngy)
    barrier = pltpu.get_barrier_semaphore()

    def line_peer(step):
        return (gx, line + lax.rem(zpos + step, ZG))

    def group_peer(step):
        other = lax.rem(seat + step, group)
        return (lax.div(other, xg), lax.rem(other, xg) * ZG + zpos)

    def greet(device):
        pl.semaphore_signal(barrier, inc=1, device_id=device, device_id_type=MESH)

    @pl.loop(1, ZG)
    def _(step):
        greet(line_peer(step))

    @pl.loop(1, group)
    def _(step):
        greet(group_peer(step))

    around = [
        (east, gy), (west, gy), (gx, north), (gx, south),
        (east, north), (west, north), (east, south), (west, south),
    ]
    for device in around:
        greet(device)

    own = pl.ds(DEPTH, SX)
    loads = [
        pltpu.make_async_copy(r_hbm, base.at[3, own], local_sem.at[0]),
        pltpu.make_async_copy(defl_hbm, defl, local_sem.at[1]),
        pltpu.make_async_copy(vel_hbm, base.at[pl.ds(0, 3), own], local_sem.at[2]),
        pltpu.make_async_copy(inv_hbm, inv, local_sem.at[3]),
    ]
    for load in loads:
        load.start()

    has_w, has_e = gx > 0, gx < ngx - 1
    has_s, has_n = gy > 0, gy < ngy - 1

    def remote(src, dst, send, recv, device):
        return pltpu.make_async_remote_copy(
            src_ref=src, dst_ref=dst, send_sem=send, recv_sem=recv,
            device_id=device, device_id_type=MESH,
        )

    def line_send(turn, row):
        row_a[turn, zpos] = row

        @pl.loop(1, ZG)
        def _(step):
            remote(row_a.at[turn, zpos], row_a.at[turn, zpos], ag_send.at[turn, 0],
                   ag_recv.at[turn, 0], line_peer(step)).start()

    def line_wait(turn):
        view = row_a.at[turn, pl.ds(0, ZG - 1)]
        remote(view, view, ag_send.at[turn, 0], ag_recv.at[turn, 0], (east, gy)).wait_recv()

    def group_send(turn, rows):
        row_b[turn, seat] = rows

        @pl.loop(1, group)
        def _(step):
            remote(row_b.at[turn, seat], row_b.at[turn, seat], ag_send.at[turn, 1],
                   ag_recv.at[turn, 1], group_peer(step)).start()

    def group_wait(turn):
        view = row_b.at[turn, pl.ds(0, group - 1)]
        remote(view, view, ag_send.at[turn, 1], ag_recv.at[turn, 1], (east, gy)).wait_recv()

    def gather_finish(turn):
        view = row_a.at[turn, pl.ds(0, ZG - 1)]
        remote(view, view, ag_send.at[turn, 0], ag_recv.at[turn, 0], (east, gy)).wait_send()
        view = row_b.at[turn, pl.ds(0, group - 1)]
        remote(view, view, ag_send.at[turn, 1], ag_recv.at[turn, 1], (east, gy)).wait_send()

    def halo_start(turn, width, mid, low, high, plow, phigh, lead=()):
        def at(ref, start, size):
            return ref.at[lead + (pl.ds(start, size),)]

        def go(src, dst, kind, device):
            remote(src, dst, halo_send.at[turn, kind], halo_recv.at[turn, kind], device).start()

        w = width
        go(at(phigh, SX - w, w), at(low, 0, w), 1, (east, north))
        go(at(phigh, 0, w), at(low, w + SX, w), 1, (west, north))
        go(at(plow, SX - w, w), at(high, 0, w), 2, (east, south))
        go(at(plow, 0, w), at(high, w + SX, w), 2, (west, south))
        go(at(phigh, 0, SX), at(low, w, SX), 1, (gx, north))
        go(at(plow, 0, SX), at(high, w, SX), 2, (gx, south))
        go(at(mid, SX, w), at(mid, 0, w), 0, (east, gy))
        go(at(mid, w, w), at(mid, w + SX, w), 0, (west, gy))

    def halo_wait(turn, width, mid, low, high, lead=(), what="recv"):
        views = [mid.at[lead + (pl.ds(0, 2 * width),)], low, high]
        for kind, view in enumerate(views):
            copy = remote(view, view, halo_send.at[turn, kind], halo_recv.at[turn, kind], (east, gy))
            if what == "recv":
                copy.wait_recv()
            else:
                copy.wait_send()

    def face_start(turn):
        slot = turn - 3

        def go(src, dst, kind, device):
            remote(src, dst, halo_send.at[turn, kind], halo_recv.at[turn, kind], device).start()

        go(face_phi.at[slot], face_lo.at[slot], 1, (gx, north))
        go(face_plo.at[slot], face_hi.at[slot], 2, (gx, south))
        go(face_own.at[slot, 1], face.at[slot, 0], 0, (east, gy))
        go(face_own.at[slot, 0], face.at[slot, 1], 0, (west, gy))

    def face_wait(turn, what="recv"):
        slot = turn - 3
        for kind, view in enumerate([face.at[slot], face_lo.at[slot], face_hi.at[slot]]):
            copy = remote(view, view, halo_send.at[turn, kind], halo_recv.at[turn, kind], (east, gy))
            if what == "recv":
                copy.wait_recv()
            else:
                copy.wait_send()

    lane_end = iota((ROWS, NZ), 1) == NZ - 1

    def stencil(p, before, centre, after):
        beside = after + coef[1, p] * before
        beside = beside + pltpu.roll(centre, ROWS - 1, 0) + coef[2, p] * pltpu.roll(centre, 1, 0)
        ahead = jnp.where(lane_end, 0.0, pltpu.roll(centre, NZ - 1, 1))
        beside = beside + ahead + coef[3, p] * pltpu.roll(centre, 1, 1)
        return coef[0, p] * centre - beside

    def split(value):
        top = value.astype(BF16)
        rest = (value - top.astype(F32)).astype(BF16)
        return jnp.concatenate([top, rest], axis=0)

    def weights(half, x):
        return defl[pl.ds(half * 16, 16), x].reshape(256, NZ)

    def restrict(plane, exact):
        totals = [None, None]
        for x in range(SX):
            value = plane(x)
            lhs = split(value) if exact else value.astype(BF16)
            for half in range(2):
                part = lax.dot_general(
                    lhs, weights(half, x), (((1,), (1,)), ((), ())), preferred_element_type=F32
                )
                totals[half] = part if totals[half] is None else totals[half] + part
        packed = []
        for total in totals:
            same = lax.rem(iota(total.shape, 0), 16) == lax.rem(iota(total.shape, 1), 16)
            kept = jnp.where(same, total, 0.0)
            packed.append(jnp.sum(kept.reshape(-1, 8, 256), axis=0))
        packed = jnp.concatenate(packed, axis=1)
        high = packed.astype(BF16).astype(F32)
        rest = packed - high
        middle = rest.astype(BF16).astype(F32)
        low = rest - middle
        stack = jnp.concatenate([high, middle, low, jnp.zeros_like(low)], axis=0).astype(BF16)
        pick = lax.div(iota((2 * 256, 128), 0), 16) == lax.rem(iota((2 * 256, 128), 1), KD)
        row = jnp.dot(stack, pick.astype(F32).astype(BF16), preferred_element_type=F32)
        row = jnp.sum(row, axis=0, keepdims=True)
        mine = lax.div(iota((1, 128), 1), KD) == lax.rem(zpos, QUAD)
        return jnp.where(mine, row, 0.0)

    def quads(turn):
        rows = []
        for start in range(0, ZG, QUAD):
            total = row_a[turn, start]
            for k in range(1, QUAD):
                total = total + row_a[turn, start + k]
            rows.append(total)
        return jnp.concatenate(rows, axis=0) if len(rows) > 1 else rows[0]

    def solve(turn, exact):
        per = ZG // QUAD
        sums = [jnp.zeros((KD, 128), F32) for _ in range(4)]
        for j in range(group * per):
            value = row_b[turn, j // per, pl.ds(j % per, 1), :]
            sums[j % 4] = sums[j % 4] + inv[:, pl.ds(j * 128, 128)] * value
        total = (sums[0] + sums[1]) + (sums[2] + sums[3])
        solved = jnp.sum(total, axis=1, keepdims=True)
        spread = jnp.where(
            iota((KD, KD * 16), 0) == lax.div(iota((KD, KD * 16), 1), 16), solved, 0.0
        )
        spread = jnp.sum(spread, axis=0, keepdims=True)
        shape = (16, KD * 16)
        lhs = jnp.where(iota(shape, 0) == lax.rem(iota(shape, 1), 16), spread, 0.0)
        return split(lhs) if exact else lhs.astype(BF16)

    def prolong(lhs, exact):
        for x in range(SX):
            out = jnp.dot(lhs[:, :256], weights(0, x), preferred_element_type=F32)
            out = out + jnp.dot(lhs[:, 256:], weights(1, x), preferred_element_type=F32)
            if exact:
                out = out[:16] + out[16:]
            corr[0, 3 + x] = out
            corr_plo[0, x] = out[0:4]
            corr_phi[0, x] = out[12:16]

    def smooth(turn, out_ref):
        rows = iota((ROWS, NZ), 0)
        inner = (rows >= 4) & (rows < 20)
        keep_y = inner | ((rows < 4) & has_s) | ((rows >= 20) & has_n)

        @pl.loop(0, SX + 6)
        def _(p):
            plane = padded(corr_lo[turn, p], corr[turn, p], corr_hi[turn, p])
            keep = keep_y & ((p >= 3) | has_w) & ((p < SX + 3) | has_e)
            ext[p] = jnp.where(keep, plane, 0.0)

        rho = 1.0 / SIGMA

        @pl.loop(0, SX + 4)
        def _(p):
            rest = q24[p] - stencil(p, ext[p], ext[p + 1], ext[p + 2])
            left[p] = rest
            upd = coef[4, p] * rest
            upd_a[p + 1] = upd
            est[p] = upd

        now, nxt = upd_a, upd_b
        for sweep in range(CHEB - 1):
            rho_next = 1.0 / (2.0 * SIGMA - rho)
            first, second = rho_next * rho, 2.0 * rho_next / 0.9
            lo = sweep
            last = sweep == CHEB - 2

            @pl.loop(lo, SX + 4 - lo)
            def _(p):
                rest = left[p] - stencil(p, now[p], now[p + 1], now[p + 2])
                upd = first * now[p + 1] + second * (coef[4, p] * rest)
                if last:
                    out_ref[p - 1] = (est[p] + upd) + ext[p + 1]
                else:
                    left[p] = rest
                    nxt[p + 1] = upd
                    est[p] = est[p] + upd

            rho = rho_next
            now, nxt = nxt, now

    def face_pack(turn, src):
        slot = turn - 3
        face_own[slot, 0] = src[1, pl.ds(4, 16), :]
        face_own[slot, 1] = src[SX, pl.ds(4, 16), :]

        @pl.loop(0, SX)
        def _(x):
            face_plo[slot, x] = src[x + 1, pl.ds(4, 1), :]
            face_phi[slot, x] = src[x + 1, pl.ds(19, 1), :]

    def face_place(turn, dst):
        slot = turn - 3
        zero4 = jnp.zeros((4, NZ), F32)
        dst[0] = jnp.where(has_w, jnp.concatenate([zero4, face[slot, 0], zero4], axis=0), 0.0)
        dst[SX + 1] = jnp.where(has_e, jnp.concatenate([zero4, face[slot, 1], zero4], axis=0), 0.0)
        rows = iota((ROWS, NZ), 0)

        @pl.loop(0, SX)
        def _(x):
            low = jnp.broadcast_to(jnp.where(has_s, face_lo[slot, x], 0.0), (ROWS, NZ))
            high = jnp.broadcast_to(jnp.where(has_n, face_hi[slot, x], 0.0), (ROWS, NZ))
            value = dst[x + 1]
            dst[x + 1] = jnp.where(rows == 3, low, jnp.where(rows == 20, high, value))

    def q_assemble(low, mid, high):
        @pl.loop(0, SX + 4)
        def _(p):
            q24[p] = padded(low(p), mid(p), high(p))

    for ref in (upd_a, upd_b):
        ref[0] = jnp.zeros((ROWS, NZ), F32)
        ref[SX + 5] = jnp.zeros((ROWS, NZ), F32)

    loads[0].wait()
    loads[1].wait()
    row = restrict(lambda x: base[3, DEPTH + x], FIRST_EXACT)
    loads[2].wait()

    @pl.loop(0, SX)
    def _(x):
        for c in range(4):
            plane = base[c, DEPTH + x]
            base_plo[c, x] = plane[0:2]
            base_phi[c, x] = plane[14:16]

    greetings = (ZG - 1) + (group - 1) + len(around)
    pl.semaphore_wait(barrier, greetings)
    line_send(0, row)
    every = (slice(None),)
    halo_start(0, DEPTH, base, base_lo, base_hi, base_plo, base_phi, every)
    line_wait(0)
    group_send(0, quads(0))
    halo_wait(0, DEPTH, base, base_lo, base_hi, every)

    rows = iota((ROWS, NZ), 0)
    cols = iota((ROWS, NZ), 1)
    keep_y = ((rows >= 4) & (rows < 20)) | ((rows >= 2) & (rows < 4) & has_s)
    keep_y = keep_y | ((rows >= 20) & (rows < 22) & has_n)

    @pl.loop(0, SX + 4)
    def _(p):
        w0, w1, w2, r = [padded(base_lo[c, p], base[c, p], base_hi[c, p]) for c in range(4)]
        diagonal = 6.0 + w0 + w1 + w2
        keep = keep_y & ((p >= DEPTH) | has_w) & ((p < SX + DEPTH) | has_e)
        coef[0, p] = diagonal
        coef[1, p] = 1.0 + w0
        coef[2, p] = 1.0 + w1
        coef[3, p] = jnp.where(cols == 0, 0.0, 1.0 + w2)
        coef[4, p] = jnp.where(keep, 1.0 / diagonal, 0.0)
        q24[p] = r

    loads[3].wait()

    def whole_precondition(turn, out_ref, exact, fill_q):
        group_wait(turn)
        lhs = solve(turn, exact)
        prolong_into(turn, lhs, exact)
        halo_start(1 + turn, 3, corr.at[turn], corr_lo.at[turn], corr_hi.at[turn],
                   corr_plo.at[turn], corr_phi.at[turn])
        fill_q()
        halo_wait(1 + turn, 3, corr.at[turn], corr_lo.at[turn], corr_hi.at[turn])
        smooth(turn, out_ref)
        face_pack(3 + turn, out_ref)
        face_start(3 + turn)
        face_wait(3 + turn)
        face_place(3 + turn, out_ref)

    def prolong_into(turn, lhs, exact):
        for x in range(SX):
            out = jnp.dot(lhs[:, :256], weights(0, x), preferred_element_type=F32)
            out = out + jnp.dot(lhs[:, 256:], weights(1, x), preferred_element_type=F32)
            if exact:
                out = out[:16] + out[16:]
            corr[turn, 3 + x] = out
            corr_plo[turn, x] = out[0:4]
            corr_phi[turn, x] = out[12:16]

    whole_precondition(0, search, FIRST_EXACT, lambda: None)

    @pl.loop(0, SX)
    def _(x):
        value = stencil(x + DEPTH, search[x], search[x + 1], search[x + 2])
        image[x] = value
        inner = value[4:20]
        img[DEPTH + x] = inner
        img_plo[x] = inner[0:2]
        img_phi[x] = inner[14:16]

    row = restrict(lambda x: img[DEPTH + x], True)
    line_send(1, row)
    halo_start(5, DEPTH, img, img_lo, img_hi, img_plo, img_phi)
    line_wait(1)
    group_send(1, quads(1))
    halo_wait(5, DEPTH, img, img_lo, img_hi)
    q_assemble(lambda p: img_lo[p], lambda p: img[p], lambda p: img_hi[p])
    whole_precondition(1, wfield, True, lambda: None)

    zero = jnp.zeros((8, NZ), F32)

    def fold(value):
        return value[0:8] + value[8:16]

    def products(x, sums):
        v = stencil(x + DEPTH, wfield[x], wfield[x + 1], wfield[x + 2])
        left[x] = v
        v = v[4:20]
        i = img[DEPTH + x]
        r = base[3, DEPTH + x]
        pairs = [(r, r), (r, i), (i, i), (v, r), (v, i), (v, v)]
        return tuple(s + fold(a * b) for s, (a, b) in zip(sums, pairs))

    sums = lax.fori_loop(0, SX, products, (zero,) * 6)
    lanes = iota((1, 128), 1)
    row = jnp.zeros((1, 128), F32)
    for k, s in enumerate(sums):
        s = jnp.sum(s, axis=0, keepdims=True)
        s = jnp.sum(s, axis=1, keepdims=True)
        row = jnp.where(lanes == k, s, row)
    line_send(2, row)
    line_wait(2)
    total = row_a[2, 0]
    for k in range(1, ZG):
        total = total + row_a[2, k]
    per = ZG // QUAD
    group_send(2, jnp.concatenate([total] * per, axis=0) if per > 1 else total)
    group_wait(2)
    total = jnp.sum(row_b[2], axis=0)[0:1]
    rr, ri, ii, vr, vi, vv = [
        jnp.sum(jnp.where(lanes == k, total, 0.0), axis=1, keepdims=True) for k in range(6)
    ]
    alpha = rr / ri
    cross = (ri - alpha * ii) - alpha * (vr - alpha * vi)
    square = ii - alpha * (2.0 * vi - alpha * vv)
    omega = cross / square

    @pl.loop(0, SX)
    def _(x):
        s = search[x + 1]
        i = image[x]
        sol = alpha * s + omega * (s - alpha * wfield[x + 1])
        sol_ref[x] = sol[4:20]
        shift = (alpha * i + omega * (i - alpha * left[x]))[4:20]
        res_ref[x] = base[3, DEPTH + x] - shift

    for turn in range(3):
        gather_finish(turn)
    halo_wait(0, DEPTH, base, base_lo, base_hi, every, "send")
    for turn in range(2):
        halo_wait(1 + turn, 3, corr.at[turn], corr_lo.at[turn], corr_hi.at[turn], (), "send")
        face_wait(3 + turn, "send")
    halo_wait(5, DEPTH, img, img_lo, img_hi, (), "send")


FIRST_EXACT = False


def solution(mesh):
    ngx, ngy = mesh.shape["gx"], mesh.shape["gy"]
    group = ngx * (ngy // ZG)
    vm = pltpu.VMEM

    def local(right_side, velocity, deflation, inverse_rows):
        out = jax.ShapeDtypeStruct((SX, SY, NZ), F32)
        plane = (ROWS, NZ)
        scratch = [
            vm((KD, SX, SY, NZ), BF16),
            vm(inverse_rows.shape, F32),
            vm((4, SX + 4, SY, NZ), F32),
            vm((4, SX + 4, 2, NZ), F32),
            vm((4, SX + 4, 2, NZ), F32),
            vm((4, SX, 2, NZ), F32),
            vm((4, SX, 2, NZ), F32),
            vm((5, SX + 4) + plane, F32),
            vm((SX + 4,) + plane, F32),
            vm((2, SX + 6, SY, NZ), F32),
            vm((2, SX + 6, 4, NZ), F32),
            vm((2, SX + 6, 4, NZ), F32),
            vm((2, SX, 4, NZ), F32),
            vm((2, SX, 4, NZ), F32),
            vm((SX + 6,) + plane, F32),
            vm((SX + 4,) + plane, F32),
            vm((SX + 6,) + plane, F32),
            vm((SX + 6,) + plane, F32),
            vm((SX + 4,) + plane, F32),
            vm((2, 2, SY, NZ), F32),
            vm((2, SX, 1, NZ), F32),
            vm((2, SX, 1, NZ), F32),
            vm((2, 2, SY, NZ), F32),
            vm((2, SX, 1, NZ), F32),
            vm((2, SX, 1, NZ), F32),
            vm((SX + 4, SY, NZ), F32),
            vm((SX + 4, 2, NZ), F32),
            vm((SX + 4, 2, NZ), F32),
            vm((SX, 2, NZ), F32),
            vm((SX, 2, NZ), F32),
            vm((SX + 2,) + plane, F32),
            vm((SX,) + plane, F32),
            vm((SX + 2,) + plane, F32),
            vm((3, ZG, 1, 128), F32),
            vm((3, group, ZG // QUAD, 128), F32),
            pltpu.SemaphoreType.DMA((4,)),
            pltpu.SemaphoreType.DMA((3, 2)),
            pltpu.SemaphoreType.DMA((3, 2)),
            pltpu.SemaphoreType.DMA((6, 3)),
            pltpu.SemaphoreType.DMA((6, 3)),
        ]

        def body(*refs):
            kernel(ngx, ngy, *refs)

        return pl.pallas_call(
            body,
            name="bicgstab",
            out_shape=(out, out),
            in_specs=[pl.BlockSpec(memory_space=pl.ANY)] * 4,
            out_specs=(pl.BlockSpec(memory_space=vm), pl.BlockSpec(memory_space=vm)),
            scratch_shapes=scratch,
            compiler_params=pltpu.CompilerParams(collective_id=0, has_side_effects=True),
        )(right_side, velocity, deflation, inverse_rows)

    return jax.shard_map(
        local,
        mesh=mesh,
        in_specs=(
            P("gx", "gy", None),
            P(None, "gx", "gy", None),
            P(None, "gx", "gy", None),
            P(("gx", "gy"), None),
        ),
        out_specs=(P("gx", "gy", None), P("gx", "gy", None)),
        check_vma=False,
    )
```

```python
import jax
import jax.numpy as jnp
from jax import lax
from jax.experimental import pallas as pl
from jax.experimental.pallas import tpu as pltpu
from jax.sharding import PartitionSpec as P

F32 = jnp.float32
BF16 = jnp.bfloat16
MESH = pl.DeviceIdType.MESH
SX, SY, NZ = 8, 16, 256
KD = 32
DEPTH = 2
CHEB = 4
ZG = 8
QUAD = 128 // KD
ROWS = 24
SIGMA = 1.0 / 0.9
AROUND = [(1, 1), (-1, 1), (1, -1), (-1, -1), (0, 1), (0, -1), (1, 0), (-1, 0)]


def iota(shape, dim):
    return lax.broadcasted_iota(jnp.int32, shape, dim)


def padded(low, middle, high):
    gap = 4 - low.shape[0]
    parts = [low, middle, high]
    if gap:
        fill = jnp.zeros((gap, NZ), F32)
        parts = [fill] + parts + [fill]
    return jnp.concatenate(parts, axis=0)


def kernel(
    ngx, ngy,
    r_hbm, vel_hbm, defl_hbm, inv_hbm, s_ref, i_ref, w_ref, v_ref, alpha_ref, omega_ref,
    defl, inv, base, base_lo, base_hi, base_plo, base_phi,
    coef, scale, pick, q24, corr, corr_lo, corr_hi, corr_plo, corr_phi, ext, left, upd0, upd1, upd2,
    face, face_lo, face_hi, face_own, face_plo, face_phi,
    img, img_lo, img_hi, img_plo, img_phi, search, wfield, row_a, row_b,
    local_sem, ag_send, ag_recv, halo_send, halo_recv,
):
    gx = lax.axis_index("gx")
    gy = lax.axis_index("gy")
    xg = ngy // ZG
    zpos = lax.rem(gy, ZG)
    xpos = lax.div(gy, ZG)
    line = xpos * ZG
    group = ngx * xg
    seat = gx * xg + xpos
    here = (gx, gy)
    barrier = pltpu.get_barrier_semaphore()

    def line_peer(step):
        return (gx, line + lax.rem(zpos + step, ZG))

    def group_peer(step):
        other = lax.rem(seat + step, group)
        return (lax.div(other, xg), lax.rem(other, xg) * ZG + zpos)

    def greet(device):
        pl.semaphore_signal(barrier, inc=1, device_id=device, device_id_type=MESH)

    own = pl.ds(DEPTH, SX)
    loads = [
        pltpu.make_async_copy(r_hbm, base.at[3, own], local_sem.at[0]),
        pltpu.make_async_copy(defl_hbm.at[pl.ds(0, 16)], defl.at[pl.ds(0, 16)], local_sem.at[1]),
        pltpu.make_async_copy(defl_hbm.at[pl.ds(16, 16)], defl.at[pl.ds(16, 16)], local_sem.at[2]),
        pltpu.make_async_copy(vel_hbm, base.at[pl.ds(0, 3), own], local_sem.at[3]),
        pltpu.make_async_copy(inv_hbm, inv, local_sem.at[4]),
    ]
    for load in loads:
        load.start()

    @pl.loop(1, ZG)
    def _(step):
        greet(line_peer(step))

    @pl.loop(1, group)
    def _(step):
        greet(group_peer(step))

    for dx, dy in AROUND:
        greet((lax.rem(gx + dx + ngx, ngx), lax.rem(gy + dy + ngy, ngy)))

    has_w, has_e = gx > 0, gx < ngx - 1
    has_s, has_n = gy > 0, gy < ngy - 1

    def remote(src, dst, send, recv, device):
        return pltpu.make_async_remote_copy(
            src_ref=src, dst_ref=dst, send_sem=send, recv_sem=recv,
            device_id=device, device_id_type=MESH,
        )

    def line_send(turn, row):
        row_a[turn, zpos] = row

        @pl.loop(1, ZG)
        def _(step):
            remote(row_a.at[turn, zpos], row_a.at[turn, zpos], ag_send.at[turn, 0],
                   ag_recv.at[turn, 0], line_peer(step)).start()

    def line_wait(turn):
        view = row_a.at[turn, pl.ds(0, ZG - 1)]
        remote(view, view, ag_send.at[turn, 0], ag_recv.at[turn, 0], here).wait_recv()

    def group_send(turn, rows):
        row_b[turn, seat] = rows

        @pl.loop(1, group)
        def _(step):
            remote(row_b.at[turn, seat], row_b.at[turn, seat], ag_send.at[turn, 1],
                   ag_recv.at[turn, 1], group_peer(step)).start()

    def group_wait(turn):
        view = row_b.at[turn, pl.ds(0, group - 1)]
        remote(view, view, ag_send.at[turn, 1], ag_recv.at[turn, 1], here).wait_recv()

    def gather_finish(turn):
        view = row_a.at[turn, pl.ds(0, ZG - 1)]
        remote(view, view, ag_send.at[turn, 0], ag_recv.at[turn, 0], here).wait_send()
        view = row_b.at[turn, pl.ds(0, group - 1)]
        remote(view, view, ag_send.at[turn, 1], ag_recv.at[turn, 1], here).wait_send()

    def beside(dx, dy):
        tests = {(-1, 0): has_w, (1, 0): has_e, (0, -1): has_s, (0, 1): has_n}
        first = tests.get((dx, 0)) if dx else None
        second = tests.get((0, dy)) if dy else None
        if first is None:
            return second
        return first if second is None else first & second

    def halo(what, turn, width, mid, low, high, plow, phigh, lead=()):
        w = width
        for k, (dx, dy) in enumerate(AROUND):
            size = w if dx else SX
            take = {1: SX - w, -1: 0, 0: 0}[dx]
            put = {1: 0, -1: w + SX, 0: w}[dx]
            source = {1: phigh, -1: plow, 0: mid}[dy]
            target = {1: low, -1: high, 0: mid}[dy]
            src = source.at[lead + (pl.ds(take + (0 if dy else w), size),)]
            dst = target.at[lead + (pl.ds(put, size),)]
            copy = remote(
                src, dst, halo_send.at[turn, k], halo_recv.at[turn, k],
                (gx + dx, gy + dy) if what == "start" else here,
            )
            act(what, copy, dx, dy)

    def act(what, copy, dx, dy):
        sign = -1 if what == "recv" else 1

        @pl.when(beside(sign * dx, sign * dy))
        def _():
            if what == "start":
                copy.start()
            elif what == "recv":
                copy.wait_recv()
            else:
                copy.wait_send()

    def faces(what, slot):
        pairs = [
            ((1, 0), face_own.at[slot, 1], face.at[slot, 0]),
            ((-1, 0), face_own.at[slot, 0], face.at[slot, 1]),
            ((0, 1), face_phi.at[slot], face_lo.at[slot]),
            ((0, -1), face_plo.at[slot], face_hi.at[slot]),
        ]
        for k, ((dx, dy), src, dst) in enumerate(pairs):
            copy = remote(
                src, dst, halo_send.at[4 + slot, k], halo_recv.at[4 + slot, k],
                (gx + dx, gy + dy) if what == "start" else here,
            )
            act(what, copy, dx, dy)

    lane_end = iota((ROWS, NZ), 1) == NZ - 1

    def shifts(before, centre, after, add, c0, c1, c2):
        ahead = jnp.where(lane_end, 0.0, pltpu.roll(centre, NZ - 1, 1))
        nexts = (after + pltpu.roll(centre, ROWS - 1, 0)) + ahead
        if add is not None:
            nexts = nexts + add
        previous = c0 * before + c1 * pltpu.roll(centre, 1, 0)
        return nexts, previous + c2 * pltpu.roll(centre, 1, 1)

    def operator(x, field):
        nexts, previous = shifts(
            field[x], field[x + 1], field[x + 2], None, coef[1, x], coef[2, x], coef[3, x]
        )
        return coef[0, x] * field[x + 1] - (nexts + previous)

    def split(value):
        top = value.astype(BF16)
        rest = (value - top.astype(F32)).astype(BF16)
        return jnp.concatenate([top, rest], axis=0)

    def weights(half, x):
        return defl[pl.ds(half * 16, 16), x].reshape(256, NZ)

    def restrict(plane, exact, ready=(None, None)):
        lhs = [split(plane(x)) if exact else plane(x).astype(BF16) for x in range(SX)]
        packed = []
        for half in range(2):
            if ready[half] is not None:
                ready[half].wait()
            total = None
            for x in range(SX):
                part = lax.dot_general(
                    lhs[x], weights(half, x), (((1,), (1,)), ((), ())), preferred_element_type=F32
                )
                total = part if total is None else total + part
            same = lax.rem(iota(total.shape, 0), 16) == lax.rem(iota(total.shape, 1), 16)
            kept = jnp.where(same, total, 0.0)
            packed.append(jnp.sum(kept.reshape(-1, 8, 256), axis=0))
        packed = jnp.concatenate(packed, axis=1)
        high = packed.astype(BF16).astype(F32)
        rest = packed - high
        middle = rest.astype(BF16).astype(F32)
        low = rest - middle
        stack = jnp.concatenate([high, middle, low, jnp.zeros_like(low)], axis=0).astype(BF16)
        row = jnp.dot(stack, pick[...], preferred_element_type=F32)
        row = jnp.sum(row, axis=0, keepdims=True)
        mine = lax.div(iota((1, 128), 1), KD) == lax.rem(zpos, QUAD)
        return jnp.where(mine, row, 0.0)

    def quads(turn):
        rows = []
        for start in range(0, ZG, QUAD):
            total = row_a[turn, start]
            for k in range(1, QUAD):
                total = total + row_a[turn, start + k]
            rows.append(total)
        return jnp.concatenate(rows, axis=0) if len(rows) > 1 else rows[0]

    def solve(turn, exact):
        per = ZG // QUAD
        sums = [jnp.zeros((KD, 128), F32) for _ in range(4)]
        for j in range(group * per):
            value = row_b[turn, j // per, pl.ds(j % per, 1), :]
            sums[j % 4] = sums[j % 4] + inv[:, pl.ds(j * 128, 128)] * value
        total = (sums[0] + sums[1]) + (sums[2] + sums[3])
        solved = jnp.sum(total, axis=1, keepdims=True)
        spread = jnp.where(
            iota((KD, KD * 16), 0) == lax.div(iota((KD, KD * 16), 1), 16), solved, 0.0
        )
        spread = jnp.sum(spread, axis=0, keepdims=True)
        shape = (16, KD * 16)
        lhs = jnp.where(iota(shape, 0) == lax.rem(iota(shape, 1), 16), spread, 0.0)
        return split(lhs) if exact else lhs.astype(BF16)

    def smooth(turn, out_ref, own_ref):
        rows = iota((ROWS, NZ), 0)
        keep_y = ((rows >= 4) & (rows < 20)) | ((rows < 4) & has_s) | ((rows >= 20) & has_n)
        box = (rows >= 2) & (rows < 22)

        @pl.loop(0, SX + 6, unroll=2)
        def _(p):
            plane = padded(corr_lo[turn, p], corr[turn, p], corr_hi[turn, p])
            keep = keep_y & ((p >= 3) | has_w) & ((p < SX + 3) | has_e)
            ext[p] = jnp.where(keep, plane, 0.0)

        def scaled(p, before, centre, after, add):
            nexts, previous = shifts(before, centre, after, add, scale[1, p], scale[2, p], scale[3, p])
            return scale[0, p] * nexts + previous

        @pl.loop(0, SX + 4, unroll=4)
        def _(p):
            centre = ext[p + 1]
            total = scaled(p, ext[p], centre, ext[p + 2], q24[p])
            upd0[p + 1] = total - jnp.where(box, centre, 0.0)

        rho = 1.0 / SIGMA
        factors = []
        for sweep in range(CHEB - 1):
            rho_next = 1.0 / (2.0 * SIGMA - rho)
            factors.append((rho_next * rho, 2.0 * rho_next / 0.9))
            rho = rho_next

        @pl.loop(0, SX + 4, unroll=4)
        def _(p):
            centre = upd0[p + 1]
            rest = scaled(p, upd0[p], centre, upd0[p + 2], None)
            left[p] = rest
            upd1[p] = factors[0][0] * centre + factors[0][1] * rest

        @pl.loop(1, SX + 3, unroll=5)
        def _(p):
            centre = upd1[p]
            rest = (left[p] - centre) + scaled(p, upd1[p - 1], centre, upd1[p + 1], None)
            left[p] = rest
            upd2[p] = factors[1][0] * centre + factors[1][1] * rest

        @pl.loop(2, SX + 2, unroll=4)
        def _(p):
            centre = upd2[p]
            rest = (left[p] - centre) + scaled(p, upd2[p - 1], centre, upd2[p + 1], None)
            upd3 = factors[2][0] * centre + factors[2][1] * rest
            value = ((upd0[p + 1] + upd1[p]) + (centre + upd3)) + ext[p + 1]
            out_ref[p - 1] = value
            inner = value[4:20]
            own_ref[p - 2] = inner
            face_plo[turn, p - 2] = inner[0:1]
            face_phi[turn, p - 2] = inner[15:16]

    def face_place(slot, dst):
        zero4 = jnp.zeros((4, NZ), F32)
        dst[0] = jnp.where(has_w, jnp.concatenate([zero4, face[slot, 0], zero4], axis=0), 0.0)
        dst[SX + 1] = jnp.where(has_e, jnp.concatenate([zero4, face[slot, 1], zero4], axis=0), 0.0)
        rows = iota((ROWS, NZ), 0)

        @pl.loop(0, SX, unroll=2)
        def _(x):
            low = jnp.broadcast_to(jnp.where(has_s, face_lo[slot, x], 0.0), (ROWS, NZ))
            high = jnp.broadcast_to(jnp.where(has_n, face_hi[slot, x], 0.0), (ROWS, NZ))
            value = dst[x + 1]
            dst[x + 1] = jnp.where(rows == 3, low, jnp.where(rows == 20, high, value))

    def q_assemble(low, mid, high):
        @pl.loop(0, SX + 4)
        def _(p):
            q24[p] = padded(low(p), mid(p), high(p))

    upd0[0] = jnp.zeros((ROWS, NZ), F32)
    upd0[SX + 5] = jnp.zeros((ROWS, NZ), F32)
    table = lax.div(iota((KD * 16, 128), 0), 16) == lax.rem(iota((KD * 16, 128), 1), KD)
    pick[...] = jnp.where(table, 1.0, 0.0).astype(BF16)
    loads[0].wait()
    row = restrict(lambda x: base[3, DEPTH + x], FIRST_EXACT, (loads[1], loads[2]))
    greetings = (ZG - 1) + (group - 1) + len(AROUND)
    pl.semaphore_wait(barrier, greetings)
    line_send(0, row)
    loads[3].wait()

    @pl.loop(0, SX)
    def _(x):
        for c in range(4):
            plane = base[c, DEPTH + x]
            base_plo[c, x] = plane[0:2]
            base_phi[c, x] = plane[14:16]

    every = (slice(None),)
    base_halo = (0, DEPTH, base, base_lo, base_hi, base_plo, base_phi, every)
    img_halo = (3, DEPTH, img, img_lo, img_hi, img_plo, img_phi)

    def corr_halo(turn):
        return (1 + turn, 3, corr.at[turn], corr_lo.at[turn], corr_hi.at[turn],
                corr_plo.at[turn], corr_phi.at[turn])

    halo("start", *base_halo)
    line_wait(0)
    group_send(0, quads(0))
    halo("recv", *base_halo)

    rows = iota((ROWS, NZ), 0)
    cols = iota((ROWS, NZ), 1)
    keep_y = ((rows >= 4) & (rows < 20)) | ((rows >= 2) & (rows < 4) & has_s)
    keep_y = keep_y | ((rows >= 20) & (rows < 22) & has_n)

    @pl.loop(0, SX + 4)
    def _(p):
        keep = keep_y & ((p >= DEPTH) | has_w) & ((p < SX + DEPTH) | has_e)
        w0, w1, w2, r = [
            jnp.where(keep, padded(base_lo[c, p], base[c, p], base_hi[c, p]), 0.0)
            for c in range(4)
        ]
        diagonal = 6.0 + w0 + w1 + w2
        jdiag = jnp.where(keep, 1.0 / diagonal, 0.0)
        c0, c1 = 1.0 + w0, 1.0 + w1
        c2 = jnp.where(cols == 0, 0.0, 1.0 + w2)
        scale[0, p] = jdiag
        scale[1, p] = jdiag * c0
        scale[2, p] = jdiag * c1
        scale[3, p] = jdiag * c2
        q24[p] = r

        @pl.when((p >= DEPTH) & (p < SX + DEPTH))
        def _():
            coef[0, p - DEPTH] = diagonal
            coef[1, p - DEPTH] = c0
            coef[2, p - DEPTH] = c1
            coef[3, p - DEPTH] = c2

    loads[4].wait()

    def precondition(turn, out_ref, own_ref, exact):
        group_wait(turn)
        lhs = solve(turn, exact)
        for x in range(SX):
            out = jnp.dot(lhs[:, :256], weights(0, x), preferred_element_type=F32)
            out = out + jnp.dot(lhs[:, 256:], weights(1, x), preferred_element_type=F32)
            if exact:
                out = out[:16] + out[16:]
            corr[turn, 3 + x] = out
            corr_plo[turn, x] = out[0:4]
            corr_phi[turn, x] = out[12:16]
        halo("start", *corr_halo(turn))
        halo("recv", *corr_halo(turn))
        smooth(turn, out_ref, own_ref)
        face_own[turn, 0] = own_ref[0]
        face_own[turn, 1] = own_ref[SX - 1]
        faces("start", turn)
        faces("recv", turn)
        face_place(turn, out_ref)

    precondition(0, search, s_ref, FIRST_EXACT)

    @pl.loop(0, SX, unroll=2)
    def _(x):
        inner = operator(x, search)[4:20]
        img[DEPTH + x] = inner
        i_ref[x] = inner
        img_plo[x] = inner[0:2]
        img_phi[x] = inner[14:16]

    row = restrict(lambda x: img[DEPTH + x], True)
    line_send(1, row)
    halo("start", *img_halo)
    line_wait(1)
    group_send(1, quads(1))
    halo("recv", *img_halo)
    keep_q = keep_y

    @pl.loop(0, SX + 4)
    def _(p):
        keep = keep_q & ((p >= DEPTH) | has_w) & ((p < SX + DEPTH) | has_e)
        q24[p] = jnp.where(keep, padded(img_lo[p], img[p], img_hi[p]), 0.0)

    precondition(1, wfield, w_ref, True)

    zero = jnp.zeros((8, NZ), F32)

    def fold(value):
        return value[0:8] + value[8:16]

    def products(x, sums):
        v = operator(x, wfield)[4:20]
        v_ref[x] = v
        i = img[DEPTH + x]
        r = base[3, DEPTH + x]
        pairs = [(r, r), (r, i), (i, i), (v, r), (v, i), (v, v)]
        return tuple(s + fold(a * b) for s, (a, b) in zip(sums, pairs))

    sums = lax.fori_loop(0, SX, products, (zero,) * 6, unroll=2)
    lanes = iota((1, 128), 1)
    row = jnp.zeros((1, 128), F32)
    for k, s in enumerate(sums):
        s = jnp.sum(s, axis=0, keepdims=True)
        s = jnp.sum(s, axis=1, keepdims=True)
        row = jnp.where(lanes == k, s, row)
    line_send(2, row)
    line_wait(2)
    total = row_a[2, 0]
    for k in range(1, ZG):
        total = total + row_a[2, k]
    per = ZG // QUAD
    group_send(2, jnp.concatenate([total] * per, axis=0) if per > 1 else total)
    group_wait(2)
    total = jnp.sum(row_b[2], axis=0)[0:1]
    rr, ri, ii, vr, vi, vv = [
        jnp.sum(jnp.where(lanes == k, total, 0.0), axis=1, keepdims=True) for k in range(6)
    ]
    alpha = rr / ri
    cross = (ri - alpha * ii) - alpha * (vr - alpha * vi)
    square = ii - alpha * (2.0 * vi - alpha * vv)
    omega = cross / square
    alpha_ref[...] = alpha
    omega_ref[...] = omega

    for turn in range(3):
        gather_finish(turn)
    halo("send", *base_halo)
    for turn in range(2):
        halo("send", *corr_halo(turn))
        faces("send", turn)
    halo("send", *img_halo)


FIRST_EXACT = False


def solution(mesh):
    ngx, ngy = mesh.shape["gx"], mesh.shape["gy"]
    group = ngx * (ngy // ZG)
    vm = pltpu.VMEM

    def local(right_side, velocity, deflation, inverse_rows):
        out = jax.ShapeDtypeStruct((SX, SY, NZ), F32)
        plane = (ROWS, NZ)
        scratch = [
            vm((KD, SX, SY, NZ), BF16),
            vm(inverse_rows.shape, F32),
            vm((4, SX + 4, SY, NZ), F32),
            vm((4, SX + 4, 2, NZ), F32),
            vm((4, SX + 4, 2, NZ), F32),
            vm((4, SX, 2, NZ), F32),
            vm((4, SX, 2, NZ), F32),
            vm((4, SX) + plane, F32),
            vm((4, SX + 4) + plane, F32),
            vm((KD * 16, 128), BF16),
            vm((SX + 4,) + plane, F32),
            vm((2, SX + 6, SY, NZ), F32),
            vm((2, SX + 6, 4, NZ), F32),
            vm((2, SX + 6, 4, NZ), F32),
            vm((2, SX, 4, NZ), F32),
            vm((2, SX, 4, NZ), F32),
            vm((SX + 6,) + plane, F32),
            vm((SX + 4,) + plane, F32),
            vm((SX + 6,) + plane, F32),
            vm((SX + 4,) + plane, F32),
            vm((SX + 4,) + plane, F32),
            vm((2, 2, SY, NZ), F32),
            vm((2, SX, 1, NZ), F32),
            vm((2, SX, 1, NZ), F32),
            vm((2, 2, SY, NZ), F32),
            vm((2, SX, 1, NZ), F32),
            vm((2, SX, 1, NZ), F32),
            vm((SX + 4, SY, NZ), F32),
            vm((SX + 4, 2, NZ), F32),
            vm((SX + 4, 2, NZ), F32),
            vm((SX, 2, NZ), F32),
            vm((SX, 2, NZ), F32),
            vm((SX + 2,) + plane, F32),
            vm((SX + 2,) + plane, F32),
            vm((3, ZG, 1, 128), F32),
            vm((3, group, ZG // QUAD, 128), F32),
            pltpu.SemaphoreType.DMA((5,)),
            pltpu.SemaphoreType.DMA((3, 2)),
            pltpu.SemaphoreType.DMA((3, 2)),
            pltpu.SemaphoreType.DMA((6, 8)),
            pltpu.SemaphoreType.DMA((6, 8)),
        ]

        def body(*refs):
            kernel(ngx, ngy, *refs)

        s, i, w, v, alpha, omega = pl.pallas_call(
            body,
            name="bicgstab",
            out_shape=(out,) * 4 + (jax.ShapeDtypeStruct((1, 1), F32),) * 2,
            in_specs=[pl.BlockSpec(memory_space=pl.ANY)] * 4,
            out_specs=(pl.BlockSpec(memory_space=vm),) * 6,
            scratch_shapes=scratch,
            compiler_params=pltpu.CompilerParams(collective_id=0, has_side_effects=True),
        )(right_side, velocity, deflation, inverse_rows)
        alpha, omega = alpha[0, 0], omega[0, 0]
        field = alpha * s + omega * (s - alpha * w)
        return field, (right_side - alpha * i) - omega * (i - alpha * v)

    return jax.shard_map(
        local,
        mesh=mesh,
        in_specs=(
            P("gx", "gy", None),
            P(None, "gx", "gy", None),
            P(None, "gx", "gy", None),
            P(("gx", "gy"), None),
        ),
        out_specs=(P("gx", "gy", None), P("gx", "gy", None)),
        check_vma=False,
    )
```

```python
import jax
import jax.numpy as jnp
from jax import lax
from jax.experimental import pallas as pl
from jax.experimental.pallas import tpu as pltpu
from jax.sharding import PartitionSpec as P

F32 = jnp.float32
BF16 = jnp.bfloat16
MESH = pl.DeviceIdType.MESH
SX, SY, NZ = 8, 16, 256
KD = 32
DEPTH = 2
CHEB = 4
ZG = 8
QUAD = 128 // KD
ROWS = 24
SIGMA = 1.0 / 0.9
FAR_FIRST = [4, 3, 5, 2, 6, 1, 7, 0]
AROUND = [(1, 1), (-1, 1), (1, -1), (-1, -1), (0, 1), (0, -1), (1, 0), (-1, 0)]


def iota(shape, dim):
    return lax.broadcasted_iota(jnp.int32, shape, dim)


def padded(low, middle, high):
    gap = 4 - low.shape[0]
    parts = [low, middle, high]
    if gap:
        fill = jnp.zeros((gap, NZ), F32)
        parts = [fill] + parts + [fill]
    return jnp.concatenate(parts, axis=0)


def kernel(
    ngx, ngy,
    r_hbm, vel_hbm, defl_hbm, inv_hbm, s_hbm, i_hbm, w_hbm, v_hbm, alpha_ref, omega_ref,
    defl, inv, base, base_lo, base_hi, base_plo, base_phi,
    coef, scale, pick, q24, corr, corr_lo, corr_hi, corr_plo, corr_phi, ext, left, upd0, upd1, upd2,
    face, face_lo, face_hi, face_own, face_plo, face_phi,
    img, img_lo, img_hi, img_plo, img_phi, search, wfield, s_own, w_own, v_own, row_a, row_b, row_all,
    local_sem, out_sem, ag_send, ag_recv, all_sends, all_recvs, halo_send, halo_recv,
):
    gx = lax.axis_index("gx")
    gy = lax.axis_index("gy")
    xg = ngy // ZG
    zpos = lax.rem(gy, ZG)
    xpos = lax.div(gy, ZG)
    line = xpos * ZG
    group = ngx * xg
    seat = gx * xg + xpos
    number = gx * ngy + gy
    here = (gx, gy)
    barrier = pltpu.get_barrier_semaphore()

    def line_peer(step):
        return (gx, line + lax.rem(zpos + step, ZG))

    def group_peer(step):
        other = lax.rem(seat + step, group)
        return (lax.div(other, xg), lax.rem(other, xg) * ZG + zpos)

    def greet(device):
        pl.semaphore_signal(barrier, inc=1, device_id=device, device_id_type=MESH)

    own = pl.ds(DEPTH, SX)
    loads = [
        pltpu.make_async_copy(r_hbm, base.at[3, own], local_sem.at[0]),
        pltpu.make_async_copy(defl_hbm.at[pl.ds(0, 16)], defl.at[pl.ds(0, 16)], local_sem.at[1]),
        pltpu.make_async_copy(defl_hbm.at[pl.ds(16, 16)], defl.at[pl.ds(16, 16)], local_sem.at[2]),
        pltpu.make_async_copy(vel_hbm, base.at[pl.ds(0, 3), own], local_sem.at[3]),
        pltpu.make_async_copy(inv_hbm, inv, local_sem.at[4]),
    ]
    for load in loads:
        load.start()

    @pl.loop(1, ZG)
    def _(step):
        greet(line_peer(step))

    @pl.loop(1, group)
    def _(step):
        greet(group_peer(step))

    for dx, dy in AROUND:
        greet((lax.rem(gx + dx + ngx, ngx), lax.rem(gy + dy + ngy, ngy)))

    has_w, has_e = gx > 0, gx < ngx - 1
    has_s, has_n = gy > 0, gy < ngy - 1

    def remote(src, dst, send, recv, device):
        return pltpu.make_async_remote_copy(
            src_ref=src, dst_ref=dst, send_sem=send, recv_sem=recv,
            device_id=device, device_id_type=MESH,
        )

    def line_send(row):
        row_a[zpos] = row

        @pl.loop(1, ZG)
        def _(step):
            remote(row_a.at[zpos], row_a.at[zpos], ag_send.at[0], ag_recv.at[0],
                   line_peer(step)).start()

    def line_wait():
        view = row_a.at[pl.ds(0, ZG - 1)]
        remote(view, view, ag_send.at[0], ag_recv.at[0], here).wait_recv()

    def group_send(rows):
        row_b[seat] = rows

        @pl.loop(1, group)
        def _(step):
            remote(row_b.at[seat], row_b.at[seat], ag_send.at[1], ag_recv.at[1],
                   group_peer(step)).start()

    def group_wait():
        view = row_b.at[pl.ds(0, group - 1)]
        remote(view, view, ag_send.at[1], ag_recv.at[1], here).wait_recv()

    def all_send(turn, row):
        slot = turn - 1
        row_all[slot, number] = row

        for dz in FAR_FIRST:
            side = lax.rem(zpos + dz, ZG)

            @pl.loop(0 if dz else 1, group, unroll=8 if dz else 1)
            def _(step):
                other = lax.rem(seat + step, group)
                device = (lax.div(other, xg), lax.rem(other, xg) * ZG + side)
                remote(row_all.at[slot, number], row_all.at[slot, number], all_sends.at[slot],
                       all_recvs.at[slot], device).start()

    def all_wait(turn, what="recv"):
        slot = turn - 1
        view = row_all.at[slot, pl.ds(0, ngx * ngy - 1)]
        copy = remote(view, view, all_sends.at[slot], all_recvs.at[slot], here)
        if what == "recv":
            copy.wait_recv()
        else:
            copy.wait_send()

    def first_finish():
        view = row_a.at[pl.ds(0, ZG - 1)]
        remote(view, view, ag_send.at[0], ag_recv.at[0], here).wait_send()
        view = row_b.at[pl.ds(0, group - 1)]
        remote(view, view, ag_send.at[1], ag_recv.at[1], here).wait_send()

    def beside(dx, dy):
        tests = {(-1, 0): has_w, (1, 0): has_e, (0, -1): has_s, (0, 1): has_n}
        first = tests.get((dx, 0)) if dx else None
        second = tests.get((0, dy)) if dy else None
        if first is None:
            return second
        return first if second is None else first & second

    def halo(what, turn, width, mid, low, high, plow, phigh, lead=()):
        w = width
        for k, (dx, dy) in enumerate(AROUND):
            size = w if dx else SX
            take = {1: SX - w, -1: 0, 0: 0}[dx]
            put = {1: 0, -1: w + SX, 0: w}[dx]
            source = {1: phigh, -1: plow, 0: mid}[dy]
            target = {1: low, -1: high, 0: mid}[dy]
            src = source.at[lead + (pl.ds(take + (0 if dy else w), size),)]
            dst = target.at[lead + (pl.ds(put, size),)]
            copy = remote(
                src, dst, halo_send.at[turn, k], halo_recv.at[turn, k],
                (gx + dx, gy + dy) if what == "start" else here,
            )
            act(what, copy, dx, dy)

    def act(what, copy, dx, dy):
        sign = -1 if what == "recv" else 1

        @pl.when(beside(sign * dx, sign * dy))
        def _():
            if what == "start":
                copy.start()
            elif what == "recv":
                copy.wait_recv()
            else:
                copy.wait_send()

    def faces(what, slot):
        pairs = [
            ((1, 0), face_own.at[slot, 1], face.at[slot, 0]),
            ((-1, 0), face_own.at[slot, 0], face.at[slot, 1]),
            ((0, 1), face_phi.at[slot], face_lo.at[slot]),
            ((0, -1), face_plo.at[slot], face_hi.at[slot]),
        ]
        for k, ((dx, dy), src, dst) in enumerate(pairs):
            copy = remote(
                src, dst, halo_send.at[4 + slot, k], halo_recv.at[4 + slot, k],
                (gx + dx, gy + dy) if what == "start" else here,
            )
            act(what, copy, dx, dy)

    lane_end = iota((ROWS, NZ), 1) == NZ - 1

    def shifts(before, centre, after, add, c0, c1, c2):
        ahead = jnp.where(lane_end, 0.0, pltpu.roll(centre, NZ - 1, 1))
        nexts = (after + pltpu.roll(centre, ROWS - 1, 0)) + ahead
        if add is not None:
            nexts = nexts + add
        previous = c0 * before + c1 * pltpu.roll(centre, 1, 0)
        return nexts, previous + c2 * pltpu.roll(centre, 1, 1)

    def operator(x, field):
        nexts, previous = shifts(
            field[x], field[x + 1], field[x + 2], None, coef[1, x], coef[2, x], coef[3, x]
        )
        return coef[0, x] * field[x + 1] - (nexts + previous)

    def split(value):
        top = value.astype(BF16)
        rest = (value - top.astype(F32)).astype(BF16)
        return jnp.concatenate([top, rest], axis=0)

    def weights(half, x):
        return defl[pl.ds(half * 16, 16), x].reshape(256, NZ)

    def restrict(plane, exact, ready=(None, None)):
        lhs = [split(plane(x)) if exact else plane(x).astype(BF16) for x in range(SX)]
        packed = []
        for half in range(2):
            if ready[half] is not None:
                ready[half].wait()
            total = None
            for x in range(SX):
                part = lax.dot_general(
                    lhs[x], weights(half, x), (((1,), (1,)), ((), ())), preferred_element_type=F32
                )
                total = part if total is None else total + part
            same = lax.rem(iota(total.shape, 0), 16) == lax.rem(iota(total.shape, 1), 16)
            kept = jnp.where(same, total, 0.0)
            packed.append(jnp.sum(kept.reshape(-1, 8, 256), axis=0))
        packed = jnp.concatenate(packed, axis=1)
        high = packed.astype(BF16).astype(F32)
        rest = packed - high
        middle = rest.astype(BF16).astype(F32)
        low = rest - middle
        stack = jnp.concatenate([high, middle, low, jnp.zeros_like(low)], axis=0).astype(BF16)
        row = jnp.dot(stack, pick[...], preferred_element_type=F32)
        row = jnp.sum(row, axis=0, keepdims=True)
        mine = lax.div(iota((1, 128), 1), KD) == lax.rem(zpos, QUAD)
        return jnp.where(mine, row, 0.0)

    def quads():
        rows = []
        for start in range(0, ZG, QUAD):
            total = row_a[start]
            for k in range(1, QUAD):
                total = total + row_a[start + k]
            rows.append(total)
        return jnp.concatenate(rows, axis=0) if len(rows) > 1 else rows[0]

    def solve(turn, exact):
        per = ZG // QUAD
        sums = [jnp.zeros((KD, 128), F32) for _ in range(4)]
        for j in range(group * per):
            if turn == 0:
                value = row_b[j // per, pl.ds(j % per, 1), :]
            else:
                first, second, third, fourth = [row_all[0, QUAD * j + k] for k in range(QUAD)]
                value = (first + second) + (third + fourth)
            sums[j % 4] = sums[j % 4] + inv[:, pl.ds(j * 128, 128)] * value
        total = (sums[0] + sums[1]) + (sums[2] + sums[3])
        solved = jnp.sum(total, axis=1, keepdims=True)
        spread = jnp.where(
            iota((KD, KD * 16), 0) == lax.div(iota((KD, KD * 16), 1), 16), solved, 0.0
        )
        spread = jnp.sum(spread, axis=0, keepdims=True)
        shape = (16, KD * 16)
        lhs = jnp.where(iota(shape, 0) == lax.rem(iota(shape, 1), 16), spread, 0.0)
        return split(lhs) if exact else lhs.astype(BF16)

    def smooth(turn, out_ref, own_ref):
        rows = iota((ROWS, NZ), 0)
        keep_y = ((rows >= 4) & (rows < 20)) | ((rows < 4) & has_s) | ((rows >= 20) & has_n)
        box = (rows >= 2) & (rows < 22)

        @pl.loop(0, SX + 6, unroll=2)
        def _(p):
            plane = padded(corr_lo[turn, p], corr[turn, p], corr_hi[turn, p])
            keep = keep_y & ((p >= 3) | has_w) & ((p < SX + 3) | has_e)
            ext[p] = jnp.where(keep, plane, 0.0)

        def scaled(p, before, centre, after, add):
            nexts, previous = shifts(before, centre, after, add, scale[1, p], scale[2, p], scale[3, p])
            return scale[0, p] * nexts + previous

        @pl.loop(0, SX + 4, unroll=4)
        def _(p):
            centre = ext[p + 1]
            total = scaled(p, ext[p], centre, ext[p + 2], q24[p])
            upd0[p + 1] = total - jnp.where(box, centre, 0.0)

        rho = 1.0 / SIGMA
        factors = []
        for sweep in range(CHEB - 1):
            rho_next = 1.0 / (2.0 * SIGMA - rho)
            factors.append((rho_next * rho, 2.0 * rho_next / 0.9))
            rho = rho_next

        @pl.loop(0, SX + 4, unroll=4)
        def _(p):
            centre = upd0[p + 1]
            rest = scaled(p, upd0[p], centre, upd0[p + 2], None)
            left[p] = rest
            upd1[p] = factors[0][0] * centre + factors[0][1] * rest

        @pl.loop(1, SX + 3, unroll=5)
        def _(p):
            centre = upd1[p]
            rest = (left[p] - centre) + scaled(p, upd1[p - 1], centre, upd1[p + 1], None)
            left[p] = rest
            upd2[p] = factors[1][0] * centre + factors[1][1] * rest

        @pl.loop(2, SX + 2, unroll=4)
        def _(p):
            centre = upd2[p]
            rest = (left[p] - centre) + scaled(p, upd2[p - 1], centre, upd2[p + 1], None)
            upd3 = factors[2][0] * centre + factors[2][1] * rest
            value = ((upd0[p + 1] + upd1[p]) + (centre + upd3)) + ext[p + 1]
            out_ref[p - 1] = value
            inner = value[4:20]
            own_ref[p - 2] = inner
            face_plo[turn, p - 2] = inner[0:1]
            face_phi[turn, p - 2] = inner[15:16]

    def face_place(slot, dst):
        zero4 = jnp.zeros((4, NZ), F32)
        dst[0] = jnp.where(has_w, jnp.concatenate([zero4, face[slot, 0], zero4], axis=0), 0.0)
        dst[SX + 1] = jnp.where(has_e, jnp.concatenate([zero4, face[slot, 1], zero4], axis=0), 0.0)
        rows = iota((ROWS, NZ), 0)

        @pl.loop(0, SX, unroll=2)
        def _(x):
            low = jnp.broadcast_to(jnp.where(has_s, face_lo[slot, x], 0.0), (ROWS, NZ))
            high = jnp.broadcast_to(jnp.where(has_n, face_hi[slot, x], 0.0), (ROWS, NZ))
            value = dst[x + 1]
            dst[x + 1] = jnp.where(rows == 3, low, jnp.where(rows == 20, high, value))

    def q_assemble(low, mid, high):
        @pl.loop(0, SX + 4)
        def _(p):
            q24[p] = padded(low(p), mid(p), high(p))

    upd0[0] = jnp.zeros((ROWS, NZ), F32)
    upd0[SX + 5] = jnp.zeros((ROWS, NZ), F32)
    table = lax.div(iota((KD * 16, 128), 0), 16) == lax.rem(iota((KD * 16, 128), 1), KD)
    pick[...] = jnp.where(table, 1.0, 0.0).astype(BF16)
    loads[0].wait()
    row = restrict(lambda x: base[3, DEPTH + x], FIRST_EXACT, (loads[1], loads[2]))
    greetings = (ZG - 1) + (group - 1) + len(AROUND)
    pl.semaphore_wait(barrier, greetings)
    line_send(row)
    loads[3].wait()

    @pl.loop(0, SX)
    def _(x):
        for c in range(4):
            plane = base[c, DEPTH + x]
            base_plo[c, x] = plane[0:2]
            base_phi[c, x] = plane[14:16]

    every = (slice(None),)
    base_halo = (0, DEPTH, base, base_lo, base_hi, base_plo, base_phi, every)
    img_halo = (3, DEPTH, img, img_lo, img_hi, img_plo, img_phi)

    def corr_halo(turn):
        return (1 + turn, 3, corr.at[turn], corr_lo.at[turn], corr_hi.at[turn],
                corr_plo.at[turn], corr_phi.at[turn])

    halo("start", *base_halo)
    line_wait()
    group_send(quads())
    halo("recv", *base_halo)

    rows = iota((ROWS, NZ), 0)
    cols = iota((ROWS, NZ), 1)
    keep_y = ((rows >= 4) & (rows < 20)) | ((rows >= 2) & (rows < 4) & has_s)
    keep_y = keep_y | ((rows >= 20) & (rows < 22) & has_n)

    @pl.loop(0, SX + 4)
    def _(p):
        keep = keep_y & ((p >= DEPTH) | has_w) & ((p < SX + DEPTH) | has_e)
        w0, w1, w2, r = [
            jnp.where(keep, padded(base_lo[c, p], base[c, p], base_hi[c, p]), 0.0)
            for c in range(4)
        ]
        diagonal = 6.0 + w0 + w1 + w2
        jdiag = jnp.where(keep, 1.0 / diagonal, 0.0)
        c0, c1 = 1.0 + w0, 1.0 + w1
        c2 = jnp.where(cols == 0, 0.0, 1.0 + w2)
        scale[0, p] = jdiag
        scale[1, p] = jdiag * c0
        scale[2, p] = jdiag * c1
        scale[3, p] = jdiag * c2
        q24[p] = r

        @pl.when((p >= DEPTH) & (p < SX + DEPTH))
        def _():
            coef[0, p - DEPTH] = diagonal
            coef[1, p - DEPTH] = c0
            coef[2, p - DEPTH] = c1
            coef[3, p - DEPTH] = c2

    loads[4].wait()

    def emit(k, src, dst):
        pltpu.make_async_copy(src, dst, out_sem.at[k]).start()

    def precondition(turn, out_ref, own_ref, exact):
        lhs = solve(turn, exact)
        for x in range(SX):
            out = jnp.dot(lhs[:, :256], weights(0, x), preferred_element_type=F32)
            out = out + jnp.dot(lhs[:, 256:], weights(1, x), preferred_element_type=F32)
            if exact:
                out = out[:16] + out[16:]
            corr[turn, 3 + x] = out
            corr_plo[turn, x] = out[0:4]
            corr_phi[turn, x] = out[12:16]
        halo("start", *corr_halo(turn))
        halo("recv", *corr_halo(turn))
        smooth(turn, out_ref, own_ref)
        face_own[turn, 0] = own_ref[0]
        face_own[turn, 1] = own_ref[SX - 1]
        faces("start", turn)
        faces("recv", turn)
        face_place(turn, out_ref)

    group_wait()
    precondition(0, search, s_own, FIRST_EXACT)
    emit(0, s_own, s_hbm)

    @pl.loop(0, SX, unroll=2)
    def _(x):
        inner = operator(x, search)[4:20]
        img[DEPTH + x] = inner
        img_plo[x] = inner[0:2]
        img_phi[x] = inner[14:16]

    row = restrict(lambda x: img[DEPTH + x], True)
    all_send(1, row)
    halo("start", *img_halo)
    emit(1, img.at[own], i_hbm)
    halo("recv", *img_halo)
    keep_q = keep_y

    @pl.loop(0, SX + 4)
    def _(p):
        keep = keep_q & ((p >= DEPTH) | has_w) & ((p < SX + DEPTH) | has_e)
        q24[p] = jnp.where(keep, padded(img_lo[p], img[p], img_hi[p]), 0.0)

    all_wait(1)
    precondition(1, wfield, w_own, True)

    zero = jnp.zeros((8, NZ), F32)

    def fold(value):
        return value[0:8] + value[8:16]

    def products(x, sums):
        v = operator(x, wfield)[4:20]
        v_own[x] = v
        i = img[DEPTH + x]
        r = base[3, DEPTH + x]
        pairs = [(r, r), (r, i), (i, i), (v, r), (v, i), (v, v)]
        return tuple(s + fold(a * b) for s, (a, b) in zip(sums, pairs))

    sums = lax.fori_loop(0, SX, products, (zero,) * 6, unroll=2)
    lanes = iota((1, 128), 1)
    row = jnp.zeros((1, 128), F32)
    for k, s in enumerate(sums):
        s = jnp.sum(s, axis=0, keepdims=True)
        s = jnp.sum(s, axis=1, keepdims=True)
        row = jnp.where(lanes == k, s, row)
    all_send(2, row)
    emit(2, w_own, w_hbm)
    emit(3, v_own, v_hbm)
    all_wait(2)
    parts = [jnp.zeros((1, 128), F32) for _ in range(8)]
    for j in range(ngx * ngy):
        parts[j % 8] = parts[j % 8] + row_all[1, j]
    while len(parts) > 1:
        parts = [parts[k] + parts[k + 1] for k in range(0, len(parts), 2)]
    total = parts[0]
    rr, ri, ii, vr, vi, vv = [
        jnp.sum(jnp.where(lanes == k, total, 0.0), axis=1, keepdims=True) for k in range(6)
    ]
    alpha = rr / ri
    cross = (ri - alpha * ii) - alpha * (vr - alpha * vi)
    square = ii - alpha * (2.0 * vi - alpha * vv)
    omega = cross / square
    alpha_ref[...] = alpha
    omega_ref[...] = omega

    for k, (src, dst) in enumerate(
        [(s_own, s_hbm), (img.at[own], i_hbm), (w_own, w_hbm), (v_own, v_hbm)]
    ):
        pltpu.make_async_copy(src, dst, out_sem.at[k]).wait()
    first_finish()
    all_wait(1, "send")
    all_wait(2, "send")
    halo("send", *base_halo)
    for turn in range(2):
        halo("send", *corr_halo(turn))
        faces("send", turn)
    halo("send", *img_halo)


FIRST_EXACT = False


def solution(mesh):
    ngx, ngy = mesh.shape["gx"], mesh.shape["gy"]
    group = ngx * (ngy // ZG)
    vm = pltpu.VMEM

    def local(right_side, velocity, deflation, inverse_rows):
        out = jax.ShapeDtypeStruct((SX, SY, NZ), F32)
        plane = (ROWS, NZ)
        scratch = [
            vm((KD, SX, SY, NZ), BF16),
            vm(inverse_rows.shape, F32),
            vm((4, SX + 4, SY, NZ), F32),
            vm((4, SX + 4, 2, NZ), F32),
            vm((4, SX + 4, 2, NZ), F32),
            vm((4, SX, 2, NZ), F32),
            vm((4, SX, 2, NZ), F32),
            vm((4, SX) + plane, F32),
            vm((4, SX + 4) + plane, F32),
            vm((KD * 16, 128), BF16),
            vm((SX + 4,) + plane, F32),
            vm((2, SX + 6, SY, NZ), F32),
            vm((2, SX + 6, 4, NZ), F32),
            vm((2, SX + 6, 4, NZ), F32),
            vm((2, SX, 4, NZ), F32),
            vm((2, SX, 4, NZ), F32),
            vm((SX + 6,) + plane, F32),
            vm((SX + 4,) + plane, F32),
            vm((SX + 6,) + plane, F32),
            vm((SX + 4,) + plane, F32),
            vm((SX + 4,) + plane, F32),
            vm((2, 2, SY, NZ), F32),
            vm((2, SX, 1, NZ), F32),
            vm((2, SX, 1, NZ), F32),
            vm((2, 2, SY, NZ), F32),
            vm((2, SX, 1, NZ), F32),
            vm((2, SX, 1, NZ), F32),
            vm((SX + 4, SY, NZ), F32),
            vm((SX + 4, 2, NZ), F32),
            vm((SX + 4, 2, NZ), F32),
            vm((SX, 2, NZ), F32),
            vm((SX, 2, NZ), F32),
            vm((SX + 2,) + plane, F32),
            vm((SX + 2,) + plane, F32),
            vm((SX, SY, NZ), F32),
            vm((SX, SY, NZ), F32),
            vm((SX, SY, NZ), F32),
            vm((ZG, 1, 128), F32),
            vm((group, ZG // QUAD, 128), F32),
            vm((2, ngx * ngy, 1, 128), F32),
            pltpu.SemaphoreType.DMA((5,)),
            pltpu.SemaphoreType.DMA((4,)),
            pltpu.SemaphoreType.DMA((2,)),
            pltpu.SemaphoreType.DMA((2,)),
            pltpu.SemaphoreType.DMA((2,)),
            pltpu.SemaphoreType.DMA((2,)),
            pltpu.SemaphoreType.DMA((6, 8)),
            pltpu.SemaphoreType.DMA((6, 8)),
        ]

        def body(*refs):
            kernel(ngx, ngy, *refs)

        s, i, w, v, alpha, omega = pl.pallas_call(
            body,
            name="bicgstab",
            out_shape=(out,) * 4 + (jax.ShapeDtypeStruct((1, 1), F32),) * 2,
            in_specs=[pl.BlockSpec(memory_space=pl.ANY)] * 4,
            out_specs=(pl.BlockSpec(memory_space=pl.ANY),) * 4 + (pl.BlockSpec(memory_space=vm),) * 2,
            scratch_shapes=scratch,
            compiler_params=pltpu.CompilerParams(collective_id=0, has_side_effects=True),
        )(right_side, velocity, deflation, inverse_rows)
        alpha, omega = alpha[0, 0], omega[0, 0]
        field = alpha * s + omega * (s - alpha * w)
        return field, (right_side - alpha * i) - omega * (i - alpha * v)

    return jax.shard_map(
        local,
        mesh=mesh,
        in_specs=(
            P("gx", "gy", None),
            P(None, "gx", "gy", None),
            P(None, "gx", "gy", None),
            P(("gx", "gy"), None),
        ),
        out_specs=(P("gx", "gy", None), P("gx", "gy", None)),
        check_vma=False,
    )
```

```python
import jax
import jax.numpy as jnp
from jax import lax
from jax.experimental import pallas as pl
from jax.experimental.pallas import tpu as pltpu
from jax.sharding import PartitionSpec as P

F32 = jnp.float32
BF16 = jnp.bfloat16
MESH = pl.DeviceIdType.MESH
SX, SY, NZ = 8, 16, 256
KD = 32
DEPTH = 2
CHEB = 4
ZG = 8
QUAD = 128 // KD
ROWS = 24
SIGMA = 1.0 / 0.9
FAR_FIRST = [4, 3, 5, 2, 6, 1, 7, 0]
AROUND = [(1, 1), (-1, 1), (1, -1), (-1, -1), (0, 1), (0, -1), (1, 0), (-1, 0)]


def iota(shape, dim):
    return lax.broadcasted_iota(jnp.int32, shape, dim)


def padded(low, middle, high):
    gap = 4 - low.shape[0]
    parts = [low, middle, high]
    if gap:
        fill = jnp.zeros((gap, NZ), F32)
        parts = [fill] + parts + [fill]
    return jnp.concatenate(parts, axis=0)


def kernel(
    ngx, ngy,
    r_hbm, vel_hbm, defl_hbm, inv_hbm, both,
    defl, inv, base, base_lo, base_hi, base_plo, base_phi,
    coef, scale, pick, q24, corr, corr_lo, corr_hi, corr_plo, corr_phi, ext, left, upd0, upd1, upd2,
    face, face_lo, face_hi, face_own, face_plo, face_phi,
    img, img_lo, img_hi, img_plo, img_phi, search, wfield, s_own, w_own, v_own, row_a, row_b, row_all,
    local_sem, ag_send, ag_recv, all_sends, all_recvs, halo_send, halo_recv,
):
    gx = lax.axis_index("gx")
    gy = lax.axis_index("gy")
    xg = ngy // ZG
    zpos = lax.rem(gy, ZG)
    xpos = lax.div(gy, ZG)
    line = xpos * ZG
    group = ngx * xg
    seat = gx * xg + xpos
    number = gx * ngy + gy
    here = (gx, gy)
    barrier = pltpu.get_barrier_semaphore()

    def line_peer(step):
        return (gx, line + lax.rem(zpos + step, ZG))

    def group_peer(step):
        other = lax.rem(seat + step, group)
        return (lax.div(other, xg), lax.rem(other, xg) * ZG + zpos)

    def greet(device):
        pl.semaphore_signal(barrier, inc=1, device_id=device, device_id_type=MESH)

    own = pl.ds(DEPTH, SX)
    loads = [
        pltpu.make_async_copy(r_hbm, base.at[3, own], local_sem.at[0]),
        pltpu.make_async_copy(defl_hbm.at[pl.ds(0, 16)], defl.at[pl.ds(0, 16)], local_sem.at[1]),
        pltpu.make_async_copy(defl_hbm.at[pl.ds(16, 16)], defl.at[pl.ds(16, 16)], local_sem.at[2]),
        pltpu.make_async_copy(vel_hbm, base.at[pl.ds(0, 3), own], local_sem.at[3]),
        pltpu.make_async_copy(inv_hbm, inv, local_sem.at[4]),
    ]
    for load in loads:
        load.start()

    @pl.loop(1, ZG)
    def _(step):
        greet(line_peer(step))

    @pl.loop(1, group)
    def _(step):
        greet(group_peer(step))

    for dx, dy in AROUND:
        greet((lax.rem(gx + dx + ngx, ngx), lax.rem(gy + dy + ngy, ngy)))

    has_w, has_e = gx > 0, gx < ngx - 1
    has_s, has_n = gy > 0, gy < ngy - 1

    def remote(src, dst, send, recv, device):
        return pltpu.make_async_remote_copy(
            src_ref=src, dst_ref=dst, send_sem=send, recv_sem=recv,
            device_id=device, device_id_type=MESH,
        )

    def line_send(row):
        row_a[zpos] = row

        @pl.loop(1, ZG)
        def _(step):
            remote(row_a.at[zpos], row_a.at[zpos], ag_send.at[0], ag_recv.at[0],
                   line_peer(step)).start()

    def line_wait():
        view = row_a.at[pl.ds(0, ZG - 1)]
        remote(view, view, ag_send.at[0], ag_recv.at[0], here).wait_recv()

    def group_send(rows):
        row_b[seat] = rows

        @pl.loop(1, group)
        def _(step):
            remote(row_b.at[seat], row_b.at[seat], ag_send.at[1], ag_recv.at[1],
                   group_peer(step)).start()

    def group_wait():
        view = row_b.at[pl.ds(0, group - 1)]
        remote(view, view, ag_send.at[1], ag_recv.at[1], here).wait_recv()

    def all_send(turn, row):
        slot = turn - 1
        row_all[slot, number] = row

        for dz in FAR_FIRST:
            side = lax.rem(zpos + dz, ZG)

            @pl.loop(0 if dz else 1, group, unroll=8 if dz else 1)
            def _(step):
                other = lax.rem(seat + step, group)
                device = (lax.div(other, xg), lax.rem(other, xg) * ZG + side)
                remote(row_all.at[slot, number], row_all.at[slot, number], all_sends.at[slot],
                       all_recvs.at[slot], device).start()

    def all_wait(turn, what="recv"):
        slot = turn - 1
        view = row_all.at[slot, pl.ds(0, ngx * ngy - 1)]
        copy = remote(view, view, all_sends.at[slot], all_recvs.at[slot], here)
        if what == "recv":
            copy.wait_recv()
        else:
            copy.wait_send()

    def first_finish():
        view = row_a.at[pl.ds(0, ZG - 1)]
        remote(view, view, ag_send.at[0], ag_recv.at[0], here).wait_send()
        view = row_b.at[pl.ds(0, group - 1)]
        remote(view, view, ag_send.at[1], ag_recv.at[1], here).wait_send()

    def beside(dx, dy):
        tests = {(-1, 0): has_w, (1, 0): has_e, (0, -1): has_s, (0, 1): has_n}
        first = tests.get((dx, 0)) if dx else None
        second = tests.get((0, dy)) if dy else None
        if first is None:
            return second
        return first if second is None else first & second

    def halo(what, turn, width, mid, low, high, plow, phigh, lead=()):
        w = width
        for k, (dx, dy) in enumerate(AROUND):
            size = w if dx else SX
            take = {1: SX - w, -1: 0, 0: 0}[dx]
            put = {1: 0, -1: w + SX, 0: w}[dx]
            source = {1: phigh, -1: plow, 0: mid}[dy]
            target = {1: low, -1: high, 0: mid}[dy]
            src = source.at[lead + (pl.ds(take + (0 if dy else w), size),)]
            dst = target.at[lead + (pl.ds(put, size),)]
            copy = remote(
                src, dst, halo_send.at[turn, k], halo_recv.at[turn, k],
                (gx + dx, gy + dy) if what == "start" else here,
            )
            act(what, copy, dx, dy)

    def act(what, copy, dx, dy):
        sign = -1 if what == "recv" else 1

        @pl.when(beside(sign * dx, sign * dy))
        def _():
            if what == "start":
                copy.start()
            elif what == "recv":
                copy.wait_recv()
            else:
                copy.wait_send()

    def faces(what, slot):
        pairs = [
            ((1, 0), face_own.at[slot, 1], face.at[slot, 0]),
            ((-1, 0), face_own.at[slot, 0], face.at[slot, 1]),
            ((0, 1), face_phi.at[slot], face_lo.at[slot]),
            ((0, -1), face_plo.at[slot], face_hi.at[slot]),
        ]
        for k, ((dx, dy), src, dst) in enumerate(pairs):
            copy = remote(
                src, dst, halo_send.at[4 + slot, k], halo_recv.at[4 + slot, k],
                (gx + dx, gy + dy) if what == "start" else here,
            )
            act(what, copy, dx, dy)

    lane_end = iota((ROWS, NZ), 1) == NZ - 1

    def shifts(before, centre, after, add, c0, c1, c2):
        ahead = jnp.where(lane_end, 0.0, pltpu.roll(centre, NZ - 1, 1))
        nexts = (after + pltpu.roll(centre, ROWS - 1, 0)) + ahead
        if add is not None:
            nexts = nexts + add
        previous = c0 * before + c1 * pltpu.roll(centre, 1, 0)
        return nexts, previous + c2 * pltpu.roll(centre, 1, 1)

    def operator(x, field):
        nexts, previous = shifts(
            field[x], field[x + 1], field[x + 2], None, coef[1, x], coef[2, x], coef[3, x]
        )
        return coef[0, x] * field[x + 1] - (nexts + previous)

    def split(value):
        top = value.astype(BF16)
        rest = (value - top.astype(F32)).astype(BF16)
        return jnp.concatenate([top, rest], axis=0)

    def weights(half, x):
        return defl[pl.ds(half * 16, 16), x].reshape(256, NZ)

    def restrict(plane, exact, ready=(None, None)):
        lhs = [split(plane(x)) if exact else plane(x).astype(BF16) for x in range(SX)]
        packed = []
        for half in range(2):
            if ready[half] is not None:
                ready[half].wait()
            total = None
            for x in range(SX):
                part = lax.dot_general(
                    lhs[x], weights(half, x), (((1,), (1,)), ((), ())), preferred_element_type=F32
                )
                total = part if total is None else total + part
            same = lax.rem(iota(total.shape, 0), 16) == lax.rem(iota(total.shape, 1), 16)
            kept = jnp.where(same, total, 0.0)
            packed.append(jnp.sum(kept.reshape(-1, 8, 256), axis=0))
        packed = jnp.concatenate(packed, axis=1)
        high = packed.astype(BF16).astype(F32)
        rest = packed - high
        middle = rest.astype(BF16).astype(F32)
        low = rest - middle
        stack = jnp.concatenate([high, middle, low, jnp.zeros_like(low)], axis=0).astype(BF16)
        row = jnp.dot(stack, pick[...], preferred_element_type=F32)
        row = jnp.sum(row, axis=0, keepdims=True)
        mine = lax.div(iota((1, 128), 1), KD) == lax.rem(zpos, QUAD)
        return jnp.where(mine, row, 0.0)

    def quads():
        rows = []
        for start in range(0, ZG, QUAD):
            total = row_a[start]
            for k in range(1, QUAD):
                total = total + row_a[start + k]
            rows.append(total)
        return jnp.concatenate(rows, axis=0) if len(rows) > 1 else rows[0]

    def solve(turn, exact):
        per = ZG // QUAD
        sums = [jnp.zeros((KD, 128), F32) for _ in range(4)]
        for j in range(group * per):
            if turn == 0:
                value = row_b[j // per, pl.ds(j % per, 1), :]
            else:
                first, second, third, fourth = [row_all[0, QUAD * j + k] for k in range(QUAD)]
                value = (first + second) + (third + fourth)
            sums[j % 4] = sums[j % 4] + inv[:, pl.ds(j * 128, 128)] * value
        total = (sums[0] + sums[1]) + (sums[2] + sums[3])
        solved = jnp.sum(total, axis=1, keepdims=True)
        spread = jnp.where(
            iota((KD, KD * 16), 0) == lax.div(iota((KD, KD * 16), 1), 16), solved, 0.0
        )
        spread = jnp.sum(spread, axis=0, keepdims=True)
        shape = (16, KD * 16)
        lhs = jnp.where(iota(shape, 0) == lax.rem(iota(shape, 1), 16), spread, 0.0)
        return split(lhs) if exact else lhs.astype(BF16)

    def smooth(turn, out_ref, own_ref):
        rows = iota((ROWS, NZ), 0)
        keep_y = ((rows >= 4) & (rows < 20)) | ((rows < 4) & has_s) | ((rows >= 20) & has_n)
        box = (rows >= 2) & (rows < 22)

        @pl.loop(0, SX + 6, unroll=2)
        def _(p):
            plane = padded(corr_lo[turn, p], corr[turn, p], corr_hi[turn, p])
            keep = keep_y & ((p >= 3) | has_w) & ((p < SX + 3) | has_e)
            ext[p] = jnp.where(keep, plane, 0.0)

        def scaled(p, before, centre, after, add):
            nexts, previous = shifts(before, centre, after, add, scale[1, p], scale[2, p], scale[3, p])
            return scale[0, p] * nexts + previous

        @pl.loop(0, SX + 4, unroll=4)
        def _(p):
            centre = ext[p + 1]
            total = scaled(p, ext[p], centre, ext[p + 2], q24[p])
            upd0[p + 1] = total - jnp.where(box, centre, 0.0)

        rho = 1.0 / SIGMA
        factors = []
        for sweep in range(CHEB - 1):
            rho_next = 1.0 / (2.0 * SIGMA - rho)
            factors.append((rho_next * rho, 2.0 * rho_next / 0.9))
            rho = rho_next

        @pl.loop(0, SX + 4, unroll=4)
        def _(p):
            centre = upd0[p + 1]
            rest = scaled(p, upd0[p], centre, upd0[p + 2], None)
            left[p] = rest
            upd1[p] = factors[0][0] * centre + factors[0][1] * rest

        @pl.loop(1, SX + 3, unroll=5)
        def _(p):
            centre = upd1[p]
            rest = (left[p] - centre) + scaled(p, upd1[p - 1], centre, upd1[p + 1], None)
            left[p] = rest
            upd2[p] = factors[1][0] * centre + factors[1][1] * rest

        @pl.loop(2, SX + 2, unroll=4)
        def _(p):
            centre = upd2[p]
            rest = (left[p] - centre) + scaled(p, upd2[p - 1], centre, upd2[p + 1], None)
            upd3 = factors[2][0] * centre + factors[2][1] * rest
            value = ((upd0[p + 1] + upd1[p]) + (centre + upd3)) + ext[p + 1]
            out_ref[p - 1] = value
            inner = value[4:20]
            own_ref[p - 2] = inner
            face_plo[turn, p - 2] = inner[0:1]
            face_phi[turn, p - 2] = inner[15:16]

    def face_place(slot, dst):
        zero4 = jnp.zeros((4, NZ), F32)
        dst[0] = jnp.where(has_w, jnp.concatenate([zero4, face[slot, 0], zero4], axis=0), 0.0)
        dst[SX + 1] = jnp.where(has_e, jnp.concatenate([zero4, face[slot, 1], zero4], axis=0), 0.0)
        rows = iota((ROWS, NZ), 0)

        @pl.loop(0, SX, unroll=2)
        def _(x):
            low = jnp.broadcast_to(jnp.where(has_s, face_lo[slot, x], 0.0), (ROWS, NZ))
            high = jnp.broadcast_to(jnp.where(has_n, face_hi[slot, x], 0.0), (ROWS, NZ))
            value = dst[x + 1]
            dst[x + 1] = jnp.where(rows == 3, low, jnp.where(rows == 20, high, value))

    def q_assemble(low, mid, high):
        @pl.loop(0, SX + 4)
        def _(p):
            q24[p] = padded(low(p), mid(p), high(p))

    upd0[0] = jnp.zeros((ROWS, NZ), F32)
    upd0[SX + 5] = jnp.zeros((ROWS, NZ), F32)
    table = lax.div(iota((KD * 16, 128), 0), 16) == lax.rem(iota((KD * 16, 128), 1), KD)
    pick[...] = jnp.where(table, 1.0, 0.0).astype(BF16)
    loads[0].wait()
    row = restrict(lambda x: base[3, DEPTH + x], FIRST_EXACT, (loads[1], loads[2]))
    greetings = (ZG - 1) + (group - 1) + len(AROUND)
    pl.semaphore_wait(barrier, greetings)
    line_send(row)
    loads[3].wait()

    @pl.loop(0, SX)
    def _(x):
        for c in range(4):
            plane = base[c, DEPTH + x]
            base_plo[c, x] = plane[0:2]
            base_phi[c, x] = plane[14:16]

    every = (slice(None),)
    base_halo = (0, DEPTH, base, base_lo, base_hi, base_plo, base_phi, every)
    img_halo = (3, DEPTH, img, img_lo, img_hi, img_plo, img_phi)

    def corr_halo(turn):
        return (1 + turn, 3, corr.at[turn], corr_lo.at[turn], corr_hi.at[turn],
                corr_plo.at[turn], corr_phi.at[turn])

    halo("start", *base_halo)
    line_wait()
    group_send(quads())
    halo("recv", *base_halo)

    rows = iota((ROWS, NZ), 0)
    cols = iota((ROWS, NZ), 1)
    keep_y = ((rows >= 4) & (rows < 20)) | ((rows >= 2) & (rows < 4) & has_s)
    keep_y = keep_y | ((rows >= 20) & (rows < 22) & has_n)

    @pl.loop(0, SX + 4)
    def _(p):
        keep = keep_y & ((p >= DEPTH) | has_w) & ((p < SX + DEPTH) | has_e)
        w0, w1, w2, r = [
            jnp.where(keep, padded(base_lo[c, p], base[c, p], base_hi[c, p]), 0.0)
            for c in range(4)
        ]
        diagonal = 6.0 + w0 + w1 + w2
        jdiag = jnp.where(keep, 1.0 / diagonal, 0.0)
        c0, c1 = 1.0 + w0, 1.0 + w1
        c2 = jnp.where(cols == 0, 0.0, 1.0 + w2)
        scale[0, p] = jdiag
        scale[1, p] = jdiag * c0
        scale[2, p] = jdiag * c1
        scale[3, p] = jdiag * c2
        q24[p] = r

        @pl.when((p >= DEPTH) & (p < SX + DEPTH))
        def _():
            coef[0, p - DEPTH] = diagonal
            coef[1, p - DEPTH] = c0
            coef[2, p - DEPTH] = c1
            coef[3, p - DEPTH] = c2

    loads[4].wait()

    def precondition(turn, out_ref, own_ref, exact):
        lhs = solve(turn, exact)
        for x in range(SX):
            out = jnp.dot(lhs[:, :256], weights(0, x), preferred_element_type=F32)
            out = out + jnp.dot(lhs[:, 256:], weights(1, x), preferred_element_type=F32)
            if exact:
                out = out[:16] + out[16:]
            corr[turn, 3 + x] = out
            corr_plo[turn, x] = out[0:4]
            corr_phi[turn, x] = out[12:16]
        halo("start", *corr_halo(turn))
        halo("recv", *corr_halo(turn))
        smooth(turn, out_ref, own_ref)
        face_own[turn, 0] = own_ref[0]
        face_own[turn, 1] = own_ref[SX - 1]
        faces("start", turn)
        faces("recv", turn)
        face_place(turn, out_ref)

    group_wait()
    precondition(0, search, s_own, FIRST_EXACT)

    @pl.loop(0, SX, unroll=2)
    def _(x):
        inner = operator(x, search)[4:20]
        img[DEPTH + x] = inner
        img_plo[x] = inner[0:2]
        img_phi[x] = inner[14:16]

    row = restrict(lambda x: img[DEPTH + x], True)
    all_send(1, row)
    halo("start", *img_halo)
    halo("recv", *img_halo)
    keep_q = keep_y

    @pl.loop(0, SX + 4)
    def _(p):
        keep = keep_q & ((p >= DEPTH) | has_w) & ((p < SX + DEPTH) | has_e)
        q24[p] = jnp.where(keep, padded(img_lo[p], img[p], img_hi[p]), 0.0)

    all_wait(1)
    precondition(1, wfield, w_own, True)

    zero = jnp.zeros((8, NZ), F32)

    def fold(value):
        return value[0:8] + value[8:16]

    def products(x, sums):
        v = operator(x, wfield)[4:20]
        v_own[x] = v
        i = img[DEPTH + x]
        r = base[3, DEPTH + x]
        pairs = [(r, r), (r, i), (i, i), (v, r), (v, i), (v, v)]
        return tuple(s + fold(a * b) for s, (a, b) in zip(sums, pairs))

    sums = lax.fori_loop(0, SX, products, (zero,) * 6, unroll=2)
    lanes = iota((1, 128), 1)
    row = jnp.zeros((1, 128), F32)
    for k, s in enumerate(sums):
        s = jnp.sum(s, axis=0, keepdims=True)
        s = jnp.sum(s, axis=1, keepdims=True)
        row = jnp.where(lanes == k, s, row)
    all_send(2, row)
    all_wait(2)
    parts = [jnp.zeros((1, 128), F32) for _ in range(8)]
    for j in range(ngx * ngy):
        parts[j % 8] = parts[j % 8] + row_all[1, j]
    while len(parts) > 1:
        parts = [parts[k] + parts[k + 1] for k in range(0, len(parts), 2)]
    total = parts[0]
    rr, ri, ii, vr, vi, vv = [
        jnp.sum(jnp.where(lanes == k, total, 0.0), axis=1, keepdims=True) for k in range(6)
    ]
    alpha = rr / ri
    cross = (ri - alpha * ii) - alpha * (vr - alpha * vi)
    square = ii - alpha * (2.0 * vi - alpha * vv)
    omega = cross / square
    for x in range(SX):
        sv, iv = s_own[x], img[DEPTH + x]
        both[0, x] = alpha * sv + omega * (sv - alpha * w_own[x])
        both[1, x] = (base[3, DEPTH + x] - alpha * iv) - omega * (iv - alpha * v_own[x])

    first_finish()
    all_wait(1, "send")
    all_wait(2, "send")
    halo("send", *base_halo)
    for turn in range(2):
        halo("send", *corr_halo(turn))
        faces("send", turn)
    halo("send", *img_halo)


FIRST_EXACT = False


def solution(mesh):
    ngx, ngy = mesh.shape["gx"], mesh.shape["gy"]
    group = ngx * (ngy // ZG)
    vm = pltpu.VMEM

    def local(right_side, velocity, deflation, inverse_rows):
        out = jax.ShapeDtypeStruct((SX, SY, NZ), F32)
        plane = (ROWS, NZ)
        scratch = [
            vm((KD, SX, SY, NZ), BF16),
            vm(inverse_rows.shape, F32),
            vm((4, SX + 4, SY, NZ), F32),
            vm((4, SX + 4, 2, NZ), F32),
            vm((4, SX + 4, 2, NZ), F32),
            vm((4, SX, 2, NZ), F32),
            vm((4, SX, 2, NZ), F32),
            vm((4, SX) + plane, F32),
            vm((4, SX + 4) + plane, F32),
            vm((KD * 16, 128), BF16),
            vm((SX + 4,) + plane, F32),
            vm((2, SX + 6, SY, NZ), F32),
            vm((2, SX + 6, 4, NZ), F32),
            vm((2, SX + 6, 4, NZ), F32),
            vm((2, SX, 4, NZ), F32),
            vm((2, SX, 4, NZ), F32),
            vm((SX + 6,) + plane, F32),
            vm((SX + 4,) + plane, F32),
            vm((SX + 6,) + plane, F32),
            vm((SX + 4,) + plane, F32),
            vm((SX + 4,) + plane, F32),
            vm((2, 2, SY, NZ), F32),
            vm((2, SX, 1, NZ), F32),
            vm((2, SX, 1, NZ), F32),
            vm((2, 2, SY, NZ), F32),
            vm((2, SX, 1, NZ), F32),
            vm((2, SX, 1, NZ), F32),
            vm((SX + 4, SY, NZ), F32),
            vm((SX + 4, 2, NZ), F32),
            vm((SX + 4, 2, NZ), F32),
            vm((SX, 2, NZ), F32),
            vm((SX, 2, NZ), F32),
            vm((SX + 2,) + plane, F32),
            vm((SX + 2,) + plane, F32),
            vm((SX, SY, NZ), F32),
            vm((SX, SY, NZ), F32),
            vm((SX, SY, NZ), F32),
            vm((ZG, 1, 128), F32),
            vm((group, ZG // QUAD, 128), F32),
            vm((2, ngx * ngy, 1, 128), F32),
            pltpu.SemaphoreType.DMA((5,)),
            pltpu.SemaphoreType.DMA((2,)),
            pltpu.SemaphoreType.DMA((2,)),
            pltpu.SemaphoreType.DMA((2,)),
            pltpu.SemaphoreType.DMA((2,)),
            pltpu.SemaphoreType.DMA((6, 8)),
            pltpu.SemaphoreType.DMA((6, 8)),
        ]

        def body(*refs):
            kernel(ngx, ngy, *refs)

        both = pl.pallas_call(
            body,
            name="bicgstab",
            out_shape=jax.ShapeDtypeStruct((2, SX, SY, NZ), F32),
            in_specs=[pl.BlockSpec(memory_space=pl.ANY)] * 4,
            out_specs=pl.BlockSpec(memory_space=vm),
            scratch_shapes=scratch,
            compiler_params=pltpu.CompilerParams(collective_id=0, has_side_effects=True),
        )(right_side, velocity, deflation, inverse_rows)
        return both[0], both[1]

    return jax.shard_map(
        local,
        mesh=mesh,
        in_specs=(
            P("gx", "gy", None),
            P(None, "gx", "gy", None),
            P(None, "gx", "gy", None),
            P(("gx", "gy"), None),
        ),
        out_specs=(P("gx", "gy", None), P("gx", "gy", None)),
        check_vma=False,
    )
```

```python
import jax
import jax.numpy as jnp
from jax import lax
from jax.experimental import pallas as pl
from jax.experimental.pallas import tpu as pltpu
from jax.sharding import PartitionSpec as P

F32 = jnp.float32
BF16 = jnp.bfloat16
MESH = pl.DeviceIdType.MESH
SX, SY, NZ = 8, 16, 256
KD = 32
DEPTH = 2
CHEB = 4
ZG = 8
QUAD = 128 // KD
ROWS = 24
SIGMA = 1.0 / 0.9
FAR_FIRST = [4, 3, 5, 2, 6, 1, 7, 0]
AROUND = [(1, 1), (-1, 1), (1, -1), (-1, -1), (0, 1), (0, -1), (1, 0), (-1, 0)]


def iota(shape, dim):
    return lax.broadcasted_iota(jnp.int32, shape, dim)


def padded(low, middle, high):
    gap = 4 - low.shape[0]
    parts = [low, middle, high]
    if gap:
        fill = jnp.zeros((gap, NZ), F32)
        parts = [fill] + parts + [fill]
    return jnp.concatenate(parts, axis=0)


def kernel(
    ngx, ngy,
    r_hbm, vel_hbm, defl_hbm, inv_hbm, both,
    natural, defl, defl_eo, lanes_ref, final, inv, base, base_lo, base_hi, base_plo, base_phi,
    coef, scale, pick, q24, corr, corr_lo, corr_hi, corr_plo, corr_phi, ext, left, upd0, upd1, upd2,
    face, face_lo, face_hi, face_own, face_plo, face_phi,
    img, img_lo, img_hi, img_plo, img_phi, search, wfield, s_own, w_own, v_own, row_a, row_b, row_all,
    local_sem, ag_send, ag_recv, all_sends, all_recvs, halo_send, halo_recv,
):
    gx = lax.axis_index("gx")
    gy = lax.axis_index("gy")
    xg = ngy // ZG
    zpos = lax.rem(gy, ZG)
    xpos = lax.div(gy, ZG)
    line = xpos * ZG
    group = ngx * xg
    seat = gx * xg + xpos
    number = gx * ngy + gy
    here = (gx, gy)
    barrier = pltpu.get_barrier_semaphore()

    def line_peer(step):
        return (gx, line + lax.rem(zpos + step, ZG))

    def group_peer(step):
        other = lax.rem(seat + step, group)
        return (lax.div(other, xg), lax.rem(other, xg) * ZG + zpos)

    def greet(device):
        pl.semaphore_signal(barrier, inc=1, device_id=device, device_id_type=MESH)

    own = pl.ds(DEPTH, SX)
    loads = [
        pltpu.make_async_copy(r_hbm, natural.at[3], local_sem.at[0]),
        pltpu.make_async_copy(defl_hbm.at[pl.ds(0, 16)], defl.at[pl.ds(0, 16)], local_sem.at[1]),
        pltpu.make_async_copy(defl_hbm.at[pl.ds(16, 16)], defl.at[pl.ds(16, 16)], local_sem.at[2]),
        pltpu.make_async_copy(vel_hbm, natural.at[pl.ds(0, 3)], local_sem.at[3]),
        pltpu.make_async_copy(inv_hbm, inv, local_sem.at[4]),
    ]
    for load in loads:
        load.start()

    @pl.loop(1, ZG)
    def _(step):
        greet(line_peer(step))

    @pl.loop(1, group)
    def _(step):
        greet(group_peer(step))

    for dx, dy in AROUND:
        greet((lax.rem(gx + dx + ngx, ngx), lax.rem(gy + dy + ngy, ngy)))

    has_w, has_e = gx > 0, gx < ngx - 1
    has_s, has_n = gy > 0, gy < ngy - 1

    def remote(src, dst, send, recv, device):
        return pltpu.make_async_remote_copy(
            src_ref=src, dst_ref=dst, send_sem=send, recv_sem=recv,
            device_id=device, device_id_type=MESH,
        )

    def line_send(row):
        row_a[zpos] = row

        @pl.loop(1, ZG)
        def _(step):
            remote(row_a.at[zpos], row_a.at[zpos], ag_send.at[0], ag_recv.at[0],
                   line_peer(step)).start()

    def line_wait():
        view = row_a.at[pl.ds(0, ZG - 1)]
        remote(view, view, ag_send.at[0], ag_recv.at[0], here).wait_recv()

    def group_send(rows):
        row_b[seat] = rows

        @pl.loop(1, group)
        def _(step):
            remote(row_b.at[seat], row_b.at[seat], ag_send.at[1], ag_recv.at[1],
                   group_peer(step)).start()

    def group_wait():
        view = row_b.at[pl.ds(0, group - 1)]
        remote(view, view, ag_send.at[1], ag_recv.at[1], here).wait_recv()

    def all_send(turn, row):
        slot = turn - 1
        row_all[slot, number] = row

        for dz in FAR_FIRST:
            side = lax.rem(zpos + dz, ZG)

            @pl.loop(0 if dz else 1, group, unroll=8 if dz else 1)
            def _(step):
                other = lax.rem(seat + step, group)
                device = (lax.div(other, xg), lax.rem(other, xg) * ZG + side)
                remote(row_all.at[slot, number], row_all.at[slot, number], all_sends.at[slot],
                       all_recvs.at[slot], device).start()

    def all_wait(turn, what="recv"):
        slot = turn - 1
        view = row_all.at[slot, pl.ds(0, ngx * ngy - 1)]
        copy = remote(view, view, all_sends.at[slot], all_recvs.at[slot], here)
        if what == "recv":
            copy.wait_recv()
        else:
            copy.wait_send()

    def first_finish():
        view = row_a.at[pl.ds(0, ZG - 1)]
        remote(view, view, ag_send.at[0], ag_recv.at[0], here).wait_send()
        view = row_b.at[pl.ds(0, group - 1)]
        remote(view, view, ag_send.at[1], ag_recv.at[1], here).wait_send()

    def beside(dx, dy):
        tests = {(-1, 0): has_w, (1, 0): has_e, (0, -1): has_s, (0, 1): has_n}
        first = tests.get((dx, 0)) if dx else None
        second = tests.get((0, dy)) if dy else None
        if first is None:
            return second
        return first if second is None else first & second

    def halo(what, turn, width, mid, low, high, plow, phigh, lead=()):
        w = width
        for k, (dx, dy) in enumerate(AROUND):
            size = w if dx else SX
            take = {1: SX - w, -1: 0, 0: 0}[dx]
            put = {1: 0, -1: w + SX, 0: w}[dx]
            source = {1: phigh, -1: plow, 0: mid}[dy]
            target = {1: low, -1: high, 0: mid}[dy]
            src = source.at[lead + (pl.ds(take + (0 if dy else w), size),)]
            dst = target.at[lead + (pl.ds(put, size),)]
            copy = remote(
                src, dst, halo_send.at[turn, k], halo_recv.at[turn, k],
                (gx + dx, gy + dy) if what == "start" else here,
            )
            act(what, copy, dx, dy)

    def act(what, copy, dx, dy):
        sign = -1 if what == "recv" else 1

        @pl.when(beside(sign * dx, sign * dy))
        def _():
            if what == "start":
                copy.start()
            elif what == "recv":
                copy.wait_recv()
            else:
                copy.wait_send()

    def faces(what, slot):
        pairs = [
            ((1, 0), face_own.at[slot, 1], face.at[slot, 0]),
            ((-1, 0), face_own.at[slot, 0], face.at[slot, 1]),
            ((0, 1), face_phi.at[slot], face_lo.at[slot]),
            ((0, -1), face_plo.at[slot], face_hi.at[slot]),
        ]
        for k, ((dx, dy), src, dst) in enumerate(pairs):
            copy = remote(
                src, dst, halo_send.at[4 + slot, k], halo_recv.at[4 + slot, k],
                (gx + dx, gy + dy) if what == "start" else here,
            )
            act(what, copy, dx, dy)

    lane_end = iota((ROWS, 128), 1) == 127

    def shifts(before, centre, after, add, c0, c1, c2):
        even, odd = centre[:, :128], centre[:, 128:]
        beyond = jnp.where(lane_end, 0.0, pltpu.roll(even, 127, 1))
        ahead = jnp.concatenate([odd, beyond], axis=1)
        behind = jnp.concatenate([pltpu.roll(odd, 1, 1), even], axis=1)
        nexts = (after + pltpu.roll(centre, ROWS - 1, 0)) + ahead
        if add is not None:
            nexts = nexts + add
        previous = c0 * before + c1 * pltpu.roll(centre, 1, 0)
        return nexts, previous + c2 * behind

    def order(value, back):
        high = value.astype(BF16)
        rest = value - high.astype(F32)
        middle = rest.astype(BF16)
        low = (rest - middle.astype(F32)).astype(BF16)
        dims = (((1,), (1 if back else 0,)), ((), ()))
        high, middle, low = [
            lax.dot_general(part, lanes_ref[...], dims, preferred_element_type=F32)
            for part in (high, middle, low)
        ]
        return high + (middle + low)

    def operator(x, field):
        nexts, previous = shifts(
            field[x], field[x + 1], field[x + 2], None, coef[1, x], coef[2, x], coef[3, x]
        )
        return coef[0, x] * field[x + 1] - (nexts + previous)

    def split(value):
        top = value.astype(BF16)
        rest = (value - top.astype(F32)).astype(BF16)
        return jnp.concatenate([top, rest], axis=0)

    def weights(vectors, half, x):
        return vectors[pl.ds(half * 16, 16), x].reshape(256, NZ)

    def restrict(vectors, plane, exact, ready=(None, None)):
        lhs = [split(plane(x)) if exact else plane(x).astype(BF16) for x in range(SX)]
        packed = []
        for half in range(2):
            if ready[half] is not None:
                ready[half].wait()
            total = None
            for x in range(SX):
                part = lax.dot_general(
                    lhs[x], weights(vectors, half, x), (((1,), (1,)), ((), ())), preferred_element_type=F32
                )
                total = part if total is None else total + part
            same = lax.rem(iota(total.shape, 0), 16) == lax.rem(iota(total.shape, 1), 16)
            kept = jnp.where(same, total, 0.0)
            packed.append(jnp.sum(kept.reshape(-1, 8, 256), axis=0))
        packed = jnp.concatenate(packed, axis=1)
        high = packed.astype(BF16).astype(F32)
        rest = packed - high
        middle = rest.astype(BF16).astype(F32)
        low = rest - middle
        stack = jnp.concatenate([high, middle, low, jnp.zeros_like(low)], axis=0).astype(BF16)
        row = jnp.dot(stack, pick[...], preferred_element_type=F32)
        row = jnp.sum(row, axis=0, keepdims=True)
        mine = lax.div(iota((1, 128), 1), KD) == lax.rem(zpos, QUAD)
        return jnp.where(mine, row, 0.0)

    def quads():
        rows = []
        for start in range(0, ZG, QUAD):
            total = row_a[start]
            for k in range(1, QUAD):
                total = total + row_a[start + k]
            rows.append(total)
        return jnp.concatenate(rows, axis=0) if len(rows) > 1 else rows[0]

    def solve(turn, exact):
        per = ZG // QUAD
        sums = [jnp.zeros((KD, 128), F32) for _ in range(4)]
        for j in range(group * per):
            if turn == 0:
                value = row_b[j // per, pl.ds(j % per, 1), :]
            else:
                first, second, third, fourth = [row_all[0, QUAD * j + k] for k in range(QUAD)]
                value = (first + second) + (third + fourth)
            sums[j % 4] = sums[j % 4] + inv[:, pl.ds(j * 128, 128)] * value
        total = (sums[0] + sums[1]) + (sums[2] + sums[3])
        solved = jnp.sum(total, axis=1, keepdims=True)
        spread = jnp.where(
            iota((KD, KD * 16), 0) == lax.div(iota((KD, KD * 16), 1), 16), solved, 0.0
        )
        spread = jnp.sum(spread, axis=0, keepdims=True)
        shape = (16, KD * 16)
        lhs = jnp.where(iota(shape, 0) == lax.rem(iota(shape, 1), 16), spread, 0.0)
        return split(lhs) if exact else lhs.astype(BF16)

    def smooth(turn, out_ref, own_ref):
        rows = iota((ROWS, NZ), 0)
        keep_y = ((rows >= 4) & (rows < 20)) | ((rows < 4) & has_s) | ((rows >= 20) & has_n)
        box = (rows >= 2) & (rows < 22)

        @pl.loop(0, SX + 6, unroll=2)
        def _(p):
            plane = padded(corr_lo[turn, p], corr[turn, p], corr_hi[turn, p])
            keep = keep_y & ((p >= 3) | has_w) & ((p < SX + 3) | has_e)
            ext[p] = jnp.where(keep, plane, 0.0)

        def scaled(p, before, centre, after, add):
            nexts, previous = shifts(before, centre, after, add, scale[1, p], scale[2, p], scale[3, p])
            return scale[0, p] * nexts + previous

        @pl.loop(0, SX + 4, unroll=4)
        def _(p):
            centre = ext[p + 1]
            total = scaled(p, ext[p], centre, ext[p + 2], q24[p])
            upd0[p + 1] = total - jnp.where(box, centre, 0.0)

        rho = 1.0 / SIGMA
        factors = []
        for sweep in range(CHEB - 1):
            rho_next = 1.0 / (2.0 * SIGMA - rho)
            factors.append((rho_next * rho, 2.0 * rho_next / 0.9))
            rho = rho_next

        @pl.loop(0, SX + 4, unroll=4)
        def _(p):
            centre = upd0[p + 1]
            rest = scaled(p, upd0[p], centre, upd0[p + 2], None)
            left[p] = rest
            upd1[p] = factors[0][0] * centre + factors[0][1] * rest

        @pl.loop(1, SX + 3, unroll=5)
        def _(p):
            centre = upd1[p]
            rest = (left[p] - centre) + scaled(p, upd1[p - 1], centre, upd1[p + 1], None)
            left[p] = rest
            upd2[p] = factors[1][0] * centre + factors[1][1] * rest

        @pl.loop(2, SX + 2, unroll=4)
        def _(p):
            centre = upd2[p]
            rest = (left[p] - centre) + scaled(p, upd2[p - 1], centre, upd2[p + 1], None)
            upd3 = factors[2][0] * centre + factors[2][1] * rest
            value = ((upd0[p + 1] + upd1[p]) + (centre + upd3)) + ext[p + 1]
            out_ref[p - 1] = value
            inner = value[4:20]
            own_ref[p - 2] = inner
            face_plo[turn, p - 2] = inner[0:1]
            face_phi[turn, p - 2] = inner[15:16]

    def face_place(slot, dst):
        zero4 = jnp.zeros((4, NZ), F32)
        dst[0] = jnp.where(has_w, jnp.concatenate([zero4, face[slot, 0], zero4], axis=0), 0.0)
        dst[SX + 1] = jnp.where(has_e, jnp.concatenate([zero4, face[slot, 1], zero4], axis=0), 0.0)
        rows = iota((ROWS, NZ), 0)

        @pl.loop(0, SX, unroll=2)
        def _(x):
            low = jnp.broadcast_to(jnp.where(has_s, face_lo[slot, x], 0.0), (ROWS, NZ))
            high = jnp.broadcast_to(jnp.where(has_n, face_hi[slot, x], 0.0), (ROWS, NZ))
            value = dst[x + 1]
            dst[x + 1] = jnp.where(rows == 3, low, jnp.where(rows == 20, high, value))

    def q_assemble(low, mid, high):
        @pl.loop(0, SX + 4)
        def _(p):
            q24[p] = padded(low(p), mid(p), high(p))

    upd0[0] = jnp.zeros((ROWS, NZ), F32)
    upd0[SX + 5] = jnp.zeros((ROWS, NZ), F32)
    table = lax.div(iota((KD * 16, 128), 0), 16) == lax.rem(iota((KD * 16, 128), 1), KD)
    pick[...] = jnp.where(table, 1.0, 0.0).astype(BF16)
    source, place = iota((NZ, NZ), 0), iota((NZ, NZ), 1)
    table = source == 2 * lax.rem(place, 128) + lax.div(place, 128)
    lanes_ref[...] = jnp.where(table, 1.0, 0.0).astype(BF16)
    loads[0].wait()
    row = restrict(defl, lambda x: natural[3, x], FIRST_EXACT, (loads[1], loads[2]))
    greetings = (ZG - 1) + (group - 1) + len(AROUND)
    pl.semaphore_wait(barrier, greetings)
    line_send(row)
    loads[3].wait()

    @pl.loop(0, SX)
    def _(x):
        planes = order(natural[:, x].reshape(4 * SY, NZ), False).reshape(4, SY, NZ)
        for c in range(4):
            plane = planes[c]
            base[c, DEPTH + x] = plane
            base_plo[c, x] = plane[0:2]
            base_phi[c, x] = plane[14:16]

    every = (slice(None),)
    base_halo = (0, DEPTH, base, base_lo, base_hi, base_plo, base_phi, every)
    img_halo = (3, DEPTH, img, img_lo, img_hi, img_plo, img_phi)

    def corr_halo(turn):
        return (1 + turn, 3, corr.at[turn], corr_lo.at[turn], corr_hi.at[turn],
                corr_plo.at[turn], corr_phi.at[turn])

    halo("start", *base_halo)
    line_wait()
    group_send(quads())
    halo("recv", *base_halo)

    rows = iota((ROWS, NZ), 0)
    cols = iota((ROWS, NZ), 1)
    keep_y = ((rows >= 4) & (rows < 20)) | ((rows >= 2) & (rows < 4) & has_s)
    keep_y = keep_y | ((rows >= 20) & (rows < 22) & has_n)

    @pl.loop(0, SX + 4)
    def _(p):
        keep = keep_y & ((p >= DEPTH) | has_w) & ((p < SX + DEPTH) | has_e)
        w0, w1, w2, r = [
            jnp.where(keep, padded(base_lo[c, p], base[c, p], base_hi[c, p]), 0.0)
            for c in range(4)
        ]
        diagonal = 6.0 + w0 + w1 + w2
        jdiag = jnp.where(keep, 1.0 / diagonal, 0.0)
        c0, c1 = 1.0 + w0, 1.0 + w1
        c2 = jnp.where(cols == 0, 0.0, 1.0 + w2)
        scale[0, p] = jdiag
        scale[1, p] = jdiag * c0
        scale[2, p] = jdiag * c1
        scale[3, p] = jdiag * c2
        q24[p] = r

        @pl.when((p >= DEPTH) & (p < SX + DEPTH))
        def _():
            coef[0, p - DEPTH] = diagonal
            coef[1, p - DEPTH] = c0
            coef[2, p - DEPTH] = c1
            coef[3, p - DEPTH] = c2

    @pl.loop(0, SX)
    def _(x):
        for half in range(2):
            moved = jnp.dot(weights(defl, half, x), lanes_ref[...], preferred_element_type=F32)
            defl_eo[pl.ds(half * 16, 16), x] = moved.astype(BF16).reshape(16, SY, NZ)

    loads[4].wait()

    def precondition(turn, out_ref, own_ref, exact):
        lhs = solve(turn, exact)
        for x in range(SX):
            out = jnp.dot(lhs[:, :256], weights(defl_eo, 0, x), preferred_element_type=F32)
            out = out + jnp.dot(lhs[:, 256:], weights(defl_eo, 1, x), preferred_element_type=F32)
            if exact:
                out = out[:16] + out[16:]
            corr[turn, 3 + x] = out
            corr_plo[turn, x] = out[0:4]
            corr_phi[turn, x] = out[12:16]
        halo("start", *corr_halo(turn))
        halo("recv", *corr_halo(turn))
        smooth(turn, out_ref, own_ref)
        face_own[turn, 0] = own_ref[0]
        face_own[turn, 1] = own_ref[SX - 1]
        faces("start", turn)
        faces("recv", turn)
        face_place(turn, out_ref)

    group_wait()
    precondition(0, search, s_own, FIRST_EXACT)

    @pl.loop(0, SX, unroll=2)
    def _(x):
        inner = operator(x, search)[4:20]
        img[DEPTH + x] = inner
        img_plo[x] = inner[0:2]
        img_phi[x] = inner[14:16]

    row = restrict(defl_eo, lambda x: img[DEPTH + x], True)
    all_send(1, row)
    halo("start", *img_halo)
    halo("recv", *img_halo)
    keep_q = keep_y

    @pl.loop(0, SX + 4)
    def _(p):
        keep = keep_q & ((p >= DEPTH) | has_w) & ((p < SX + DEPTH) | has_e)
        q24[p] = jnp.where(keep, padded(img_lo[p], img[p], img_hi[p]), 0.0)

    all_wait(1)
    precondition(1, wfield, w_own, True)

    zero = jnp.zeros((8, NZ), F32)

    def fold(value):
        return value[0:8] + value[8:16]

    def products(x, sums):
        v = operator(x, wfield)[4:20]
        v_own[x] = v
        i = img[DEPTH + x]
        r = base[3, DEPTH + x]
        pairs = [(r, r), (r, i), (i, i), (v, r), (v, i), (v, v)]
        return tuple(s + fold(a * b) for s, (a, b) in zip(sums, pairs))

    sums = lax.fori_loop(0, SX, products, (zero,) * 6, unroll=2)
    lanes = iota((1, 128), 1)
    row = jnp.zeros((1, 128), F32)
    for k, s in enumerate(sums):
        s = jnp.sum(s, axis=0, keepdims=True)
        s = jnp.sum(s, axis=1, keepdims=True)
        row = jnp.where(lanes == k, s, row)
    all_send(2, row)

    @pl.loop(0, SX)
    def _(x):
        fields = [s_own[x], img[DEPTH + x], w_own[x], v_own[x]]
        final[:, x] = order(jnp.concatenate(fields, axis=0), True).reshape(4, SY, NZ)

    all_wait(2)
    parts = [jnp.zeros((1, 128), F32) for _ in range(8)]
    for j in range(ngx * ngy):
        parts[j % 8] = parts[j % 8] + row_all[1, j]
    while len(parts) > 1:
        parts = [parts[k] + parts[k + 1] for k in range(0, len(parts), 2)]
    total = parts[0]
    rr, ri, ii, vr, vi, vv = [
        jnp.sum(jnp.where(lanes == k, total, 0.0), axis=1, keepdims=True) for k in range(6)
    ]
    alpha = rr / ri
    cross = (ri - alpha * ii) - alpha * (vr - alpha * vi)
    square = ii - alpha * (2.0 * vi - alpha * vv)
    omega = cross / square
    for x in range(SX):
        sv, iv, wv, vv = final[0, x], final[1, x], final[2, x], final[3, x]
        both[0, x] = alpha * sv + omega * (sv - alpha * wv)
        both[1, x] = (natural[3, x] - alpha * iv) - omega * (iv - alpha * vv)

    first_finish()
    all_wait(1, "send")
    all_wait(2, "send")
    halo("send", *base_halo)
    for turn in range(2):
        halo("send", *corr_halo(turn))
        faces("send", turn)
    halo("send", *img_halo)


FIRST_EXACT = False


def solution(mesh):
    ngx, ngy = mesh.shape["gx"], mesh.shape["gy"]
    group = ngx * (ngy // ZG)
    vm = pltpu.VMEM

    def local(right_side, velocity, deflation, inverse_rows):
        out = jax.ShapeDtypeStruct((SX, SY, NZ), F32)
        plane = (ROWS, NZ)
        scratch = [
            vm((4, SX, SY, NZ), F32),
            vm((KD, SX, SY, NZ), BF16),
            vm((KD, SX, SY, NZ), BF16),
            vm((NZ, NZ), BF16),
            vm((4, SX, SY, NZ), F32),
            vm(inverse_rows.shape, F32),
            vm((4, SX + 4, SY, NZ), F32),
            vm((4, SX + 4, 2, NZ), F32),
            vm((4, SX + 4, 2, NZ), F32),
            vm((4, SX, 2, NZ), F32),
            vm((4, SX, 2, NZ), F32),
            vm((4, SX) + plane, F32),
            vm((4, SX + 4) + plane, F32),
            vm((KD * 16, 128), BF16),
            vm((SX + 4,) + plane, F32),
            vm((2, SX + 6, SY, NZ), F32),
            vm((2, SX + 6, 4, NZ), F32),
            vm((2, SX + 6, 4, NZ), F32),
            vm((2, SX, 4, NZ), F32),
            vm((2, SX, 4, NZ), F32),
            vm((SX + 6,) + plane, F32),
            vm((SX + 4,) + plane, F32),
            vm((SX + 6,) + plane, F32),
            vm((SX + 4,) + plane, F32),
            vm((SX + 4,) + plane, F32),
            vm((2, 2, SY, NZ), F32),
            vm((2, SX, 1, NZ), F32),
            vm((2, SX, 1, NZ), F32),
            vm((2, 2, SY, NZ), F32),
            vm((2, SX, 1, NZ), F32),
            vm((2, SX, 1, NZ), F32),
            vm((SX + 4, SY, NZ), F32),
            vm((SX + 4, 2, NZ), F32),
            vm((SX + 4, 2, NZ), F32),
            vm((SX, 2, NZ), F32),
            vm((SX, 2, NZ), F32),
            vm((SX + 2,) + plane, F32),
            vm((SX + 2,) + plane, F32),
            vm((SX, SY, NZ), F32),
            vm((SX, SY, NZ), F32),
            vm((SX, SY, NZ), F32),
            vm((ZG, 1, 128), F32),
            vm((group, ZG // QUAD, 128), F32),
            vm((2, ngx * ngy, 1, 128), F32),
            pltpu.SemaphoreType.DMA((5,)),
            pltpu.SemaphoreType.DMA((2,)),
            pltpu.SemaphoreType.DMA((2,)),
            pltpu.SemaphoreType.DMA((2,)),
            pltpu.SemaphoreType.DMA((2,)),
            pltpu.SemaphoreType.DMA((6, 8)),
            pltpu.SemaphoreType.DMA((6, 8)),
        ]

        def body(*refs):
            kernel(ngx, ngy, *refs)

        both = pl.pallas_call(
            body,
            name="bicgstab",
            out_shape=jax.ShapeDtypeStruct((2, SX, SY, NZ), F32),
            in_specs=[pl.BlockSpec(memory_space=pl.ANY)] * 4,
            out_specs=pl.BlockSpec(memory_space=vm),
            scratch_shapes=scratch,
            compiler_params=pltpu.CompilerParams(collective_id=0, has_side_effects=True),
        )(right_side, velocity, deflation, inverse_rows)
        return both[0], both[1]

    return jax.shard_map(
        local,
        mesh=mesh,
        in_specs=(
            P("gx", "gy", None),
            P(None, "gx", "gy", None),
            P(None, "gx", "gy", None),
            P(("gx", "gy"), None),
        ),
        out_specs=(P("gx", "gy", None), P("gx", "gy", None)),
        check_vma=False,
    )
```

```python
import jax
import jax.numpy as jnp
from jax import lax
from jax.experimental import pallas as pl
from jax.experimental.pallas import tpu as pltpu
from jax.sharding import PartitionSpec as P

F32 = jnp.float32
BF16 = jnp.bfloat16
MESH = pl.DeviceIdType.MESH
SX, SY, NZ = 8, 16, 256
KD = 32
DEPTH = 2
CHEB = 4
ZG = 8
QUAD = 128 // KD
ROWS = 24
SIGMA = 1.0 / 0.9


def hops(step, ring):
    return min(step, ring - step)


def near_last(ring):
    return sorted(range(ring), key=lambda step: -hops(step, ring))
AROUND = [(1, 1), (-1, 1), (1, -1), (-1, -1), (0, 1), (0, -1), (1, 0), (-1, 0)]


def iota(shape, dim):
    return lax.broadcasted_iota(jnp.int32, shape, dim)


def padded(low, middle, high):
    gap = 4 - low.shape[0]
    parts = [low, middle, high]
    if gap:
        fill = jnp.zeros((gap, NZ), F32)
        parts = [fill] + parts + [fill]
    return jnp.concatenate(parts, axis=0)


def kernel(
    ngx, ngy,
    r_hbm, vel_hbm, defl_hbm, inv_hbm, both,
    natural, defl, defl_eo, lanes_ref, final, inv, base, base_lo, base_hi, base_plo, base_phi,
    coef, scale, pick, q24, corr, corr_lo, corr_hi, corr_plo, corr_phi, ext, left, upd0, upd1, upd2,
    face, face_lo, face_hi, face_own, face_plo, face_phi,
    img, img_lo, img_hi, img_plo, img_phi, search, wfield, s_own, w_own, v_own, row_a, row_b, row_all,
    local_sem, ag_send, ag_recv, all_sends, all_recvs, halo_send, halo_recv,
):
    gx = lax.axis_index("gx")
    gy = lax.axis_index("gy")
    xg = ngy // ZG
    zpos = lax.rem(gy, ZG)
    xpos = lax.div(gy, ZG)
    line = xpos * ZG
    group = ngx * xg
    seat = gx * xg + xpos
    number = gx * ngy + gy
    here = (gx, gy)
    barrier = pltpu.get_barrier_semaphore()

    def line_peer(step):
        return (gx, line + lax.rem(zpos + step, ZG))

    def spread(act, dz, dx):
        other = lax.rem(xpos + dx, xg) * ZG + lax.rem(zpos + dz, ZG)

        @pl.loop(0, ngx, unroll=ngx)
        def _(step):
            act((lax.rem(gx + step + ngx // 2, ngx), other))

    def group_each(act):
        for dx in near_last(xg):
            if dx:
                spread(act, 0, dx)
        mine(act)

    def mine(act):
        @pl.loop(1, ngx, unroll=ngx - 1)
        def _(step):
            act((lax.rem(gx + step, ngx), gy))

    def all_each(act):
        pairs = [(dz, dx) for dz in range(ZG) for dx in range(xg) if dz or dx]
        pairs.sort(key=lambda p: -hops(p[0], ZG) - hops(p[1], xg))
        for dz, dx in pairs:
            spread(act, dz, dx)
        mine(act)

    def greet(device):
        pl.semaphore_signal(barrier, inc=1, device_id=device, device_id_type=MESH)

    own = pl.ds(DEPTH, SX)
    loads = [
        pltpu.make_async_copy(r_hbm, natural.at[3], local_sem.at[0]),
        pltpu.make_async_copy(defl_hbm.at[pl.ds(0, 16)], defl.at[pl.ds(0, 16)], local_sem.at[1]),
        pltpu.make_async_copy(defl_hbm.at[pl.ds(16, 16)], defl.at[pl.ds(16, 16)], local_sem.at[2]),
        pltpu.make_async_copy(vel_hbm, natural.at[pl.ds(0, 3)], local_sem.at[3]),
        pltpu.make_async_copy(inv_hbm, inv, local_sem.at[4]),
    ]
    for load in loads:
        load.start()

    for step in near_last(ZG):
        if step:
            greet(line_peer(step))
    group_each(greet)

    for dx, dy in AROUND:
        greet((lax.rem(gx + dx + ngx, ngx), lax.rem(gy + dy + ngy, ngy)))

    has_w, has_e = gx > 0, gx < ngx - 1
    has_s, has_n = gy > 0, gy < ngy - 1

    def remote(src, dst, send, recv, device):
        return pltpu.make_async_remote_copy(
            src_ref=src, dst_ref=dst, send_sem=send, recv_sem=recv,
            device_id=device, device_id_type=MESH,
        )

    def line_send(row):
        row_a[zpos] = row

        for step in near_last(ZG):
            if step:
                remote(row_a.at[zpos], row_a.at[zpos], ag_send.at[0], ag_recv.at[0],
                       line_peer(step)).start()

    def line_wait():
        view = row_a.at[pl.ds(0, ZG - 1)]
        remote(view, view, ag_send.at[0], ag_recv.at[0], here).wait_recv()

    def group_send(rows):
        row_b[seat] = rows

        group_each(lambda device: remote(
            row_b.at[seat], row_b.at[seat], ag_send.at[1], ag_recv.at[1], device).start())

    def group_wait():
        view = row_b.at[pl.ds(0, group - 1)]
        remote(view, view, ag_send.at[1], ag_recv.at[1], here).wait_recv()

    def all_send(turn, row):
        slot = turn - 1
        row_all[slot, number] = row

        all_each(lambda device: remote(
            row_all.at[slot, number], row_all.at[slot, number], all_sends.at[slot],
            all_recvs.at[slot], device).start())

    def all_wait(turn, what="recv"):
        slot = turn - 1
        view = row_all.at[slot, pl.ds(0, ngx * ngy - 1)]
        copy = remote(view, view, all_sends.at[slot], all_recvs.at[slot], here)
        if what == "recv":
            copy.wait_recv()
        else:
            copy.wait_send()

    def first_finish():
        view = row_a.at[pl.ds(0, ZG - 1)]
        remote(view, view, ag_send.at[0], ag_recv.at[0], here).wait_send()
        view = row_b.at[pl.ds(0, group - 1)]
        remote(view, view, ag_send.at[1], ag_recv.at[1], here).wait_send()

    def beside(dx, dy):
        tests = {(-1, 0): has_w, (1, 0): has_e, (0, -1): has_s, (0, 1): has_n}
        first = tests.get((dx, 0)) if dx else None
        second = tests.get((0, dy)) if dy else None
        if first is None:
            return second
        return first if second is None else first & second

    def halo(what, turn, width, mid, low, high, plow, phigh, lead=()):
        w = width
        for k, (dx, dy) in enumerate(AROUND):
            size = w if dx else SX
            take = {1: SX - w, -1: 0, 0: 0}[dx]
            put = {1: 0, -1: w + SX, 0: w}[dx]
            source = {1: phigh, -1: plow, 0: mid}[dy]
            target = {1: low, -1: high, 0: mid}[dy]
            src = source.at[lead + (pl.ds(take + (0 if dy else w), size),)]
            dst = target.at[lead + (pl.ds(put, size),)]
            copy = remote(
                src, dst, halo_send.at[turn, k], halo_recv.at[turn, k],
                (gx + dx, gy + dy) if what == "start" else here,
            )
            act(what, copy, dx, dy)

    def act(what, copy, dx, dy):
        sign = -1 if what == "recv" else 1

        @pl.when(beside(sign * dx, sign * dy))
        def _():
            if what == "start":
                copy.start()
            elif what == "recv":
                copy.wait_recv()
            else:
                copy.wait_send()

    def faces(what, slot):
        pairs = [
            ((1, 0), face_own.at[slot, 1], face.at[slot, 0]),
            ((-1, 0), face_own.at[slot, 0], face.at[slot, 1]),
            ((0, 1), face_phi.at[slot], face_lo.at[slot]),
            ((0, -1), face_plo.at[slot], face_hi.at[slot]),
        ]
        for k, ((dx, dy), src, dst) in enumerate(pairs):
            copy = remote(
                src, dst, halo_send.at[4 + slot, k], halo_recv.at[4 + slot, k],
                (gx + dx, gy + dy) if what == "start" else here,
            )
            act(what, copy, dx, dy)

    lane_end = iota((ROWS, 128), 1) == 127

    def shifts(before, centre, after, add, c0, c1, c2):
        even, odd = centre[:, :128], centre[:, 128:]
        beyond = jnp.where(lane_end, 0.0, pltpu.roll(even, 127, 1))
        ahead = jnp.concatenate([odd, beyond], axis=1)
        behind = jnp.concatenate([pltpu.roll(odd, 1, 1), even], axis=1)
        nexts = (after + pltpu.roll(centre, ROWS - 1, 0)) + ahead
        if add is not None:
            nexts = nexts + add
        previous = c0 * before + c1 * pltpu.roll(centre, 1, 0)
        return nexts, previous + c2 * behind

    def order(value, back):
        high = value.astype(BF16)
        rest = value - high.astype(F32)
        middle = rest.astype(BF16)
        low = (rest - middle.astype(F32)).astype(BF16)
        dims = (((1,), (1 if back else 0,)), ((), ()))
        high, middle, low = [
            lax.dot_general(part, lanes_ref[...], dims, preferred_element_type=F32)
            for part in (high, middle, low)
        ]
        return high + (middle + low)

    def operator(x, field):
        nexts, previous = shifts(
            field[x], field[x + 1], field[x + 2], None, coef[1, x], coef[2, x], coef[3, x]
        )
        return coef[0, x] * field[x + 1] - (nexts + previous)

    def split(value):
        top = value.astype(BF16)
        rest = (value - top.astype(F32)).astype(BF16)
        return jnp.concatenate([top, rest], axis=0)

    def weights(vectors, half, x):
        return vectors[pl.ds(half * 16, 16), x].reshape(256, NZ)

    def restrict(vectors, plane, exact, ready=(None, None)):
        lhs = [split(plane(x)) if exact else plane(x).astype(BF16) for x in range(SX)]
        packed = []
        for half in range(2):
            if ready[half] is not None:
                ready[half].wait()
            total = None
            for x in range(SX):
                part = lax.dot_general(
                    lhs[x], weights(vectors, half, x), (((1,), (1,)), ((), ())), preferred_element_type=F32
                )
                total = part if total is None else total + part
            same = lax.rem(iota(total.shape, 0), 16) == lax.rem(iota(total.shape, 1), 16)
            kept = jnp.where(same, total, 0.0)
            packed.append(jnp.sum(kept.reshape(-1, 8, 256), axis=0))
        packed = jnp.concatenate(packed, axis=1)
        high = packed.astype(BF16).astype(F32)
        rest = packed - high
        middle = rest.astype(BF16).astype(F32)
        low = rest - middle
        stack = jnp.concatenate([high, middle, low, jnp.zeros_like(low)], axis=0).astype(BF16)
        row = jnp.dot(stack, pick[...], preferred_element_type=F32)
        row = jnp.sum(row, axis=0, keepdims=True)
        mine = lax.div(iota((1, 128), 1), KD) == lax.rem(zpos, QUAD)
        return jnp.where(mine, row, 0.0)

    def quads():
        rows = []
        for start in range(0, ZG, QUAD):
            total = row_a[start]
            for k in range(1, QUAD):
                total = total + row_a[start + k]
            rows.append(total)
        return jnp.concatenate(rows, axis=0) if len(rows) > 1 else rows[0]

    def solve(turn, exact):
        per = ZG // QUAD
        sums = [jnp.zeros((KD, 128), F32) for _ in range(4)]
        for j in range(group * per):
            if turn == 0:
                value = row_b[j // per, pl.ds(j % per, 1), :]
            else:
                first, second, third, fourth = [row_all[0, QUAD * j + k] for k in range(QUAD)]
                value = (first + second) + (third + fourth)
            sums[j % 4] = sums[j % 4] + inv[:, pl.ds(j * 128, 128)] * value
        total = (sums[0] + sums[1]) + (sums[2] + sums[3])
        solved = jnp.sum(total, axis=1, keepdims=True)
        spread = jnp.where(
            iota((KD, KD * 16), 0) == lax.div(iota((KD, KD * 16), 1), 16), solved, 0.0
        )
        spread = jnp.sum(spread, axis=0, keepdims=True)
        shape = (16, KD * 16)
        lhs = jnp.where(iota(shape, 0) == lax.rem(iota(shape, 1), 16), spread, 0.0)
        return split(lhs) if exact else lhs.astype(BF16)

    def smooth(turn, out_ref, own_ref):
        rows = iota((ROWS, NZ), 0)
        keep_y = ((rows >= 4) & (rows < 20)) | ((rows < 4) & has_s) | ((rows >= 20) & has_n)
        box = (rows >= 2) & (rows < 22)

        @pl.loop(0, SX + 6, unroll=2)
        def _(p):
            plane = padded(corr_lo[turn, p], corr[turn, p], corr_hi[turn, p])
            keep = keep_y & ((p >= 3) | has_w) & ((p < SX + 3) | has_e)
            ext[p] = jnp.where(keep, plane, 0.0)

        def scaled(p, before, centre, after, add):
            nexts, previous = shifts(before, centre, after, add, scale[1, p], scale[2, p], scale[3, p])
            return scale[0, p] * nexts + previous

        @pl.loop(0, SX + 4, unroll=4)
        def _(p):
            centre = ext[p + 1]
            total = scaled(p, ext[p], centre, ext[p + 2], q24[p])
            upd0[p + 1] = total - jnp.where(box, centre, 0.0)

        rho = 1.0 / SIGMA
        factors = []
        for sweep in range(CHEB - 1):
            rho_next = 1.0 / (2.0 * SIGMA - rho)
            factors.append((rho_next * rho, 2.0 * rho_next / 0.9))
            rho = rho_next

        @pl.loop(0, SX + 4, unroll=4)
        def _(p):
            centre = upd0[p + 1]
            rest = scaled(p, upd0[p], centre, upd0[p + 2], None)
            left[p] = rest
            upd1[p] = factors[0][0] * centre + factors[0][1] * rest

        @pl.loop(1, SX + 3, unroll=5)
        def _(p):
            centre = upd1[p]
            rest = (left[p] - centre) + scaled(p, upd1[p - 1], centre, upd1[p + 1], None)
            left[p] = rest
            upd2[p] = factors[1][0] * centre + factors[1][1] * rest

        @pl.loop(2, SX + 2, unroll=4)
        def _(p):
            centre = upd2[p]
            rest = (left[p] - centre) + scaled(p, upd2[p - 1], centre, upd2[p + 1], None)
            upd3 = factors[2][0] * centre + factors[2][1] * rest
            value = ((upd0[p + 1] + upd1[p]) + (centre + upd3)) + ext[p + 1]
            out_ref[p - 1] = value
            inner = value[4:20]
            own_ref[p - 2] = inner
            face_plo[turn, p - 2] = inner[0:1]
            face_phi[turn, p - 2] = inner[15:16]

    def face_place(slot, dst):
        zero4 = jnp.zeros((4, NZ), F32)
        dst[0] = jnp.where(has_w, jnp.concatenate([zero4, face[slot, 0], zero4], axis=0), 0.0)
        dst[SX + 1] = jnp.where(has_e, jnp.concatenate([zero4, face[slot, 1], zero4], axis=0), 0.0)
        rows = iota((ROWS, NZ), 0)

        @pl.loop(0, SX, unroll=2)
        def _(x):
            low = jnp.broadcast_to(jnp.where(has_s, face_lo[slot, x], 0.0), (ROWS, NZ))
            high = jnp.broadcast_to(jnp.where(has_n, face_hi[slot, x], 0.0), (ROWS, NZ))
            value = dst[x + 1]
            dst[x + 1] = jnp.where(rows == 3, low, jnp.where(rows == 20, high, value))

    def q_assemble(low, mid, high):
        @pl.loop(0, SX + 4)
        def _(p):
            q24[p] = padded(low(p), mid(p), high(p))

    upd0[0] = jnp.zeros((ROWS, NZ), F32)
    upd0[SX + 5] = jnp.zeros((ROWS, NZ), F32)
    table = lax.div(iota((KD * 16, 128), 0), 16) == lax.rem(iota((KD * 16, 128), 1), KD)
    pick[...] = jnp.where(table, 1.0, 0.0).astype(BF16)
    source, place = iota((NZ, NZ), 0), iota((NZ, NZ), 1)
    table = source == 2 * lax.rem(place, 128) + lax.div(place, 128)
    lanes_ref[...] = jnp.where(table, 1.0, 0.0).astype(BF16)
    loads[0].wait()
    row = restrict(defl, lambda x: natural[3, x], FIRST_EXACT, (loads[1], loads[2]))
    greetings = (ZG - 1) + (group - 1) + len(AROUND)
    pl.semaphore_wait(barrier, greetings)
    line_send(row)
    loads[3].wait()

    @pl.loop(0, SX)
    def _(x):
        planes = order(natural[:, x].reshape(4 * SY, NZ), False).reshape(4, SY, NZ)
        for c in range(4):
            plane = planes[c]
            base[c, DEPTH + x] = plane
            base_plo[c, x] = plane[0:2]
            base_phi[c, x] = plane[14:16]

    every = (slice(None),)
    base_halo = (0, DEPTH, base, base_lo, base_hi, base_plo, base_phi, every)
    img_halo = (3, DEPTH, img, img_lo, img_hi, img_plo, img_phi)

    def corr_halo(turn):
        return (1 + turn, 3, corr.at[turn], corr_lo.at[turn], corr_hi.at[turn],
                corr_plo.at[turn], corr_phi.at[turn])

    halo("start", *base_halo)
    line_wait()
    group_send(quads())
    halo("recv", *base_halo)

    rows = iota((ROWS, NZ), 0)
    cols = iota((ROWS, NZ), 1)
    keep_y = ((rows >= 4) & (rows < 20)) | ((rows >= 2) & (rows < 4) & has_s)
    keep_y = keep_y | ((rows >= 20) & (rows < 22) & has_n)

    @pl.loop(0, SX + 4)
    def _(p):
        keep = keep_y & ((p >= DEPTH) | has_w) & ((p < SX + DEPTH) | has_e)
        w0, w1, w2, r = [
            jnp.where(keep, padded(base_lo[c, p], base[c, p], base_hi[c, p]), 0.0)
            for c in range(4)
        ]
        diagonal = 6.0 + w0 + w1 + w2
        jdiag = jnp.where(keep, 1.0 / diagonal, 0.0)
        c0, c1 = 1.0 + w0, 1.0 + w1
        c2 = jnp.where(cols == 0, 0.0, 1.0 + w2)
        scale[0, p] = jdiag
        scale[1, p] = jdiag * c0
        scale[2, p] = jdiag * c1
        scale[3, p] = jdiag * c2
        q24[p] = r

        @pl.when((p >= DEPTH) & (p < SX + DEPTH))
        def _():
            coef[0, p - DEPTH] = diagonal
            coef[1, p - DEPTH] = c0
            coef[2, p - DEPTH] = c1
            coef[3, p - DEPTH] = c2

    @pl.loop(0, SX)
    def _(x):
        for half in range(2):
            moved = jnp.dot(weights(defl, half, x), lanes_ref[...], preferred_element_type=F32)
            defl_eo[pl.ds(half * 16, 16), x] = moved.astype(BF16).reshape(16, SY, NZ)

    loads[4].wait()

    def precondition(turn, out_ref, own_ref, exact):
        lhs = solve(turn, exact)
        for x in range(SX):
            out = jnp.dot(lhs[:, :256], weights(defl_eo, 0, x), preferred_element_type=F32)
            out = out + jnp.dot(lhs[:, 256:], weights(defl_eo, 1, x), preferred_element_type=F32)
            if exact:
                out = out[:16] + out[16:]
            corr[turn, 3 + x] = out
            corr_plo[turn, x] = out[0:4]
            corr_phi[turn, x] = out[12:16]
        halo("start", *corr_halo(turn))
        halo("recv", *corr_halo(turn))
        smooth(turn, out_ref, own_ref)
        face_own[turn, 0] = own_ref[0]
        face_own[turn, 1] = own_ref[SX - 1]
        faces("start", turn)
        faces("recv", turn)
        face_place(turn, out_ref)

    group_wait()
    precondition(0, search, s_own, FIRST_EXACT)

    @pl.loop(0, SX, unroll=2)
    def _(x):
        inner = operator(x, search)[4:20]
        img[DEPTH + x] = inner
        img_plo[x] = inner[0:2]
        img_phi[x] = inner[14:16]

    row = restrict(defl_eo, lambda x: img[DEPTH + x], True)
    all_send(1, row)
    halo("start", *img_halo)
    halo("recv", *img_halo)
    keep_q = keep_y

    @pl.loop(0, SX + 4)
    def _(p):
        keep = keep_q & ((p >= DEPTH) | has_w) & ((p < SX + DEPTH) | has_e)
        q24[p] = jnp.where(keep, padded(img_lo[p], img[p], img_hi[p]), 0.0)

    all_wait(1)
    precondition(1, wfield, w_own, True)

    zero = jnp.zeros((8, NZ), F32)

    def fold(value):
        return value[0:8] + value[8:16]

    def products(x, sums):
        v = operator(x, wfield)[4:20]
        v_own[x] = v
        i = img[DEPTH + x]
        r = base[3, DEPTH + x]
        pairs = [(r, r), (r, i), (i, i), (v, r), (v, i), (v, v)]
        return tuple(s + fold(a * b) for s, (a, b) in zip(sums, pairs))

    sums = lax.fori_loop(0, SX, products, (zero,) * 6, unroll=2)
    lanes = iota((1, 128), 1)
    row = jnp.zeros((1, 128), F32)
    for k, s in enumerate(sums):
        s = jnp.sum(s, axis=0, keepdims=True)
        s = jnp.sum(s, axis=1, keepdims=True)
        row = jnp.where(lanes == k, s, row)
    all_send(2, row)

    @pl.loop(0, SX)
    def _(x):
        fields = [s_own[x], img[DEPTH + x], w_own[x], v_own[x]]
        final[:, x] = order(jnp.concatenate(fields, axis=0), True).reshape(4, SY, NZ)

    all_wait(2)
    parts = [jnp.zeros((1, 128), F32) for _ in range(8)]
    for j in range(ngx * ngy):
        parts[j % 8] = parts[j % 8] + row_all[1, j]
    while len(parts) > 1:
        parts = [parts[k] + parts[k + 1] for k in range(0, len(parts), 2)]
    total = parts[0]
    rr, ri, ii, vr, vi, vv = [
        jnp.sum(jnp.where(lanes == k, total, 0.0), axis=1, keepdims=True) for k in range(6)
    ]
    alpha = rr / ri
    cross = (ri - alpha * ii) - alpha * (vr - alpha * vi)
    square = ii - alpha * (2.0 * vi - alpha * vv)
    omega = cross / square
    for x in range(SX):
        sv, iv, wv, vv = final[0, x], final[1, x], final[2, x], final[3, x]
        both[0, x] = alpha * sv + omega * (sv - alpha * wv)
        both[1, x] = (natural[3, x] - alpha * iv) - omega * (iv - alpha * vv)

    first_finish()
    all_wait(1, "send")
    all_wait(2, "send")
    halo("send", *base_halo)
    for turn in range(2):
        halo("send", *corr_halo(turn))
        faces("send", turn)
    halo("send", *img_halo)


FIRST_EXACT = False


def solution(mesh):
    ngx, ngy = mesh.shape["gx"], mesh.shape["gy"]
    group = ngx * (ngy // ZG)
    vm = pltpu.VMEM

    def local(right_side, velocity, deflation, inverse_rows):
        out = jax.ShapeDtypeStruct((SX, SY, NZ), F32)
        plane = (ROWS, NZ)
        scratch = [
            vm((4, SX, SY, NZ), F32),
            vm((KD, SX, SY, NZ), BF16),
            vm((KD, SX, SY, NZ), BF16),
            vm((NZ, NZ), BF16),
            vm((4, SX, SY, NZ), F32),
            vm(inverse_rows.shape, F32),
            vm((4, SX + 4, SY, NZ), F32),
            vm((4, SX + 4, 2, NZ), F32),
            vm((4, SX + 4, 2, NZ), F32),
            vm((4, SX, 2, NZ), F32),
            vm((4, SX, 2, NZ), F32),
            vm((4, SX) + plane, F32),
            vm((4, SX + 4) + plane, F32),
            vm((KD * 16, 128), BF16),
            vm((SX + 4,) + plane, F32),
            vm((2, SX + 6, SY, NZ), F32),
            vm((2, SX + 6, 4, NZ), F32),
            vm((2, SX + 6, 4, NZ), F32),
            vm((2, SX, 4, NZ), F32),
            vm((2, SX, 4, NZ), F32),
            vm((SX + 6,) + plane, F32),
            vm((SX + 4,) + plane, F32),
            vm((SX + 6,) + plane, F32),
            vm((SX + 4,) + plane, F32),
            vm((SX + 4,) + plane, F32),
            vm((2, 2, SY, NZ), F32),
            vm((2, SX, 1, NZ), F32),
            vm((2, SX, 1, NZ), F32),
            vm((2, 2, SY, NZ), F32),
            vm((2, SX, 1, NZ), F32),
            vm((2, SX, 1, NZ), F32),
            vm((SX + 4, SY, NZ), F32),
            vm((SX + 4, 2, NZ), F32),
            vm((SX + 4, 2, NZ), F32),
            vm((SX, 2, NZ), F32),
            vm((SX, 2, NZ), F32),
            vm((SX + 2,) + plane, F32),
            vm((SX + 2,) + plane, F32),
            vm((SX, SY, NZ), F32),
            vm((SX, SY, NZ), F32),
            vm((SX, SY, NZ), F32),
            vm((ZG, 1, 128), F32),
            vm((group, ZG // QUAD, 128), F32),
            vm((2, ngx * ngy, 1, 128), F32),
            pltpu.SemaphoreType.DMA((5,)),
            pltpu.SemaphoreType.DMA((2,)),
            pltpu.SemaphoreType.DMA((2,)),
            pltpu.SemaphoreType.DMA((2,)),
            pltpu.SemaphoreType.DMA((2,)),
            pltpu.SemaphoreType.DMA((6, 8)),
            pltpu.SemaphoreType.DMA((6, 8)),
        ]

        def body(*refs):
            kernel(ngx, ngy, *refs)

        both = pl.pallas_call(
            body,
            name="bicgstab",
            out_shape=jax.ShapeDtypeStruct((2, SX, SY, NZ), F32),
            in_specs=[pl.BlockSpec(memory_space=pl.ANY)] * 4,
            out_specs=pl.BlockSpec(memory_space=vm),
            scratch_shapes=scratch,
            compiler_params=pltpu.CompilerParams(collective_id=0, has_side_effects=True),
        )(right_side, velocity, deflation, inverse_rows)
        return both[0], both[1]

    return jax.shard_map(
        local,
        mesh=mesh,
        in_specs=(
            P("gx", "gy", None),
            P(None, "gx", "gy", None),
            P(None, "gx", "gy", None),
            P(("gx", "gy"), None),
        ),
        out_specs=(P("gx", "gy", None), P("gx", "gy", None)),
        check_vma=False,
    )
```

```python
import jax
import jax.numpy as jnp
from jax import lax
from jax.experimental import pallas as pl
from jax.experimental.pallas import tpu as pltpu
from jax.sharding import PartitionSpec as P

F32 = jnp.float32
BF16 = jnp.bfloat16
MESH = pl.DeviceIdType.MESH
SX, SY, NZ = 8, 16, 256
KD = 32
DEPTH = 2
CHEB = 4
ZG = 8
QUAD = 128 // KD
ROWS = 24
SIGMA = 1.0 / 0.9


def hops(step, ring):
    return min(step, ring - step)


def near_last(ring):
    return sorted(range(ring), key=lambda step: -hops(step, ring))
AROUND = [(1, 1), (-1, 1), (1, -1), (-1, -1), (0, 1), (0, -1), (1, 0), (-1, 0)]


def iota(shape, dim):
    return lax.broadcasted_iota(jnp.int32, shape, dim)


def padded(low, middle, high):
    gap = 4 - low.shape[0]
    parts = [low, middle, high]
    if gap:
        fill = jnp.zeros((gap, NZ), F32)
        parts = [fill] + parts + [fill]
    return jnp.concatenate(parts, axis=0)


def kernel(
    ngx, ngy,
    r_hbm, vel_hbm, defl_hbm, inv_hbm, both,
    natural, defl, defl_eo, lanes_ref, final, inv, base, base_lo, base_hi, base_plo, base_phi,
    coef, scale, pick, q24, corr, corr_lo, corr_hi, corr_plo, corr_phi, ext, left, upd0, upd1, upd2,
    face_lo, face_hi, face_plo, face_phi,
    img, img_lo, img_hi, img_plo, img_phi, search, wfield, v_own, row_a, row_b, row_all,
    local_sem, ag_send, ag_recv, all_sends, all_recvs, halo_send, halo_recv,
):
    gx = lax.axis_index("gx")
    gy = lax.axis_index("gy")
    xg = ngy // ZG
    zpos = lax.rem(gy, ZG)
    xpos = lax.div(gy, ZG)
    line = xpos * ZG
    group = ngx * xg
    seat = gx * xg + xpos
    number = gx * ngy + gy
    here = (gx, gy)
    barrier = pltpu.get_barrier_semaphore()

    def line_peer(step):
        return (gx, line + lax.rem(zpos + step, ZG))

    def spread(act, dz, dx):
        other = lax.rem(xpos + dx, xg) * ZG + lax.rem(zpos + dz, ZG)

        @pl.loop(0, ngx, unroll=ngx)
        def _(step):
            act((lax.rem(gx + step + ngx // 2, ngx), other))

    def group_each(act):
        for dx in near_last(xg):
            if dx:
                spread(act, 0, dx)
        mine(act)

    def mine(act):
        @pl.loop(1, ngx, unroll=ngx - 1)
        def _(step):
            act((lax.rem(gx + step, ngx), gy))

    def all_each(act, between=None):
        pairs = [(dz, dx) for dz in range(ZG) for dx in range(xg) if dz or dx]
        pairs.sort(key=lambda p: -hops(p[0], ZG) - hops(p[1], xg))
        for place, (dz, dx) in enumerate(pairs):
            if place == len(pairs) // 2 and between is not None:
                between()
            spread(act, dz, dx)
        mine(act)

    def greet(device):
        pl.semaphore_signal(barrier, inc=1, device_id=device, device_id_type=MESH)

    own = pl.ds(DEPTH, SX)
    loads = [
        pltpu.make_async_copy(r_hbm, natural.at[3], local_sem.at[0]),
        pltpu.make_async_copy(defl_hbm.at[pl.ds(0, 16)], defl.at[pl.ds(0, 16)], local_sem.at[1]),
        pltpu.make_async_copy(defl_hbm.at[pl.ds(16, 16)], defl.at[pl.ds(16, 16)], local_sem.at[2]),
        pltpu.make_async_copy(vel_hbm, natural.at[pl.ds(0, 3)], local_sem.at[3]),
        pltpu.make_async_copy(inv_hbm, inv, local_sem.at[4]),
    ]
    for load in loads:
        load.start()

    for step in near_last(ZG):
        if step:
            greet(line_peer(step))
    group_each(greet)

    for dx, dy in AROUND:
        greet((lax.rem(gx + dx + ngx, ngx), lax.rem(gy + dy + ngy, ngy)))

    has_w, has_e = gx > 0, gx < ngx - 1
    has_s, has_n = gy > 0, gy < ngy - 1

    def remote(src, dst, send, recv, device):
        return pltpu.make_async_remote_copy(
            src_ref=src, dst_ref=dst, send_sem=send, recv_sem=recv,
            device_id=device, device_id_type=MESH,
        )

    def line_send(row):
        row_a[zpos] = row

        for step in near_last(ZG):
            if step:
                remote(row_a.at[zpos], row_a.at[zpos], ag_send.at[0], ag_recv.at[0],
                       line_peer(step)).start()

    def line_wait():
        view = row_a.at[pl.ds(0, ZG - 1)]
        remote(view, view, ag_send.at[0], ag_recv.at[0], here).wait_recv()

    def group_send(rows):
        row_b[seat] = rows

        group_each(lambda device: remote(
            row_b.at[seat], row_b.at[seat], ag_send.at[1], ag_recv.at[1], device).start())

    def group_wait():
        view = row_b.at[pl.ds(0, group - 1)]
        remote(view, view, ag_send.at[1], ag_recv.at[1], here).wait_recv()

    def all_send(turn, row, between=None):
        slot = turn - 1
        row_all[slot, number] = row

        all_each(lambda device: remote(
            row_all.at[slot, number], row_all.at[slot, number], all_sends.at[slot],
            all_recvs.at[slot], device).start(), between)

    def all_wait(turn, what="recv"):
        slot = turn - 1
        view = row_all.at[slot, pl.ds(0, ngx * ngy - 1)]
        copy = remote(view, view, all_sends.at[slot], all_recvs.at[slot], here)
        if what == "recv":
            copy.wait_recv()
        else:
            copy.wait_send()

    def first_finish():
        view = row_a.at[pl.ds(0, ZG - 1)]
        remote(view, view, ag_send.at[0], ag_recv.at[0], here).wait_send()
        view = row_b.at[pl.ds(0, group - 1)]
        remote(view, view, ag_send.at[1], ag_recv.at[1], here).wait_send()

    def beside(dx, dy):
        tests = {(-1, 0): has_w, (1, 0): has_e, (0, -1): has_s, (0, 1): has_n}
        first = tests.get((dx, 0)) if dx else None
        second = tests.get((0, dy)) if dy else None
        if first is None:
            return second
        return first if second is None else first & second

    def halo(what, turn, width, mid, low, high, plow, phigh, lead=()):
        w = width
        for k, (dx, dy) in enumerate(AROUND):
            size = w if dx else SX
            take = {1: SX - w, -1: 0, 0: 0}[dx]
            put = {1: 0, -1: w + SX, 0: w}[dx]
            source = {1: phigh, -1: plow, 0: mid}[dy]
            target = {1: low, -1: high, 0: mid}[dy]
            src = source.at[lead + (pl.ds(take + (0 if dy else w), size),)]
            dst = target.at[lead + (pl.ds(put, size),)]
            copy = remote(
                src, dst, halo_send.at[turn, k], halo_recv.at[turn, k],
                (gx + dx, gy + dy) if what == "start" else here,
            )
            act(what, copy, dx, dy)

    def act(what, copy, dx, dy):
        sign = -1 if what == "recv" else 1

        @pl.when(beside(sign * dx, sign * dy))
        def _():
            if what == "start":
                copy.start()
            elif what == "recv":
                copy.wait_recv()
            else:
                copy.wait_send()

    def faces(what, slot, field, kinds=(0, 1, 2, 3)):
        pairs = [
            ((1, 0), field.at[SX], field.at[0]),
            ((-1, 0), field.at[1], field.at[SX + 1]),
            ((0, 1), face_phi.at[slot], face_lo.at[slot]),
            ((0, -1), face_plo.at[slot], face_hi.at[slot]),
        ]
        for k in kinds:
            (dx, dy), src, dst = pairs[k]
            copy = remote(
                src, dst, halo_send.at[4 + slot, k], halo_recv.at[4 + slot, k],
                (gx + dx, gy + dy) if what == "start" else here,
            )
            act(what, copy, dx, dy)

    lane_end = iota((ROWS, 128), 1) == 127

    def shifts(before, centre, after, add, c0, c1, c2):
        even, odd = centre[:, :128], centre[:, 128:]
        beyond = jnp.where(lane_end, 0.0, pltpu.roll(even, 127, 1))
        ahead = jnp.concatenate([odd, beyond], axis=1)
        behind = jnp.concatenate([pltpu.roll(odd, 1, 1), even], axis=1)
        nexts = (after + pltpu.roll(centre, ROWS - 1, 0)) + ahead
        if add is not None:
            nexts = nexts + add
        previous = c0 * before + c1 * pltpu.roll(centre, 1, 0)
        return nexts, previous + c2 * behind

    def order(value, back):
        high = value.astype(BF16)
        rest = value - high.astype(F32)
        middle = rest.astype(BF16)
        low = (rest - middle.astype(F32)).astype(BF16)
        dims = (((1,), (1 if back else 0,)), ((), ()))
        high, middle, low = [
            lax.dot_general(part, lanes_ref[...], dims, preferred_element_type=F32)
            for part in (high, middle, low)
        ]
        return high + (middle + low)

    def operator(x, field):
        nexts, previous = shifts(
            field[x], field[x + 1], field[x + 2], None, coef[1, x], coef[2, x], coef[3, x]
        )
        return coef[0, x] * field[x + 1] - (nexts + previous)

    def split(value):
        top = value.astype(BF16)
        rest = (value - top.astype(F32)).astype(BF16)
        return jnp.concatenate([top, rest], axis=0)

    def weights(vectors, half, x):
        return vectors[pl.ds(half * 16, 16), x].reshape(256, NZ)

    def restrict(vectors, plane, exact, ready=(None, None)):
        lhs = [split(plane(x)) if exact else plane(x).astype(BF16) for x in range(SX)]
        packed = []
        for half in range(2):
            if ready[half] is not None:
                ready[half].wait()
            total = None
            for x in range(SX):
                part = lax.dot_general(
                    lhs[x], weights(vectors, half, x), (((1,), (1,)), ((), ())), preferred_element_type=F32
                )
                total = part if total is None else total + part
            same = lax.rem(iota(total.shape, 0), 16) == lax.rem(iota(total.shape, 1), 16)
            kept = jnp.where(same, total, 0.0)
            packed.append(jnp.sum(kept.reshape(-1, 8, 256), axis=0))
        packed = jnp.concatenate(packed, axis=1)
        high = packed.astype(BF16).astype(F32)
        rest = packed - high
        middle = rest.astype(BF16).astype(F32)
        low = rest - middle
        stack = jnp.concatenate([high, middle, low, jnp.zeros_like(low)], axis=0).astype(BF16)
        row = jnp.dot(stack, pick[...], preferred_element_type=F32)
        row = jnp.sum(row, axis=0, keepdims=True)
        mine = lax.div(iota((1, 128), 1), KD) == lax.rem(zpos, QUAD)
        return jnp.where(mine, row, 0.0)

    def quads():
        rows = []
        for start in range(0, ZG, QUAD):
            total = row_a[start]
            for k in range(1, QUAD):
                total = total + row_a[start + k]
            rows.append(total)
        return jnp.concatenate(rows, axis=0) if len(rows) > 1 else rows[0]

    def solve(turn, exact):
        per = ZG // QUAD
        sums = [jnp.zeros((KD, 128), F32) for _ in range(4)]
        for j in range(group * per):
            if turn == 0:
                value = row_b[j // per, pl.ds(j % per, 1), :]
            else:
                first, second, third, fourth = [row_all[0, QUAD * j + k] for k in range(QUAD)]
                value = (first + second) + (third + fourth)
            sums[j % 4] = sums[j % 4] + inv[:, pl.ds(j * 128, 128)] * value
        total = (sums[0] + sums[1]) + (sums[2] + sums[3])
        solved = jnp.sum(total, axis=1, keepdims=True)
        spread = jnp.where(
            iota((KD, KD * 16), 0) == lax.div(iota((KD, KD * 16), 1), 16), solved, 0.0
        )
        spread = jnp.sum(spread, axis=0, keepdims=True)
        shape = (16, KD * 16)
        lhs = jnp.where(iota(shape, 0) == lax.rem(iota(shape, 1), 16), spread, 0.0)
        return split(lhs) if exact else lhs.astype(BF16)

    def smooth(turn, out_ref):
        rows = iota((ROWS, NZ), 0)
        keep_y = ((rows >= 4) & (rows < 20)) | ((rows < 4) & has_s) | ((rows >= 20) & has_n)
        box = (rows >= 2) & (rows < 22)

        @pl.loop(0, SX + 6, unroll=2)
        def _(p):
            plane = padded(corr_lo[turn, p], corr[turn, p], corr_hi[turn, p])
            keep = keep_y & ((p >= 3) | has_w) & ((p < SX + 3) | has_e)
            ext[p] = jnp.where(keep, plane, 0.0)

        def scaled(p, before, centre, after, add):
            nexts, previous = shifts(before, centre, after, add, scale[1, p], scale[2, p], scale[3, p])
            return scale[0, p] * nexts + previous

        @pl.loop(0, SX + 4, unroll=4)
        def _(p):
            centre = ext[p + 1]
            total = scaled(p, ext[p], centre, ext[p + 2], q24[p])
            upd0[p + 1] = total - jnp.where(box, centre, 0.0)

        rho = 1.0 / SIGMA
        factors = []
        for sweep in range(CHEB - 1):
            rho_next = 1.0 / (2.0 * SIGMA - rho)
            factors.append((rho_next * rho, 2.0 * rho_next / 0.9))
            rho = rho_next

        @pl.loop(0, SX + 4, unroll=4)
        def _(p):
            centre = upd0[p + 1]
            rest = scaled(p, upd0[p], centre, upd0[p + 2], None)
            left[p] = rest
            upd1[p] = factors[0][0] * centre + factors[0][1] * rest

        @pl.loop(1, SX + 3, unroll=5)
        def _(p):
            centre = upd1[p]
            rest = (left[p] - centre) + scaled(p, upd1[p - 1], centre, upd1[p + 1], None)
            left[p] = rest
            upd2[p] = factors[1][0] * centre + factors[1][1] * rest

        @pl.loop(2, SX + 2, unroll=4)
        def _(p):
            centre = upd2[p]
            rest = (left[p] - centre) + scaled(p, upd2[p - 1], centre, upd2[p + 1], None)
            upd3 = factors[2][0] * centre + factors[2][1] * rest
            value = ((upd0[p + 1] + upd1[p]) + (centre + upd3)) + ext[p + 1]
            out_ref[p - 1] = value
            face_plo[turn, p - 2] = value[4:5]
            face_phi[turn, p - 2] = value[19:20]

    def face_place(slot, dst):
        rows = iota((ROWS, NZ), 0)

        @pl.loop(0, SX, unroll=2)
        def _(x):
            low = jnp.broadcast_to(jnp.where(has_s, face_lo[slot, x], 0.0), (ROWS, NZ))
            high = jnp.broadcast_to(jnp.where(has_n, face_hi[slot, x], 0.0), (ROWS, NZ))
            value = dst[x + 1]
            dst[x + 1] = jnp.where(rows == 3, low, jnp.where(rows == 20, high, value))

    def q_assemble(low, mid, high):
        @pl.loop(0, SX + 4)
        def _(p):
            q24[p] = padded(low(p), mid(p), high(p))

    upd0[0] = jnp.zeros((ROWS, NZ), F32)
    upd0[SX + 5] = jnp.zeros((ROWS, NZ), F32)
    for there, plane in ((has_w, 0), (has_e, SX + 1)):

        @pl.when(jnp.logical_not(there))
        def _():
            search[plane] = jnp.zeros((ROWS, NZ), F32)
            wfield[plane] = jnp.zeros((ROWS, NZ), F32)

    table = lax.div(iota((KD * 16, 128), 0), 16) == lax.rem(iota((KD * 16, 128), 1), KD)
    pick[...] = jnp.where(table, 1.0, 0.0).astype(BF16)
    source, place = iota((NZ, NZ), 0), iota((NZ, NZ), 1)
    table = source == 2 * lax.rem(place, 128) + lax.div(place, 128)
    lanes_ref[...] = jnp.where(table, 1.0, 0.0).astype(BF16)
    loads[0].wait()
    row = restrict(defl, lambda x: natural[3, x], FIRST_EXACT, (loads[1], loads[2]))
    greetings = (ZG - 1) + (group - 1) + len(AROUND)
    pl.semaphore_wait(barrier, greetings)
    line_send(row)
    loads[3].wait()

    @pl.loop(0, SX)
    def _(x):
        planes = order(natural[:, x].reshape(4 * SY, NZ), False).reshape(4, SY, NZ)
        for c in range(4):
            plane = planes[c]
            base[c, DEPTH + x] = plane
            base_plo[c, x] = plane[0:2]
            base_phi[c, x] = plane[14:16]

    every = (slice(None),)
    base_halo = (0, DEPTH, base, base_lo, base_hi, base_plo, base_phi, every)
    img_halo = (3, DEPTH, img, img_lo, img_hi, img_plo, img_phi)

    def corr_halo(turn):
        return (1 + turn, 3, corr.at[turn], corr_lo.at[turn], corr_hi.at[turn],
                corr_plo.at[turn], corr_phi.at[turn])

    halo("start", *base_halo)
    line_wait()
    group_send(quads())
    halo("recv", *base_halo)

    rows = iota((ROWS, NZ), 0)
    cols = iota((ROWS, NZ), 1)
    keep_y = ((rows >= 4) & (rows < 20)) | ((rows >= 2) & (rows < 4) & has_s)
    keep_y = keep_y | ((rows >= 20) & (rows < 22) & has_n)

    @pl.loop(0, SX + 4)
    def _(p):
        keep = keep_y & ((p >= DEPTH) | has_w) & ((p < SX + DEPTH) | has_e)
        w0, w1, w2, r = [
            jnp.where(keep, padded(base_lo[c, p], base[c, p], base_hi[c, p]), 0.0)
            for c in range(4)
        ]
        diagonal = 6.0 + w0 + w1 + w2
        jdiag = jnp.where(keep, 1.0 / diagonal, 0.0)
        c0, c1 = 1.0 + w0, 1.0 + w1
        c2 = jnp.where(cols == 0, 0.0, 1.0 + w2)
        scale[0, p] = jdiag
        scale[1, p] = jdiag * c0
        scale[2, p] = jdiag * c1
        scale[3, p] = jdiag * c2
        q24[p] = r

        @pl.when((p >= DEPTH) & (p < SX + DEPTH))
        def _():
            coef[0, p - DEPTH] = diagonal
            coef[1, p - DEPTH] = c0
            coef[2, p - DEPTH] = c1
            coef[3, p - DEPTH] = c2

    @pl.loop(0, SX)
    def _(x):
        for half in range(2):
            moved = jnp.dot(weights(defl, half, x), lanes_ref[...], preferred_element_type=F32)
            defl_eo[pl.ds(half * 16, 16), x] = moved.astype(BF16).reshape(16, SY, NZ)

    loads[4].wait()

    def precondition(turn, out_ref, exact):
        lhs = solve(turn, exact)
        for x in range(SX):
            out = jnp.dot(lhs[:, :256], weights(defl_eo, 0, x), preferred_element_type=F32)
            out = out + jnp.dot(lhs[:, 256:], weights(defl_eo, 1, x), preferred_element_type=F32)
            if exact:
                out = out[:16] + out[16:]
            corr[turn, 3 + x] = out
            corr_plo[turn, x] = out[0:3]
            corr_phi[turn, x] = out[13:16]
        halo("start", *corr_halo(turn))
        halo("recv", *corr_halo(turn))
        smooth(turn, out_ref)
        faces("start", turn, out_ref)
        faces("recv", turn, out_ref)
        faces("send", turn, out_ref, (0, 1))
        face_place(turn, out_ref)

    group_wait()
    precondition(0, search, FIRST_EXACT)

    @pl.loop(0, SX, unroll=2)
    def _(x):
        inner = operator(x, search)[4:20]
        img[DEPTH + x] = inner
        img_plo[x] = inner[0:2]
        img_phi[x] = inner[14:16]

    row = restrict(defl_eo, lambda x: img[DEPTH + x], True)
    all_send(1, row, lambda: halo("start", *img_halo))
    halo("recv", *img_halo)
    keep_q = keep_y

    @pl.loop(0, SX + 4)
    def _(p):
        keep = keep_q & ((p >= DEPTH) | has_w) & ((p < SX + DEPTH) | has_e)
        q24[p] = jnp.where(keep, padded(img_lo[p], img[p], img_hi[p]), 0.0)

    zero = jnp.zeros((8, NZ), F32)

    def fold(value):
        return value[0:8] + value[8:16]

    def early(x, sums):
        i = img[DEPTH + x]
        r = base[3, DEPTH + x]
        pairs = [(r, r), (r, i), (i, i)]
        return tuple(s + fold(a * b) for s, (a, b) in zip(sums, pairs))

    early_sums = lax.fori_loop(0, SX, early, (zero,) * 3, unroll=2)
    lanes = iota((1, 128), 1)

    def pack(row, sums, start):
        for k, s in enumerate(sums):
            s = jnp.sum(s, axis=0, keepdims=True)
            s = jnp.sum(s, axis=1, keepdims=True)
            row = jnp.where(lanes == start + k, s, row)
        return row

    early_row = pack(jnp.zeros((1, 128), F32), early_sums, 0)
    all_wait(1)
    precondition(1, wfield, True)

    def products(x, sums):
        v = operator(x, wfield)[4:20]
        v_own[x] = v
        i = img[DEPTH + x]
        r = base[3, DEPTH + x]
        pairs = [(v, r), (v, i), (v, v)]
        return tuple(s + fold(a * b) for s, (a, b) in zip(sums, pairs))

    row = pack(early_row, lax.fori_loop(0, SX, products, (zero,) * 3, unroll=2), 3)
    all_send(2, row)

    @pl.loop(0, SX)
    def _(x):
        fields = [search[x + 1][4:20], img[DEPTH + x], wfield[x + 1][4:20], v_own[x]]
        final[:, x] = order(jnp.concatenate(fields, axis=0), True).reshape(4, SY, NZ)

    all_wait(2)
    parts = [jnp.zeros((1, 128), F32) for _ in range(8)]
    for j in range(ngx * ngy):
        parts[j % 8] = parts[j % 8] + row_all[1, j]
    while len(parts) > 1:
        parts = [parts[k] + parts[k + 1] for k in range(0, len(parts), 2)]
    total = parts[0]
    rr, ri, ii, vr, vi, vv = [
        jnp.sum(jnp.where(lanes == k, total, 0.0), axis=1, keepdims=True) for k in range(6)
    ]
    alpha = rr / ri
    cross = (ri - alpha * ii) - alpha * (vr - alpha * vi)
    square = ii - alpha * (2.0 * vi - alpha * vv)
    omega = cross / square
    for x in range(SX):
        sv, iv, wv, vv = final[0, x], final[1, x], final[2, x], final[3, x]
        both[0, x] = alpha * sv + omega * (sv - alpha * wv)
        both[1, x] = (natural[3, x] - alpha * iv) - omega * (iv - alpha * vv)

    first_finish()
    all_wait(1, "send")
    all_wait(2, "send")
    halo("send", *base_halo)
    for turn in range(2):
        halo("send", *corr_halo(turn))
        faces("send", turn, (search, wfield)[turn], (2, 3))
    halo("send", *img_halo)


FIRST_EXACT = False


def solution(mesh):
    ngx, ngy = mesh.shape["gx"], mesh.shape["gy"]
    group = ngx * (ngy // ZG)
    vm = pltpu.VMEM

    def local(right_side, velocity, deflation, inverse_rows):
        out = jax.ShapeDtypeStruct((SX, SY, NZ), F32)
        plane = (ROWS, NZ)
        scratch = [
            vm((4, SX, SY, NZ), F32),
            vm((KD, SX, SY, NZ), BF16),
            vm((KD, SX, SY, NZ), BF16),
            vm((NZ, NZ), BF16),
            vm((4, SX, SY, NZ), F32),
            vm(inverse_rows.shape, F32),
            vm((4, SX + 4, SY, NZ), F32),
            vm((4, SX + 4, 2, NZ), F32),
            vm((4, SX + 4, 2, NZ), F32),
            vm((4, SX, 2, NZ), F32),
            vm((4, SX, 2, NZ), F32),
            vm((4, SX) + plane, F32),
            vm((4, SX + 4) + plane, F32),
            vm((KD * 16, 128), BF16),
            vm((SX + 4,) + plane, F32),
            vm((2, SX + 6, SY, NZ), F32),
            vm((2, SX + 6, 3, NZ), F32),
            vm((2, SX + 6, 3, NZ), F32),
            vm((2, SX, 3, NZ), F32),
            vm((2, SX, 3, NZ), F32),
            vm((SX + 6,) + plane, F32),
            vm((SX + 4,) + plane, F32),
            vm((SX + 6,) + plane, F32),
            vm((SX + 4,) + plane, F32),
            vm((SX + 4,) + plane, F32),
            vm((2, SX, 1, NZ), F32),
            vm((2, SX, 1, NZ), F32),
            vm((2, SX, 1, NZ), F32),
            vm((2, SX, 1, NZ), F32),
            vm((SX + 4, SY, NZ), F32),
            vm((SX + 4, 2, NZ), F32),
            vm((SX + 4, 2, NZ), F32),
            vm((SX, 2, NZ), F32),
            vm((SX, 2, NZ), F32),
            vm((SX + 2,) + plane, F32),
            vm((SX + 2,) + plane, F32),
            vm((SX, SY, NZ), F32),
            vm((ZG, 1, 128), F32),
            vm((group, ZG // QUAD, 128), F32),
            vm((2, ngx * ngy, 1, 128), F32),
            pltpu.SemaphoreType.DMA((5,)),
            pltpu.SemaphoreType.DMA((2,)),
            pltpu.SemaphoreType.DMA((2,)),
            pltpu.SemaphoreType.DMA((2,)),
            pltpu.SemaphoreType.DMA((2,)),
            pltpu.SemaphoreType.DMA((6, 8)),
            pltpu.SemaphoreType.DMA((6, 8)),
        ]

        def body(*refs):
            kernel(ngx, ngy, *refs)

        both = pl.pallas_call(
            body,
            name="bicgstab",
            out_shape=jax.ShapeDtypeStruct((2, SX, SY, NZ), F32),
            in_specs=[pl.BlockSpec(memory_space=pl.ANY)] * 4,
            out_specs=pl.BlockSpec(memory_space=vm),
            scratch_shapes=scratch,
            compiler_params=pltpu.CompilerParams(collective_id=0, has_side_effects=True),
        )(right_side, velocity, deflation, inverse_rows)
        return both[0], both[1]

    return jax.shard_map(
        local,
        mesh=mesh,
        in_specs=(
            P("gx", "gy", None),
            P(None, "gx", "gy", None),
            P(None, "gx", "gy", None),
            P(("gx", "gy"), None),
        ),
        out_specs=(P("gx", "gy", None), P("gx", "gy", None)),
        check_vma=False,
    )
```

```python
import jax
import jax.numpy as jnp
from jax import lax
from jax.experimental import pallas as pl
from jax.experimental.pallas import tpu as pltpu
from jax.sharding import PartitionSpec as P

F32 = jnp.float32
BF16 = jnp.bfloat16
MESH = pl.DeviceIdType.MESH
SX, SY, NZ = 8, 16, 256
KD = 32
DEPTH = 2
CHEB = 4
ZG = 8
QUAD = 128 // KD
ROWS = 24
SIGMA = 1.0 / 0.9


def hops(step, ring):
    return min(step, ring - step)


def near_last(ring):
    return sorted(range(ring), key=lambda step: -hops(step, ring))
AROUND = [(1, 1), (-1, 1), (1, -1), (-1, -1), (0, 1), (0, -1), (1, 0), (-1, 0)]


def iota(shape, dim):
    return lax.broadcasted_iota(jnp.int32, shape, dim)


def padded(low, middle, high):
    gap = 4 - low.shape[0]
    parts = [low, middle, high]
    if gap:
        fill = jnp.zeros((gap, NZ), F32)
        parts = [fill] + parts + [fill]
    return jnp.concatenate(parts, axis=0)


def kernel(
    ngx, ngy,
    r_hbm, vel_hbm, defl_hbm, inv_hbm, both,
    natural, defl, defl_eo, lanes_ref, final, inv, base, base_lo, base_hi, base_plo, base_phi,
    coef, scale, pick, q24, corr, corr_lo, corr_hi, corr_plo, corr_phi, ext, left, upd0, upd1, upd2,
    face_lo, face_hi, face_plo, face_phi,
    img, img_lo, img_hi, img_plo, img_phi, search, wfield, v_own, row_a, row_b, row_all,
    local_sem, ag_send, ag_recv, all_sends, all_recvs, halo_send, halo_recv,
):
    gx = lax.axis_index("gx")
    gy = lax.axis_index("gy")
    xg = ngy // ZG
    zpos = lax.rem(gy, ZG)
    xpos = lax.div(gy, ZG)
    line = xpos * ZG
    group = ngx * xg
    seat = gx * xg + xpos
    number = gx * ngy + gy
    here = (gx, gy)
    barrier = pltpu.get_barrier_semaphore()

    def line_peer(step):
        return (gx, line + lax.rem(zpos + step, ZG))

    def spread(act, dz, dx):
        other = lax.rem(xpos + dx, xg) * ZG + lax.rem(zpos + dz, ZG)

        @pl.loop(0, ngx, unroll=ngx)
        def _(step):
            act((lax.rem(gx + step + ngx // 2, ngx), other))

    def group_each(act):
        for dx in near_last(xg):
            if dx:
                spread(act, 0, dx)
        mine(act)

    def mine(act):
        @pl.loop(1, ngx, unroll=ngx - 1)
        def _(step):
            act((lax.rem(gx + step, ngx), gy))

    def all_each(act, between=None):
        pairs = [(dz, dx) for dz in range(ZG) for dx in range(xg) if dz or dx]
        pairs.sort(key=lambda p: -hops(p[0], ZG) - hops(p[1], xg))
        for place, (dz, dx) in enumerate(pairs):
            if place == len(pairs) // 2 and between is not None:
                between()
            spread(act, dz, dx)
        mine(act)

    def greet(device):
        pl.semaphore_signal(barrier, inc=1, device_id=device, device_id_type=MESH)

    own = pl.ds(DEPTH, SX)
    loads = [
        pltpu.make_async_copy(r_hbm, natural.at[3], local_sem.at[0]),
        pltpu.make_async_copy(defl_hbm.at[pl.ds(0, 16)], defl.at[pl.ds(0, 16)], local_sem.at[1]),
        pltpu.make_async_copy(defl_hbm.at[pl.ds(16, 16)], defl.at[pl.ds(16, 16)], local_sem.at[2]),
        pltpu.make_async_copy(vel_hbm, natural.at[pl.ds(0, 3)], local_sem.at[3]),
        pltpu.make_async_copy(inv_hbm, inv, local_sem.at[4]),
    ]
    for load in loads:
        load.start()

    for step in near_last(ZG):
        if step:
            greet(line_peer(step))
    group_each(greet)

    for dx, dy in AROUND:
        greet((lax.rem(gx + dx + ngx, ngx), lax.rem(gy + dy + ngy, ngy)))

    has_w, has_e = gx > 0, gx < ngx - 1
    has_s, has_n = gy > 0, gy < ngy - 1

    def remote(src, dst, send, recv, device):
        return pltpu.make_async_remote_copy(
            src_ref=src, dst_ref=dst, send_sem=send, recv_sem=recv,
            device_id=device, device_id_type=MESH,
        )

    def line_send(row):
        row_a[zpos] = row

        for step in near_last(ZG):
            if step:
                remote(row_a.at[zpos], row_a.at[zpos], ag_send.at[0], ag_recv.at[0],
                       line_peer(step)).start()

    def line_wait():
        view = row_a.at[pl.ds(0, ZG - 1)]
        remote(view, view, ag_send.at[0], ag_recv.at[0], here).wait_recv()

    def group_send(rows):
        row_b[seat] = rows

        group_each(lambda device: remote(
            row_b.at[seat], row_b.at[seat], ag_send.at[1], ag_recv.at[1], device).start())

    def group_wait():
        view = row_b.at[pl.ds(0, group - 1)]
        remote(view, view, ag_send.at[1], ag_recv.at[1], here).wait_recv()

    def all_send(turn, row, between=None):
        slot = turn - 1
        row_all[slot, number] = row

        all_each(lambda device: remote(
            row_all.at[slot, number], row_all.at[slot, number], all_sends.at[slot],
            all_recvs.at[slot], device).start(), between)

    def all_wait(turn, what="recv"):
        slot = turn - 1
        view = row_all.at[slot, pl.ds(0, ngx * ngy - 1)]
        copy = remote(view, view, all_sends.at[slot], all_recvs.at[slot], here)
        if what == "recv":
            copy.wait_recv()
        else:
            copy.wait_send()

    def first_finish():
        view = row_a.at[pl.ds(0, ZG - 1)]
        remote(view, view, ag_send.at[0], ag_recv.at[0], here).wait_send()
        view = row_b.at[pl.ds(0, group - 1)]
        remote(view, view, ag_send.at[1], ag_recv.at[1], here).wait_send()

    def beside(dx, dy):
        tests = {(-1, 0): has_w, (1, 0): has_e, (0, -1): has_s, (0, 1): has_n}
        first = tests.get((dx, 0)) if dx else None
        second = tests.get((0, dy)) if dy else None
        if first is None:
            return second
        return first if second is None else first & second

    def halo(what, turn, width, mid, low, high, plow, phigh, lead=()):
        w = width
        for k, (dx, dy) in enumerate(AROUND):
            size = w if dx else SX
            take = {1: SX - w, -1: 0, 0: 0}[dx]
            put = {1: 0, -1: w + SX, 0: w}[dx]
            source = {1: phigh, -1: plow, 0: mid}[dy]
            target = {1: low, -1: high, 0: mid}[dy]
            src = source.at[lead + (pl.ds(take + (0 if dy else w), size),)]
            dst = target.at[lead + (pl.ds(put, size),)]
            copy = remote(
                src, dst, halo_send.at[turn, k], halo_recv.at[turn, k],
                (gx + dx, gy + dy) if what == "start" else here,
            )
            act(what, copy, dx, dy)

    def act(what, copy, dx, dy):
        sign = -1 if what == "recv" else 1

        @pl.when(beside(sign * dx, sign * dy))
        def _():
            if what == "start":
                copy.start()
            elif what == "recv":
                copy.wait_recv()
            else:
                copy.wait_send()

    def faces(what, slot, field, kinds=(0, 1, 2, 3)):
        pairs = [
            ((1, 0), field.at[SX], field.at[0]),
            ((-1, 0), field.at[1], field.at[SX + 1]),
            ((0, 1), face_phi.at[slot], face_lo.at[slot]),
            ((0, -1), face_plo.at[slot], face_hi.at[slot]),
        ]
        for k in kinds:
            (dx, dy), src, dst = pairs[k]
            copy = remote(
                src, dst, halo_send.at[4 + slot, k], halo_recv.at[4 + slot, k],
                (gx + dx, gy + dy) if what == "start" else here,
            )
            act(what, copy, dx, dy)

    lane_end = iota((ROWS, 128), 1) == 127

    def shifts(before, centre, after, add, c0, c1, c2):
        even, odd = centre[:, :128], centre[:, 128:]
        beyond = jnp.where(lane_end, 0.0, pltpu.roll(even, 127, 1))
        ahead = jnp.concatenate([odd, beyond], axis=1)
        behind = jnp.concatenate([pltpu.roll(odd, 1, 1), even], axis=1)
        nexts = (after + pltpu.roll(centre, ROWS - 1, 0)) + ahead
        if add is not None:
            nexts = nexts + add
        previous = c0 * before + c1 * pltpu.roll(centre, 1, 0)
        return nexts, previous + c2 * behind

    def order(value, back):
        high = value.astype(BF16)
        rest = value - high.astype(F32)
        middle = rest.astype(BF16)
        low = (rest - middle.astype(F32)).astype(BF16)
        dims = (((1,), (1 if back else 0,)), ((), ()))
        high, middle, low = [
            lax.dot_general(part, lanes_ref[...], dims, preferred_element_type=F32)
            for part in (high, middle, low)
        ]
        return high + (middle + low)

    def operator(x, field):
        nexts, previous = shifts(
            field[x], field[x + 1], field[x + 2], None, coef[1, x], coef[2, x], coef[3, x]
        )
        return coef[0, x] * field[x + 1] - (nexts + previous)

    def split(value):
        top = value.astype(BF16)
        rest = (value - top.astype(F32)).astype(BF16)
        return jnp.concatenate([top, rest], axis=0)

    def weights(vectors, half, x):
        return vectors[pl.ds(half * 16, 16), x].reshape(256, NZ)

    def restrict(vectors, plane, exact, ready=(None, None)):
        lhs = [split(plane(x)) if exact else plane(x).astype(BF16) for x in range(SX)]
        packed = []
        for half in range(2):
            if ready[half] is not None:
                ready[half].wait()
            total = None
            for x in range(SX):
                part = lax.dot_general(
                    lhs[x], weights(vectors, half, x), (((1,), (1,)), ((), ())), preferred_element_type=F32
                )
                total = part if total is None else total + part
            same = lax.rem(iota(total.shape, 0), 16) == lax.rem(iota(total.shape, 1), 16)
            kept = jnp.where(same, total, 0.0)
            packed.append(jnp.sum(kept.reshape(-1, 8, 256), axis=0))
        packed = jnp.concatenate(packed, axis=1)
        high = packed.astype(BF16).astype(F32)
        rest = packed - high
        middle = rest.astype(BF16).astype(F32)
        low = rest - middle
        stack = jnp.concatenate([high, middle, low, jnp.zeros_like(low)], axis=0).astype(BF16)
        row = jnp.dot(stack, pick[...], preferred_element_type=F32)
        row = jnp.sum(row, axis=0, keepdims=True)
        mine = lax.div(iota((1, 128), 1), KD) == lax.rem(zpos, QUAD)
        return jnp.where(mine, row, 0.0)

    def quads():
        rows = []
        for start in range(0, ZG, QUAD):
            total = row_a[start]
            for k in range(1, QUAD):
                total = total + row_a[start + k]
            rows.append(total)
        return jnp.concatenate(rows, axis=0) if len(rows) > 1 else rows[0]

    def solve(turn, exact):
        per = ZG // QUAD
        sums = [jnp.zeros((KD, 128), F32) for _ in range(4)]
        for j in range(group * per):
            if turn == 0:
                value = row_b[j // per, pl.ds(j % per, 1), :]
            else:
                first, second, third, fourth = [row_all[0, QUAD * j + k] for k in range(QUAD)]
                value = (first + second) + (third + fourth)
            sums[j % 4] = sums[j % 4] + inv[:, pl.ds(j * 128, 128)] * value
        total = (sums[0] + sums[1]) + (sums[2] + sums[3])
        solved = jnp.sum(total, axis=1, keepdims=True)
        spread = jnp.where(
            iota((KD, KD * 16), 0) == lax.div(iota((KD, KD * 16), 1), 16), solved, 0.0
        )
        spread = jnp.sum(spread, axis=0, keepdims=True)
        shape = (16, KD * 16)
        lhs = jnp.where(iota(shape, 0) == lax.rem(iota(shape, 1), 16), spread, 0.0)
        return split(lhs) if exact else lhs.astype(BF16)

    def smooth(turn, out_ref):
        rows = iota((ROWS, NZ), 0)
        keep_y = ((rows >= 4) & (rows < 20)) | ((rows < 4) & has_s) | ((rows >= 20) & has_n)
        box = (rows >= 2) & (rows < 22)

        @pl.loop(0, SX + 6, unroll=2)
        def _(p):
            plane = padded(corr_lo[turn, p], corr[turn, p], corr_hi[turn, p])
            keep = keep_y & ((p >= 3) | has_w) & ((p < SX + 3) | has_e)
            ext[p] = jnp.where(keep, plane, 0.0)

        def scaled(p, before, centre, after, add):
            nexts, previous = shifts(before, centre, after, add, scale[1, p], scale[2, p], scale[3, p])
            return scale[0, p] * nexts + previous

        @pl.loop(0, SX + 4, unroll=4)
        def _(p):
            centre = ext[p + 1]
            total = scaled(p, ext[p], centre, ext[p + 2], q24[p])
            upd0[p + 1] = total - jnp.where(box, centre, 0.0)

        rho = 1.0 / SIGMA
        factors = []
        for sweep in range(CHEB - 1):
            rho_next = 1.0 / (2.0 * SIGMA - rho)
            factors.append((rho_next * rho, 2.0 * rho_next / 0.9))
            rho = rho_next

        @pl.loop(0, SX + 4, unroll=4)
        def _(p):
            centre = upd0[p + 1]
            rest = scaled(p, upd0[p], centre, upd0[p + 2], None)
            left[p] = rest
            upd1[p] = factors[0][0] * centre + factors[0][1] * rest

        @pl.loop(1, SX + 3, unroll=5)
        def _(p):
            centre = upd1[p]
            rest = (left[p] - centre) + scaled(p, upd1[p - 1], centre, upd1[p + 1], None)
            left[p] = rest
            upd2[p] = factors[1][0] * centre + factors[1][1] * rest

        @pl.loop(2, SX + 2, unroll=4)
        def _(p):
            centre = upd2[p]
            rest = (left[p] - centre) + scaled(p, upd2[p - 1], centre, upd2[p + 1], None)
            upd3 = factors[2][0] * centre + factors[2][1] * rest
            value = ((upd0[p + 1] + upd1[p]) + (centre + upd3)) + ext[p + 1]
            out_ref[p - 1] = value
            face_plo[turn, p - 2] = value[4:5]
            face_phi[turn, p - 2] = value[19:20]

    def face_place(slot, dst):
        rows = iota((ROWS, NZ), 0)

        @pl.loop(0, SX, unroll=2)
        def _(x):
            low = jnp.broadcast_to(jnp.where(has_s, face_lo[slot, x], 0.0), (ROWS, NZ))
            high = jnp.broadcast_to(jnp.where(has_n, face_hi[slot, x], 0.0), (ROWS, NZ))
            value = dst[x + 1]
            dst[x + 1] = jnp.where(rows == 3, low, jnp.where(rows == 20, high, value))

    def q_assemble(low, mid, high):
        @pl.loop(0, SX + 4)
        def _(p):
            q24[p] = padded(low(p), mid(p), high(p))

    upd0[0] = jnp.zeros((ROWS, NZ), F32)
    upd0[SX + 5] = jnp.zeros((ROWS, NZ), F32)
    for there, plane in ((has_w, 0), (has_e, SX + 1)):

        @pl.when(jnp.logical_not(there))
        def _():
            search[plane] = jnp.zeros((ROWS, NZ), F32)
            wfield[plane] = jnp.zeros((ROWS, NZ), F32)

    table = lax.div(iota((KD * 16, 128), 0), 16) == lax.rem(iota((KD * 16, 128), 1), KD)
    pick[...] = jnp.where(table, 1.0, 0.0).astype(BF16)
    source, place = iota((NZ, NZ), 0), iota((NZ, NZ), 1)
    table = source == 2 * lax.rem(place, 128) + lax.div(place, 128)
    lanes_ref[...] = jnp.where(table, 1.0, 0.0).astype(BF16)
    loads[0].wait()
    row = restrict(defl, lambda x: natural[3, x], FIRST_EXACT, (loads[1], loads[2]))
    greetings = (ZG - 1) + (group - 1) + len(AROUND)
    pl.semaphore_wait(barrier, greetings)
    line_send(row)
    loads[3].wait()

    @pl.loop(0, SX)
    def _(x):
        planes = order(natural[:, x].reshape(4 * SY, NZ), False).reshape(4, SY, NZ)
        for c in range(4):
            plane = planes[c]
            base[c, DEPTH + x] = plane
            base_plo[c, x] = plane[0:2]
            base_phi[c, x] = plane[14:16]

    every = (slice(None),)
    base_halo = (0, DEPTH, base, base_lo, base_hi, base_plo, base_phi, every)
    img_halo = (3, DEPTH, img, img_lo, img_hi, img_plo, img_phi)

    def corr_halo(turn):
        return (1 + turn, 3, corr.at[turn], corr_lo.at[turn], corr_hi.at[turn],
                corr_plo.at[turn], corr_phi.at[turn])

    halo("start", *base_halo)
    line_wait()
    group_send(quads())
    halo("recv", *base_halo)

    rows = iota((ROWS, NZ), 0)
    cols = iota((ROWS, NZ), 1)
    keep_y = ((rows >= 4) & (rows < 20)) | ((rows >= 2) & (rows < 4) & has_s)
    keep_y = keep_y | ((rows >= 20) & (rows < 22) & has_n)

    @pl.loop(0, SX + 4)
    def _(p):
        keep = keep_y & ((p >= DEPTH) | has_w) & ((p < SX + DEPTH) | has_e)
        w0, w1, w2, r = [
            jnp.where(keep, padded(base_lo[c, p], base[c, p], base_hi[c, p]), 0.0)
            for c in range(4)
        ]
        diagonal = 6.0 + w0 + w1 + w2
        jdiag = jnp.where(keep, 1.0 / diagonal, 0.0)
        c0, c1 = 1.0 + w0, 1.0 + w1
        c2 = jnp.where(cols == 0, 0.0, 1.0 + w2)
        scale[0, p] = jdiag
        scale[1, p] = jdiag * c0
        scale[2, p] = jdiag * c1
        scale[3, p] = jdiag * c2
        q24[p] = r

        @pl.when((p >= DEPTH) & (p < SX + DEPTH))
        def _():
            coef[0, p - DEPTH] = diagonal
            coef[1, p - DEPTH] = c0
            coef[2, p - DEPTH] = c1
            coef[3, p - DEPTH] = c2

    @pl.loop(0, SX)
    def _(x):
        for half in range(2):
            moved = jnp.dot(weights(defl, half, x), lanes_ref[...], preferred_element_type=F32)
            defl_eo[pl.ds(half * 16, 16), x] = moved.astype(BF16).reshape(16, SY, NZ)

    loads[4].wait()

    def precondition(turn, out_ref, exact):
        lhs = solve(turn, exact)
        for x in range(SX):
            out = jnp.dot(lhs[:, :256], weights(defl_eo, 0, x), preferred_element_type=F32)
            out = out + jnp.dot(lhs[:, 256:], weights(defl_eo, 1, x), preferred_element_type=F32)
            if exact:
                out = out[:16] + out[16:]
            corr[turn, 3 + x] = out
            corr_plo[turn, x] = out[0:3]
            corr_phi[turn, x] = out[13:16]
        halo("start", *corr_halo(turn))
        halo("recv", *corr_halo(turn))
        smooth(turn, out_ref)
        faces("start", turn, out_ref)
        faces("recv", turn, out_ref)
        faces("send", turn, out_ref, (0, 1))
        face_place(turn, out_ref)

    group_wait()
    precondition(0, search, FIRST_EXACT)

    @pl.loop(0, SX, unroll=2)
    def _(x):
        inner = operator(x, search)[4:20]
        img[DEPTH + x] = inner
        img_plo[x] = inner[0:2]
        img_phi[x] = inner[14:16]

    row = restrict(defl_eo, lambda x: img[DEPTH + x], True)
    all_send(1, row, lambda: halo("start", *img_halo))
    halo("recv", *img_halo)
    keep_q = keep_y

    @pl.loop(0, SX + 4)
    def _(p):
        keep = keep_q & ((p >= DEPTH) | has_w) & ((p < SX + DEPTH) | has_e)
        q24[p] = jnp.where(keep, padded(img_lo[p], img[p], img_hi[p]), 0.0)

    zero = jnp.zeros((8, NZ), F32)

    def fold(value):
        return value[0:8] + value[8:16]

    def early(x, sums):
        i = img[DEPTH + x]
        r = base[3, DEPTH + x]
        pairs = [(r, r), (r, i), (i, i)]
        return tuple(s + fold(a * b) for s, (a, b) in zip(sums, pairs))

    early_sums = lax.fori_loop(0, SX, early, (zero,) * 3, unroll=2)
    lanes = iota((1, 128), 1)

    def pack(row, sums, start):
        for k, s in enumerate(sums):
            s = jnp.sum(s, axis=0, keepdims=True)
            s = jnp.sum(s, axis=1, keepdims=True)
            row = jnp.where(lanes == start + k, s, row)
        return row

    early_row = pack(jnp.zeros((1, 128), F32), early_sums, 0)
    all_wait(1)
    precondition(1, wfield, True)

    def products(x, sums):
        v = operator(x, wfield)[4:20]
        v_own[x] = v
        i = img[DEPTH + x]
        r = base[3, DEPTH + x]
        pairs = [(v, r), (v, i), (v, v)]
        return tuple(s + fold(a * b) for s, (a, b) in zip(sums, pairs))

    row = pack(early_row, lax.fori_loop(0, SX, products, (zero,) * 3, unroll=2), 3)
    all_send(2, row)

    @pl.loop(0, SX)
    def _(x):
        fields = [search[x + 1][4:20], img[DEPTH + x], wfield[x + 1][4:20], v_own[x]]
        final[:, x] = order(jnp.concatenate(fields, axis=0), True).reshape(4, SY, NZ)

    all_wait(2)
    parts = [jnp.zeros((1, 128), F32) for _ in range(8)]
    for j in range(ngx * ngy):
        parts[j % 8] = parts[j % 8] + row_all[1, j]
    while len(parts) > 1:
        parts = [parts[k] + parts[k + 1] for k in range(0, len(parts), 2)]
    total = parts[0]
    rr, ri, ii, vr, vi, vv = [
        jnp.sum(jnp.where(lanes == k, total, 0.0), axis=1, keepdims=True) for k in range(6)
    ]
    alpha = rr / ri
    cross = (ri - alpha * ii) - alpha * (vr - alpha * vi)
    square = ii - alpha * (2.0 * vi - alpha * vv)
    omega = cross / square
    for x in range(SX):
        sv, iv, wv, vv = final[0, x], final[1, x], final[2, x], final[3, x]
        both[0, x] = alpha * sv + omega * (sv - alpha * wv)
        both[1, x] = (natural[3, x] - alpha * iv) - omega * (iv - alpha * vv)

    first_finish()
    all_wait(1, "send")
    all_wait(2, "send")
    halo("send", *base_halo)
    for turn in range(2):
        halo("send", *corr_halo(turn))
        faces("send", turn, (search, wfield)[turn], (2, 3))
    halo("send", *img_halo)


FIRST_EXACT = False


def solution(mesh):
    ngx, ngy = mesh.shape["gx"], mesh.shape["gy"]
    group = ngx * (ngy // ZG)
    vm = pltpu.VMEM

    def local(right_side, velocity, deflation, inverse_rows):
        out = jax.ShapeDtypeStruct((SX, SY, NZ), F32)
        plane = (ROWS, NZ)
        scratch = [
            vm((4, SX, SY, NZ), F32),
            vm((KD, SX, SY, NZ), BF16),
            vm((KD, SX, SY, NZ), BF16),
            vm((NZ, NZ), BF16),
            vm((4, SX, SY, NZ), F32),
            vm(inverse_rows.shape, F32),
            vm((4, SX + 4, SY, NZ), F32),
            vm((4, SX + 4, 2, NZ), F32),
            vm((4, SX + 4, 2, NZ), F32),
            vm((4, SX, 2, NZ), F32),
            vm((4, SX, 2, NZ), F32),
            vm((4, SX) + plane, F32),
            vm((4, SX + 4) + plane, F32),
            vm((KD * 16, 128), BF16),
            vm((SX + 4,) + plane, F32),
            vm((2, SX + 6, SY, NZ), F32),
            vm((2, SX + 6, 3, NZ), F32),
            vm((2, SX + 6, 3, NZ), F32),
            vm((2, SX, 3, NZ), F32),
            vm((2, SX, 3, NZ), F32),
            vm((SX + 6,) + plane, F32),
            vm((SX + 4,) + plane, F32),
            vm((SX + 6,) + plane, F32),
            vm((SX + 4,) + plane, F32),
            vm((SX + 4,) + plane, F32),
            vm((2, SX, 1, NZ), F32),
            vm((2, SX, 1, NZ), F32),
            vm((2, SX, 1, NZ), F32),
            vm((2, SX, 1, NZ), F32),
            vm((SX + 4, SY, NZ), F32),
            vm((SX + 4, 2, NZ), F32),
            vm((SX + 4, 2, NZ), F32),
            vm((SX, 2, NZ), F32),
            vm((SX, 2, NZ), F32),
            vm((SX + 2,) + plane, F32),
            vm((SX + 2,) + plane, F32),
            vm((SX, SY, NZ), F32),
            vm((ZG, 1, 128), F32),
            vm((group, ZG // QUAD, 128), F32),
            vm((2, ngx * ngy, 1, 128), F32),
            pltpu.SemaphoreType.DMA((5,)),
            pltpu.SemaphoreType.DMA((2,)),
            pltpu.SemaphoreType.DMA((2,)),
            pltpu.SemaphoreType.DMA((2,)),
            pltpu.SemaphoreType.DMA((2,)),
            pltpu.SemaphoreType.DMA((6, 8)),
            pltpu.SemaphoreType.DMA((6, 8)),
        ]

        def body(*refs):
            kernel(ngx, ngy, *refs)

        both = pl.pallas_call(
            body,
            name="bicgstab",
            out_shape=jax.ShapeDtypeStruct((2, SX, SY, NZ), F32),
            in_specs=[pl.BlockSpec(memory_space=pl.ANY)] * 4,
            out_specs=pl.BlockSpec(memory_space=vm),
            scratch_shapes=scratch,
            compiler_params=pltpu.CompilerParams(collective_id=0, has_side_effects=True, vmem_limit_bytes=56000000),
        )(right_side, velocity, deflation, inverse_rows)
        return both[0], both[1]

    return jax.shard_map(
        local,
        mesh=mesh,
        in_specs=(
            P("gx", "gy", None),
            P(None, "gx", "gy", None),
            P(None, "gx", "gy", None),
            P(("gx", "gy"), None),
        ),
        out_specs=(P("gx", "gy", None), P("gx", "gy", None)),
        check_vma=False,
    )
```
